32 devices in a mesh: tile: 8 (over z, y), rep: 4 (over x, core).
Axes of the slice: x: 2, y: 2, z: 4, core: 2. Of those that a mesh axis runs over, the one named last changes fastest.
Arguments:
- inputs: bfloat16 [4, 32, 64, 4, 8, 128], P('rep', 'tile'), may hold values from -20 to 20
- w_spatial: bfloat16 [9, 64, 64], replicated, may hold values from -0.25 to 0.25
- w_temporal: bfloat16 [2, 3, 64, 64], replicated, may hold values from -0.4375 to 0.4375
- w_head: bfloat16 [64], replicated, may hold values from -0.75 to 0.75
- targets: bfloat16 [4, 32, 4096], P('rep', None, 'tile'), may hold values from 0 to 1
- valid: int32 [4, 32], P('rep'), may hold values 0 or 1
Outputs:
- logits: bfloat16 [4, 32, 4096], P('rep', None, 'tile')
- grad_inputs: bfloat16 [4, 32, 64, 4, 8, 128], P('rep', 'tile')
- grad_spatial: float32 [9, 64, 64], P(None, 'rep')
- grad_temporal: float32 [2, 3, 64, 64], P(None, None, 'rep')
- grad_head: float32 [64], P('rep')
The draws below stay inside these ranges and needn't reach their ends.
All inputs are finite; a program needn't handle non-finite values. No bound on the sum of `valid` on one device may be relied on, other than what follows from the above.
Results may differ from the reference program's by a relative error of at most 0.024.
Values may be sent and summed in bfloat16 or wider, within the bound.
No kernel may reach another device: no remote copies, remote signals or barrier semaphores. Data moves between devices by JAX's collectives and lax.ppermute only.
A program may use at most 128 MiB of HBM per device.

```python
import jax
import jax.numpy as jnp
from jax import lax

C = 64
FRAMES = 32
Z = 4
H = 8
W = 128
TL = 2
SAMPLES = 4
VOX = 4096


def draw_inputs(key, part):
    subkeys = jax.random.split(key, 3)
    full_shape = (SAMPLES, FRAMES, C, Z, H, W)
    channel_scale = jnp.exp(jax.random.uniform(subkeys[1], (1, 1, C, 1, 1, 1), jnp.float32, -1.15, 1.15))
    cell_scale = jnp.exp(jax.random.uniform(subkeys[2], (SAMPLES, FRAMES, 1, Z, H, W), jnp.float32, -1.15, 1.15))
    base_value = jax.random.normal(subkeys[0], full_shape, jnp.float32)
    base_value = jnp.clip(base_value, -4.0, 4.0)
    return (0.5 * base_value * channel_scale * cell_scale).astype(jnp.bfloat16)


def place_ends(drawn, stream_key, smallest, top_value):
    spot = [jax.random.randint(jax.random.fold_in(stream_key, axis), (), 0, length) for axis, length in enumerate(drawn.shape)]
    widest = drawn.shape.index(max(drawn.shape))
    neighbour = spot[:widest] + [(spot[widest] + 1) % drawn.shape[widest]] + spot[widest + 1:]
    return drawn.at[tuple(spot)].set(smallest).at[tuple(neighbour)].set(top_value)


def level_of(own_key, extent, cuts, least, high):
    gain, own = 1.0, jax.random.fold_in(own_key, 6)
    for dim, blocks in cuts:
        steps = jnp.exp(jax.random.uniform(jax.random.fold_in(own, dim), (blocks,), jnp.float32, least / len(cuts), high / len(cuts)))
        gain = gain * jnp.repeat(steps, extent[dim] // blocks).reshape([-1 if axis == dim else 1 for axis in range(len(extent))])
    return gain


def normal_values(own_key, shape, width, most, held_as=jnp.bfloat16):
    entries = width * jax.random.normal(own_key, shape, jnp.float32)
    return jnp.clip(entries, min=-most, max=most).astype(held_as)


def setup_inputs(seed: int = 0) -> dict:
    key_list = jax.random.split(jax.random.key(seed), 7)
    return {
        "inputs": draw_inputs(jax.random.fold_in(key_list[6], 71), 0),
        "w_spatial": normal_values(key_list[1], (9, C, C), (9 * C) ** -0.5, 0.25),
        "w_temporal": normal_values(key_list[2], (TL, 3, C, C), (3 * C) ** -0.5, 0.4375),
        "w_head": normal_values(key_list[3], (C,), C ** -0.5, 0.75),
        "targets": jnp.clip(1.0 * jax.random.uniform(key_list[4], (SAMPLES, FRAMES, VOX), jnp.float32) ** level_of(key_list[4], (SAMPLES, FRAMES, VOX), ((0, 4), (2, 8)), -0.2, 0.2), 0.0, 1.0).astype(jnp.bfloat16),
        "valid": place_ends((jax.random.randint(key_list[5], (SAMPLES, FRAMES), 0, 4) < 3).astype(jnp.int32), jax.random.fold_in(key_list[5], 1), 0, 1),
    }


epsilon = 1e-06

def product(pattern, left_side, right_side):
    return jnp.einsum(pattern, left_side.astype(jnp.float32), right_side.astype(jnp.float32), precision=lax.Precision.HIGHEST)

def row_masks(first_row, row_count, height):
    row_index = first_row + jnp.arange(row_count, dtype=jnp.int32)
    within = row_index % height
    upper_ok = (within > 0).astype(jnp.bfloat16)[:, None]
    lower_ok = (within < height - 1).astype(jnp.bfloat16)[:, None]
    return (upper_ok, lower_ok)

def shifted(bordered, upper_ok, lower_ok, row_step, col_step):
    row_count = bordered.shape[2] - 2
    row_width = bordered.shape[3] - 2
    window = bordered[:, :, 1 + row_step:1 + row_step + row_count, 1 + col_step:1 + col_step + row_width]
    if row_step == -1:
        window = window * upper_ok
    if row_step == 1:
        window = window * lower_ok
    return window

def border_cols(padded):
    return jnp.pad(padded, ((0, 0), (0, 0), (0, 0), (1, 1)))

def spatial_forward(padded, upper_ok, lower_ok, w_spatial):
    bordered = border_cols(padded)
    accumulated = jnp.zeros((), jnp.float32)
    for tap_index in range(9):
        accumulated = accumulated + product('oc,fcrw->forw', w_spatial[tap_index], shifted(bordered, upper_ok, lower_ok, tap_index // 3 - 1, tap_index % 3 - 1))
    return accumulated

def spatial_backward(padded, padded_grad, upper_ok, lower_ok, w_spatial):
    bordered = border_cols(padded)
    bordered_grad = border_cols(padded_grad)
    center = padded_grad[:, :, 1:-1, :]
    gradients = []
    accumulated = jnp.zeros((), jnp.float32)
    for tap_index in range(9):
        row_step = tap_index // 3 - 1
        col_step = tap_index % 3 - 1
        gradients.append(product('forw,fcrw->oc', center, shifted(bordered, upper_ok, lower_ok, row_step, col_step)))
        accumulated = accumulated + product('oc,forw->fcrw', w_spatial[tap_index], shifted(bordered_grad, upper_ok, lower_ok, -row_step, -col_step))
    return (jnp.stack(gradients), accumulated.astype(jnp.bfloat16))

def activate(values):
    return (values * jax.nn.sigmoid(values)).astype(jnp.bfloat16)

def silu_grad(values):
    sigmoid_value = jax.nn.sigmoid(values)
    return sigmoid_value * (1.0 + values * (1.0 - sigmoid_value))

def rms_factor(hidden):
    return lax.rsqrt(lax.optimization_barrier(jnp.mean(hidden * hidden, axis=1, keepdims=True)) + epsilon)

def norm_backward(hidden, inverse_rms, incoming):
    unit_value = hidden * inverse_rms
    return inverse_rms * (incoming - unit_value * lax.optimization_barrier(jnp.mean(incoming * unit_value, axis=1, keepdims=True)))

def temporal_pass(hidden, w_temporal, w_head, target, frame_mask):
    frame_count = hidden.shape[0]
    stored = []
    for layer_index in range(w_temporal.shape[0]):
        dilation = 2 ** layer_index
        inverse_rms = rms_factor(hidden)
        normed = (hidden * inverse_rms).astype(jnp.bfloat16)
        padded = jnp.pad(normed, ((dilation, dilation), (0, 0), (0, 0)))
        mixed_out = jnp.zeros((), jnp.float32)
        for tap_index in range(3):
            offset = tap_index * dilation
            mixed_out = mixed_out + product('oc,fcv->fov', w_temporal[layer_index, tap_index], padded[offset:offset + frame_count])
        stored.append((hidden, inverse_rms, padded, mixed_out))
        hidden = hidden + mixed_out * jax.nn.sigmoid(mixed_out)
    inverse_rms = rms_factor(hidden)
    final_normed = (hidden * inverse_rms).astype(jnp.bfloat16)
    logit_values = product('c,fcv->fv', w_head, final_normed)
    weighting = frame_mask.astype(jnp.float32)[:, None] / frame_count
    dlogit = weighting * (jax.nn.sigmoid(logit_values) - target.astype(jnp.float32))
    grad_head = jnp.einsum('fv,fcv->c', dlogit, final_normed.astype(jnp.float32), precision=lax.Precision.HIGHEST)
    dfinal = w_head.astype(jnp.float32)[None, :, None] * dlogit[:, None, :]
    dhidden = norm_backward(hidden, inverse_rms, dfinal)
    gradients = [None] * len(stored)
    for layer_index in reversed(range(len(stored))):
        dilation = 2 ** layer_index
        earlier, inverse_rms, padded, mixed_out = stored[layer_index]
        dmixed = (dhidden * silu_grad(mixed_out)).astype(jnp.bfloat16)
        padded_grad = jnp.pad(dmixed, ((dilation, dilation), (0, 0), (0, 0)))
        tap_grads = []
        dnormed = jnp.zeros((), jnp.float32)
        for tap_index in range(3):
            offset = tap_index * dilation
            tap_grads.append(product('fov,fcv->oc', dmixed, padded[offset:offset + frame_count]))
            reverse_offset = (2 - tap_index) * dilation
            dnormed = dnormed + product('oc,fov->fcv', w_temporal[layer_index, tap_index], padded_grad[reverse_offset:reverse_offset + frame_count])
        gradients[layer_index] = jnp.stack(tap_grads)
        dhidden = dhidden + norm_backward(earlier, inverse_rms, dnormed)
    return (logit_values, dhidden.astype(jnp.bfloat16), jnp.stack(gradients), grad_head)

def reference(inputs, w_spatial, w_temporal, w_head, targets, valid):
    row_count = Z * H
    upper_ok, lower_ok = row_masks(0, row_count, H)

    def one_sample(sample_items):
        sample, target, frame_mask = sample_items
        local_block = sample.reshape(FRAMES, C, row_count, W)
        padded = jnp.pad(local_block, ((0, 0), (0, 0), (1, 1), (0, 0)))
        before = spatial_forward(padded, upper_ok, lower_ok, w_spatial)
        features = activate(before)
        hidden = features.reshape(FRAMES, C, row_count * W).astype(jnp.float32)
        logit_values, dfeatures, grad_temporal, grad_head = temporal_pass(hidden, w_temporal, w_head, target, frame_mask)
        dbefore = (dfeatures.reshape(FRAMES, C, row_count, W).astype(jnp.float32) * silu_grad(before)).astype(jnp.bfloat16)
        padded_grad = jnp.pad(dbefore, ((0, 0), (0, 0), (1, 1), (0, 0)))
        grad_spatial, dinputs = spatial_backward(padded, padded_grad, upper_ok, lower_ok, w_spatial)
        return (logit_values.astype(jnp.bfloat16), dinputs.reshape(FRAMES, C, Z, H, W), grad_spatial, grad_temporal, grad_head)
    logits, grad_inputs, spatial_all, temporal_all, head_all = lax.map(one_sample, (inputs, targets, valid))
    return (logits, grad_inputs, lax.optimization_barrier(jnp.sum(spatial_all, axis=0)), lax.optimization_barrier(jnp.sum(temporal_all, axis=0)), lax.optimization_barrier(jnp.sum(head_all, axis=0)))
```

```python
import functools

import jax
import jax.numpy as jnp
from jax import lax
from jax.experimental import pallas as pl
from jax.experimental.pallas import tpu as pltpu
from jax.sharding import PartitionSpec as P

EPS = 1e-06
HALO = 6
F32 = jnp.float32
BF16 = jnp.bfloat16


def sigmoid(u):
    return 0.5 * jnp.tanh(0.5 * u) + 0.5


def dot_nn(a, b):
    return jnp.dot(a, b, preferred_element_type=F32)


def dot_nt(a, b):
    return lax.dot_general(a, b, (((1,), (1,)), ((), ())), preferred_element_type=F32)


def channel_sum(v):
    return jnp.sum(v, axis=0, keepdims=True)


def layer_kernel(
    dims,
    meta_ref,
    weight_ref,
    x_ref,
    wf_ref,
    wb_ref,
    wt_ref,
    wtb_ref,
    wh_ref,
    whc_ref,
    tgt_ref,
    logit_ref,
    dx_ref,
    gs_ref,
    gt_ref,
    gh_ref,
    xt,
    xs,
    xtmp,
    ds,
    feats,
    spre,
    n0,
    inv0,
    h1,
    n1,
    inv1,
    sp0,
    dh2,
    dm1,
    dm0,
):
    own, chans, rows, width, total = dims
    vox = rows * width
    step = 2 * width
    lo, hi = HALO, HALO + own
    first = meta_ref[0]
    lane = lax.broadcasted_iota(jnp.int32, (chans, width), 1)
    not_first = (lane > 0).astype(F32)
    not_last = (lane < width - 1).astype(F32)

    def frame_ok(f):
        g = first + f - HALO
        return jnp.where((g >= 0) & (g < total), 1.0, 0.0).astype(F32)

    def spread(row, dst, r, order):
        prev = pltpu.roll(row, 1, 1) * not_first
        nxt = pltpu.roll(row, width - 1, 1) * not_last
        parts = (prev, row, nxt) if order > 0 else (nxt, row, prev)
        for j in range(3):
            dst[j * chans : (j + 1) * chans, r * width : (r + 1) * width] = parts[j].astype(BF16)

    def conv(w_ref, src, sign):
        outs = [dot_nn(w_ref[...], src[:, p * step : (p + 1) * step]) for p in range(vox // step)]

        def piece(i, r):
            block = outs[r // 2]
            return block[i * chans : (i + 1) * chans, (r % 2) * width : (r % 2 + 1) * width]

        result = []
        for r in range(rows):
            acc = piece(1, r)
            for i in (-1, 1):
                rr = r + sign * i
                if 0 <= rr < rows:
                    acc = acc + piece(i + 1, rr)
            result.append(acc)
        return result

    def forward(f, keep):
        xt[...] = x_ref[f].astype(F32)
        dst = xs.at[f - HALO] if keep else xtmp
        for r in range(rows):
            spread(xt[pl.ds(r, chans, stride=rows), :], dst, r, 1)
        pre_rows = conv(wf_ref, dst, 1)
        for r in range(rows):
            cols = slice(r * width, (r + 1) * width)
            pre = pre_rows[r]
            s = sigmoid(pre)
            y = pre * s
            feat = y.astype(BF16)
            feats[f, :, cols] = feat
            if keep:
                spre[f - HALO, :, cols] = s + y * (1.0 - s)
            hid = feat.astype(F32)
            inv = lax.rsqrt(channel_sum(hid * hid) * (1.0 / chans) + EPS)
            n0[f, :, cols] = (hid * inv).astype(BF16)
            if keep:
                inv0[f - HALO, :, cols] = inv

    def loop(a, b, fn):
        lax.fori_loop(a, b, lambda f, c: (fn(f), c)[1], 0)

    loop(0, lo, lambda f: forward(f, False))
    loop(lo, hi, lambda f: forward(f, True))
    loop(hi, hi + HALO, lambda f: forward(f, False))

    def stack(ref, f0, f1, f2, cols):
        return jnp.concatenate([ref[f0, :, cols], ref[f1, :, cols], ref[f2, :, cols]], axis=0)

    chunks = [slice(p * step, (p + 1) * step) for p in range(vox // step)]

    def layer0(f):
        ok = frame_ok(f)
        for cols in chunks:
            mixed = dot_nn(wt_ref[0], stack(n0, f - 1, f, f + 1, cols))
            s = sigmoid(mixed)
            y = mixed * s
            hid = feats[f, :, cols].astype(F32) + y
            inv = lax.rsqrt(channel_sum(hid * hid) * (1.0 / chans) + EPS) * ok
            h1[f, :, cols] = hid
            n1[f, :, cols] = (hid * inv).astype(BF16)
            inv1[f, :, cols] = inv
            sp0[f, :, cols] = s + y * (1.0 - s)

    loop(1, hi + HALO - 1, layer0)

    gh_ref[...] = jnp.zeros_like(gh_ref)
    gt_ref[...] = jnp.zeros_like(gt_ref)
    gs_ref[...] = jnp.zeros_like(gs_ref)

    def layer1(f):
        weight = weight_ref[f - 3]
        mine = jnp.where((f >= lo) & (f < hi), 1.0, 0.0).astype(F32)
        for cols in chunks:
            mixed = dot_nn(wt_ref[1], stack(n1, f - 2, f, f + 2, cols))
            s = sigmoid(mixed)
            y = mixed * s
            hid = h1[f, :, cols] + y
            inv = lax.rsqrt(channel_sum(hid * hid) * (1.0 / chans) + EPS)
            unit = hid * inv
            final = unit.astype(BF16)
            logit = dot_nn(wh_ref[...], final)[0:1]
            logit_ref[f - 3, :, cols] = logit
            dlogit = weight * (sigmoid(logit) - tgt_ref[f - 3, :, cols].astype(F32))
            gh_ref[...] += dot_nt(jnp.broadcast_to((dlogit * mine).astype(BF16), (16, step)), final)
            dhid = (inv * dlogit) * (whc_ref[...] - unit * (logit * (1.0 / chans)))
            dh2[f, :, cols] = dhid
            dm1[f, :, cols] = (dhid * (s + y * (1.0 - s))).astype(BF16)

    loop(3, hi + 3, layer1)

    def back1(f):
        ok = frame_ok(f)
        for cols in chunks:
            dnorm = dot_nn(wtb_ref[1], stack(dm1, f + 2, f, f - 2, cols))
            unit = n1[f, :, cols].astype(F32)
            mean = channel_sum(dnorm * unit) * (1.0 / chans)
            dhid = dh2[f, :, cols] + inv1[f, :, cols] * (dnorm - unit * mean)
            dh2[f, :, cols] = dhid
            dm0[f, :, cols] = (dhid * (sp0[f, :, cols] * ok)).astype(BF16)

    loop(lo - 1, hi + 1, back1)

    def back0(f):
        b = f - HALO
        for p, cols in enumerate(chunks):
            near0 = stack(dm0, f + 1, f, f - 1, cols)
            dnorm = dot_nn(wtb_ref[0], near0)
            unit = n0[f, :, cols].astype(F32)
            mean = channel_sum(dnorm * unit) * (1.0 / chans)
            dhid = dh2[f, :, cols] + inv0[b, :, cols] * (dnorm - unit * mean)
            dfeat = dhid.astype(BF16).astype(F32)
            dpre = (dfeat * spre[b, :, cols]).astype(BF16).astype(F32)
            for r in range(2):
                spread(dpre[:, r * width : (r + 1) * width], ds, 2 * p + r, -1)
        dx_rows = conv(wb_ref, ds, -1)
        for r in range(rows):
            xt[pl.ds(r, chans, stride=rows), :] = dx_rows[r]
        dx_ref[b] = xt[...].astype(BF16)
        center = ds[chans : 2 * chans, :]
        blank = jnp.zeros((chans, width), BF16)
        taller = jnp.concatenate([center[:, width:], blank], axis=1)
        lower = jnp.concatenate([blank, center[:, :-width]], axis=1)
        gs_ref[...] += dot_nt(jnp.concatenate([taller, center, lower], axis=0), xs[b])
        every = slice(0, vox)
        gt_ref[0] += dot_nt(dm0[f], stack(n0, f - 1, f, f + 1, every))
        gt_ref[1] += dot_nt(dm1[f], stack(n1, f - 2, f, f + 2, every))

    loop(lo, hi, back0)


def run_layer(meta, weights, x, wf, wb, wt, wtb, wh, whc, tgt, dims):
    own, chans, rows, width, total = dims
    vox = rows * width
    every = own + 2 * HALO
    sds = jax.ShapeDtypeStruct
    smem = pl.BlockSpec(memory_space=pltpu.SMEM)
    vmem = pl.BlockSpec(memory_space=pltpu.VMEM)
    return pl.pallas_call(
        functools.partial(layer_kernel, dims),
        name="block",
        out_shape=(
            sds((own + 6, 1, vox), F32),
            sds((own, chans * rows, width), BF16),
            sds((3 * chans, 3 * chans), F32),
            sds((2, chans, 3 * chans), F32),
            sds((16, chans), F32),
        ),
        in_specs=[smem, smem] + [vmem] * 8,
        out_specs=[vmem] * 5,
        scratch_shapes=[
            pltpu.VMEM((chans * rows, width), F32),
            pltpu.VMEM((own, 3 * chans, vox), BF16),
            pltpu.VMEM((3 * chans, vox), BF16),
            pltpu.VMEM((3 * chans, vox), BF16),
            pltpu.VMEM((every, chans, vox), BF16),
            pltpu.VMEM((own, chans, vox), F32),
            pltpu.VMEM((every, chans, vox), BF16),
            pltpu.VMEM((own, 1, vox), F32),
            pltpu.VMEM((every, chans, vox), F32),
            pltpu.VMEM((every, chans, vox), BF16),
            pltpu.VMEM((every, 1, vox), F32),
            pltpu.VMEM((every, chans, vox), F32),
            pltpu.VMEM((every, chans, vox), F32),
            pltpu.VMEM((every, chans, vox), BF16),
            pltpu.VMEM((every, chans, vox), BF16),
        ],
        compiler_params=pltpu.CompilerParams(vmem_limit_bytes=56 * 1024 * 1024),
        cost_estimate=pl.CostEstimate(
            flops=4_000_000_000, bytes_accessed=6_000_000, transcendentals=1_000_000
        ),
    )(meta, weights, x, wf, wb, wt, wtb, wh, whc, tgt)


def group_size(tiles, frames_here, layers):
    for g in range(1, layers + 1):
        if layers % g == 0 and tiles % g == 0 and g * frames_here >= HALO:
            return g
    return layers


def pick(parts, start):
    doubled = jnp.stack(parts + parts)
    return lax.dynamic_slice_in_dim(doubled, start, len(parts), 0)


def body(inputs, w_spatial, w_temporal, w_head, targets, valid):
    _, here, chans, layers, rows, width = inputs.shape
    tiles = lax.axis_size("tile")
    total = here * tiles
    g = group_size(tiles, here, layers)
    per = layers // g
    own = g * here
    groups = tiles // g
    vox = rows * width
    t = lax.axis_index("tile")
    q, m = t // g, t % g
    spot = targets.shape[2]
    share = tiles // g
    x = inputs[0].reshape(here, chans, layers, rows * width)
    x = x.reshape(here, chans, g, per, rows, width)

    def swap(value, s):
        pairs = [(a, a // g * g + (a % g + s) % g) for a in range(tiles)]
        return lax.ppermute(value, "tile", pairs)

    def hop(value, d):
        pairs = [(a, a + d * g) for a in range(tiles) if 0 <= a + d * g < tiles]
        return lax.ppermute(value, "tile", pairs)

    def of_member(k):
        return lax.dynamic_index_in_dim(x, k % g, 2, False)

    w9 = w_spatial.reshape(3, 3, chans, chans)
    wf = w9.transpose(0, 2, 1, 3).reshape(3 * chans, 3 * chans)
    wb = w9.transpose(0, 3, 1, 2).reshape(3 * chans, 3 * chans)
    wt = w_temporal.transpose(0, 2, 1, 3).reshape(2, chans, 3 * chans)
    wtb = w_temporal.transpose(0, 3, 1, 2).reshape(2, chans, 3 * chans)
    wh = jnp.broadcast_to(w_head[None, :], (16, chans))
    whc = w_head.astype(F32)[:, None]

    around = lax.all_gather(targets[0], "tile", axis=0, tiled=False)
    mine = lax.dynamic_slice_in_dim(around, m * share, share, 0)
    mine = mine.transpose(1, 0, 2).reshape(total, per, vox)
    mine = jnp.pad(mine, ((3, 3), (0, 0), (0, 0)))
    mine = lax.dynamic_slice_in_dim(mine, q * own, own + 6, 0)
    frame_weight = jnp.pad(valid[0].astype(F32) / total, (3, 3))
    frame_weight = lax.dynamic_slice_in_dim(frame_weight, q * own, own + 6, 0)
    meta = (q * own)[None].astype(jnp.int32)

    dims = (own, chans, rows, width, total)
    results = []
    for layer in range(per):
        pieces = [of_member(m)[:, :, layer]]
        for s in range(1, g):
            pieces.append(swap(of_member(m + s)[:, :, layer], s))
        block = pick(pieces[::-1], g - 1 - m).reshape(own, chans, rows, width)
        before, after = [], []
        left = HALO
        d = 1
        while left > 0:
            n = min(left, own)
            before.insert(0, hop(block[own - n :], d))
            after.append(hop(block[:n], -d))
            left -= n
            d += 1
        full = jnp.concatenate(before + [block] + after, axis=0)
        full = full.reshape(own + 2 * HALO, chans * rows, width)
        results.append(
            run_layer(
                meta, frame_weight, full, wf, wb, wt, wtb, wh, whc, mine[:, layer][:, None], dims
            )
        )

    back = []
    for layer in range(per):
        dx = results[layer][1].reshape(g, here, chans, rows, width)
        parts = [lax.dynamic_index_in_dim(dx, m, 0, False)]
        for s in range(1, g):
            parts.append(swap(lax.dynamic_index_in_dim(dx, (m - s) % g, 0, False), -s))
        back.append(pick(parts, (g - m) % g))
    grad = jnp.stack(back, axis=3)
    grad = grad.transpose(1, 2, 0, 3, 4, 5).reshape(1, here, chans, layers, rows, width)

    logits = jnp.concatenate([r[0][3 : 3 + own, 0] for r in results], axis=1).astype(BF16)
    logits = lax.all_gather(logits, "tile", axis=0, tiled=False)
    logits = logits.reshape(groups, g, own, share, spot)
    logits = lax.dynamic_index_in_dim(logits, t // share, 1, False)
    logits = lax.dynamic_index_in_dim(logits, t % share, 2, False)
    logits = logits.reshape(1, total, spot)

    gs = sum(r[2] for r in results).reshape(3, chans, 3, chans).transpose(1, 0, 2, 3)
    gt = sum(r[3] for r in results).reshape(2, chans, 3, chans).transpose(1, 0, 2, 3)
    gh = sum(r[4] for r in results)[0][:, None]
    flat = jnp.concatenate([gs.reshape(chans, -1), gt.reshape(chans, -1), gh], axis=1)
    flat = lax.psum_scatter(flat.astype(BF16), "rep", scatter_dimension=0, tiled=True)
    flat = lax.psum(flat, "tile").astype(F32)
    part = flat.shape[0]
    gs = flat[:, : 9 * chans].reshape(part, 9, chans).transpose(1, 0, 2)
    gt = flat[:, 9 * chans : 15 * chans].reshape(part, 2, 3, chans).transpose(1, 2, 0, 3)
    return logits, grad, gs, gt, flat[:, 15 * chans]


def solution(mesh):
    placed = (
        P("rep", "tile", None, None, None, None),
        P(),
        P(),
        P(),
        P("rep", None, "tile"),
        P("rep", None),
    )
    return jax.shard_map(
        body,
        mesh=mesh,
        in_specs=placed,
        out_specs=(
            P("rep", None, "tile"),
            P("rep", "tile", None, None, None, None),
            P(None, "rep", None),
            P(None, None, "rep", None),
            P("rep"),
        ),
        check_vma=False,
    )
```

```python
import functools

import jax
import jax.numpy as jnp
from jax import lax
from jax.experimental import pallas as pl
from jax.experimental.pallas import tpu as pltpu
from jax.sharding import PartitionSpec as P

EPS = 1e-06
HALO = 6
F32 = jnp.float32
BF16 = jnp.bfloat16
VMEM_LIMIT = 52 * 1024 * 1024


def sigmoid(u):
    return 0.5 * jnp.tanh(0.5 * u) + 0.5


def dot_nn(a, b):
    return jnp.dot(a, b, preferred_element_type=F32)


def dot_nt(a, b):
    return lax.dot_general(a, b, (((1,), (1,)), ((), ())), preferred_element_type=F32)


def channel_sum(v):
    return jnp.sum(v, axis=0, keepdims=True)


def spread(row, dst, r, order):
    chans, width = row.shape
    lane = lax.broadcasted_iota(jnp.int32, (chans, width), 1)
    prev = jnp.where(lane > 0, pltpu.roll(row, 1, 1), 0.0)
    nxt = jnp.where(lane < width - 1, pltpu.roll(row, width - 1, 1), 0.0)
    parts = (prev, row, nxt) if order > 0 else (nxt, row, prev)
    for j in range(3):
        dst[j * chans : (j + 1) * chans, r * width : (r + 1) * width] = parts[j].astype(BF16)


def conv_rows(w_ref, src, sign, rows, chans, width):
    step = 2 * width
    outs = [dot_nn(w_ref[...], src[:, p * step : (p + 1) * step]) for p in range(rows // 2)]

    def piece(i, r):
        half = slice((r % 2) * width, (r % 2 + 1) * width)
        return outs[r // 2][i * chans : (i + 1) * chans, half]

    result = []
    for r in range(rows):
        acc = piece(1, r)
        for i in (-1, 1):
            if 0 <= r + sign * i < rows:
                acc = acc + piece(i + 1, r + sign * i)
        result.append(acc)
    return result


def forward_kernel(meta_ref, x_ref, wf_ref, feat_ref, slope_ref, xs_ref, xt):
    _, chans, _, rows, width = x_ref.shape
    xt[...] = x_ref[0, :, 0].astype(F32).reshape(chans * rows, width)
    dst = xs_ref.at[0]
    for r in range(rows):
        spread(xt[pl.ds(r, chans, stride=rows), :], dst, r, 1)
    for r, pre in enumerate(conv_rows(wf_ref, dst, 1, rows, chans, width)):
        cols = slice(r * width, (r + 1) * width)
        s = sigmoid(pre)
        y = pre * s
        feat_ref[0, :, cols] = y.astype(BF16)
        slope_ref[0, :, cols] = (s + y * (1.0 - s)).astype(BF16)


def run_forward(layer, x, wf):
    n, chans, _, rows, width = x.shape
    vox = rows * width
    sds = jax.ShapeDtypeStruct
    return pl.pallas_call(
        forward_kernel,
        name="conv_forward",
        out_shape=(
            sds((n, chans, vox), BF16),
            sds((n, chans, vox), BF16),
            sds((n, 3 * chans, vox), BF16),
        ),
        grid_spec=pltpu.PrefetchScalarGridSpec(
            num_scalar_prefetch=1,
            grid=(n,),
            in_specs=[
                pl.BlockSpec((1, chans, 1, rows, width), lambda f, meta: (f, 0, meta[0], 0, 0)),
                pl.BlockSpec((3 * chans, 3 * chans), lambda f, meta: (0, 0)),
            ],
            out_specs=[
                pl.BlockSpec((1, chans, vox), lambda f, meta: (f, 0, 0)),
                pl.BlockSpec((1, chans, vox), lambda f, meta: (f, 0, 0)),
                pl.BlockSpec((1, 3 * chans, vox), lambda f, meta: (f, 0, 0)),
            ],
            scratch_shapes=[pltpu.VMEM((chans * rows, width), F32)],
        ),
        cost_estimate=pl.CostEstimate(
            flops=2 * n * 9 * chans * chans * vox,
            bytes_accessed=n * chans * vox * 12,
            transcendentals=n * chans * vox,
        ),
    )(layer, x, wf)


def backward_kernel(aliased, meta_ref, dpre_ref, wb_ref, *rest):
    dx_ref, ds, xt = rest[-3:]
    _, chans, _, rows, width = dx_ref.shape
    for r in range(rows):
        spread(dpre_ref[0, :, r * width : (r + 1) * width].astype(F32), ds, r, -1)
    for r, row in enumerate(conv_rows(wb_ref, ds, -1, rows, chans, width)):
        xt[pl.ds(r, chans, stride=rows), :] = row
    dx_ref[0, :, 0] = xt[...].astype(BF16).reshape(chans, rows, width)


def run_backward(meta, dpre, wb, n, layers, rows, into):
    chans, vox = dpre.shape[1:]
    width = vox // rows
    aliased = into is not None
    return pl.pallas_call(
        functools.partial(backward_kernel, aliased),
        name="conv_backward",
        out_shape=jax.ShapeDtypeStruct((n, chans, layers, rows, width), BF16),
        grid_spec=pltpu.PrefetchScalarGridSpec(
            num_scalar_prefetch=1,
            grid=(n,),
            in_specs=[
                pl.BlockSpec((1, chans, vox), lambda f, meta: (meta[0] + f, 0, 0)),
                pl.BlockSpec((3 * chans, 3 * chans), lambda f, meta: (0, 0)),
            ]
            + [pl.BlockSpec(memory_space=pl.ANY)] * aliased,
            out_specs=pl.BlockSpec(
                (1, chans, 1, rows, width), lambda f, meta: (f, 0, meta[1], 0, 0)
            ),
            scratch_shapes=[
                pltpu.VMEM((3 * chans, vox), BF16),
                pltpu.VMEM((chans * rows, width), F32),
            ],
        ),
        input_output_aliases={3: 0} if aliased else {},
        cost_estimate=pl.CostEstimate(
            flops=2 * n * 9 * chans * chans * vox,
            bytes_accessed=n * chans * vox * 4,
            transcendentals=0,
        ),
    )(meta, dpre, wb, *([into] if aliased else []))


def temporal_kernel(
    counts,
    dims,
    meta_ref,
    weight_ref,
    wt_ref,
    wtb_ref,
    whc_ref,
    tgt_ref,
    init_ref,
    *rest,
):
    own, chans, vox, total, members, width = dims
    here = own // members
    pieces = rest[: len(counts)]
    slope_in = rest[len(counts) : len(counts) + members]
    xs_in = rest[len(counts) + members : len(counts) + 2 * members]
    (
        logit_ref,
        dpre_ref,
        grad_ref,
        feats,
        slope,
        xs,
        n0,
        inv0,
        h1,
        n1,
        inv1,
        sp0,
        dh2,
        dm1,
        dm0,
        final_ref,
        dlog,
        sems,
    ) = rest[len(counts) + 2 * members :]
    step = min(256, vox)
    lo, hi = HALO, HALO + own
    first = meta_ref[0]
    chunks = [slice(p * step, (p + 1) * step) for p in range(vox // step)]
    whole = slice(0, vox)

    early = [
        pltpu.make_async_copy(src, feats.at[pl.ds(meta_ref[1 + k], n)], sems.at[k])
        for k, (src, n) in enumerate(zip(pieces, counts))
    ]
    late = []
    for k in range(members):
        spot = pl.ds(meta_ref[1 + k] - HALO, here)
        late.append(pltpu.make_async_copy(slope_in[k], slope.at[spot], sems.at[len(early) + k]))
        late.append(
            pltpu.make_async_copy(xs_in[k], xs.at[spot], sems.at[len(early) + members + k])
        )
    for copy in early + late:
        copy.start()
    for copy in early:
        copy.wait()

    def frame_ok(f):
        g = first + f - HALO
        return jnp.where((g >= 0) & (g < total), 1.0, 0.0).astype(F32)

    def loop(a, b, *fns):
        def every(f, carry):
            for fn in fns:
                fn(f)
            return carry

        lax.fori_loop(a, b, every, 0)

    def stack(ref, f0, f1, f2, cols):
        return jnp.concatenate([ref[f0, :, cols], ref[f1, :, cols], ref[f2, :, cols]], axis=0)

    def rms(hid):
        return lax.rsqrt(channel_sum(hid * hid) * (1.0 / chans) + EPS)

    def norm0(f):
        for cols in chunks:
            hid = feats[f, :, cols].astype(F32)
            inv = rms(hid)
            n0[f, :, cols] = (hid * inv).astype(BF16)
            inv0[f, :, cols] = inv

    def layer0(f):
        ok = frame_ok(f)
        for cols in chunks:
            mixed = dot_nn(wt_ref[0], stack(n0, f - 1, f, f + 1, cols))
            s = sigmoid(mixed)
            y = mixed * s
            hid = feats[f, :, cols].astype(F32) + y
            inv = rms(hid) * ok
            h1[f, :, cols] = hid
            n1[f, :, cols] = (hid * inv).astype(BF16)
            inv1[f, :, cols] = inv
            sp0[f, :, cols] = s + y * (1.0 - s)

    def layer1(f):
        weight = weight_ref[f - 3]
        for cols in chunks:
            mixed = dot_nn(wt_ref[1], stack(n1, f - 2, f, f + 2, cols))
            s = sigmoid(mixed)
            y = mixed * s
            hid = h1[f, :, cols] + y
            inv = rms(hid)
            unit = hid * inv
            final = unit.astype(BF16)
            logit = channel_sum(final.astype(F32) * whc_ref[...])
            logit_ref[f - 3, :, cols] = logit
            dlogit = weight * (sigmoid(logit) - tgt_ref[f - 3, :, cols].astype(F32))
            final_ref[f, :, cols] = final
            dlog[f, :, cols] = dlogit
            dhid = (inv * dlogit) * (whc_ref[...] - unit * (logit * (1.0 / chans)))
            dh2[f, :, cols] = dhid
            dm1[f, :, cols] = (dhid * (s + y * (1.0 - s))).astype(BF16)

    def back1(f):
        ok = frame_ok(f)
        for cols in chunks:
            dnorm = dot_nn(wtb_ref[1], stack(dm1, f + 2, f, f - 2, cols))
            unit = n1[f, :, cols].astype(F32)
            mean = channel_sum(dnorm * unit) * (1.0 / chans)
            dhid = dh2[f, :, cols] + inv1[f, :, cols] * (dnorm - unit * mean)
            dh2[f, :, cols] = dhid
            dm0[f, :, cols] = (dhid * (sp0[f, :, cols] * ok)).astype(BF16)

    def back0(f):
        b = f - HALO
        for cols in chunks:
            dnorm = dot_nn(wtb_ref[0], stack(dm0, f + 1, f, f - 1, cols))
            unit = n0[f, :, cols].astype(F32)
            mean = channel_sum(dnorm * unit) * (1.0 / chans)
            dhid = dh2[f, :, cols] + inv0[f, :, cols] * (dnorm - unit * mean)
            dfeat = dhid.astype(BF16).astype(F32)
            dpre_ref[b, :, cols] = (dfeat * slope[b, :, cols].astype(F32)).astype(BF16)

    def weights(f):
        b = f - HALO
        center = dpre_ref[b]
        blank = jnp.zeros((chans, width), BF16)
        taller = jnp.concatenate([center[:, width:], blank], axis=1)
        lower = jnp.concatenate([blank, center[:, :-width]], axis=1)
        for i, rows in enumerate((taller, center, lower)):
            grad_ref[i] += dot_nt(rows, xs[b])
        grad_ref[3] += dot_nt(dm0[f], stack(n0, f - 1, f, f + 1, whole))
        grad_ref[4] += dot_nt(dm1[f], stack(n1, f - 2, f, f + 2, whole))
        head = jnp.broadcast_to(dlog[f].astype(BF16), (chans, vox))
        grad_ref[5, :, :chans] += dot_nt(head, final_ref[f])

    grad_ref[...] = init_ref[...]
    loop(0, hi + HALO, norm0)
    loop(1, hi + HALO - 1, layer0)
    loop(3, hi + 3, layer1)
    loop(lo - 1, hi + 1, back1)
    for copy in late:
        copy.wait()
    loop(lo, hi, back0)
    loop(lo, hi, weights)


def run_temporal(meta, weights, wt, wtb, whc, tgt, init, pieces, slopes, xss, own, width, total):
    counts = tuple(p.shape[0] for p in pieces)
    members = len(slopes)
    chans, vox = pieces[0].shape[1:]
    every = own + 2 * HALO
    sds = jax.ShapeDtypeStruct
    smem = pl.BlockSpec(memory_space=pltpu.SMEM)
    vmem = pl.BlockSpec(memory_space=pltpu.VMEM)
    hbm = pl.BlockSpec(memory_space=pl.ANY)
    loose = len(pieces) + 2 * members
    frame = lambda n, c, dt: pltpu.VMEM((n, c, vox), dt)
    return pl.pallas_call(
        functools.partial(temporal_kernel, counts, (own, chans, vox, total, members, width)),
        name="temporal",
        out_shape=(
            sds((own + 6, 1, vox), F32),
            sds((own, chans, vox), BF16),
            sds((6, chans, 3 * chans), F32),
        ),
        in_specs=[smem, smem] + [vmem] * 5 + [hbm] * loose,
        out_specs=[vmem] * 3,
        scratch_shapes=[
            frame(every, chans, BF16),
            frame(own, chans, BF16),
            frame(own, 3 * chans, BF16),
            frame(every, chans, BF16),
            frame(every, 1, F32),
            frame(every, chans, F32),
            frame(every, chans, BF16),
            frame(every, 1, F32),
            frame(every, chans, F32),
            frame(every, chans, F32),
            frame(every, chans, BF16),
            frame(every, chans, BF16),
            frame(every, chans, BF16),
            frame(every, 1, F32),
            pltpu.SemaphoreType.DMA((loose,)),
        ],
        compiler_params=pltpu.CompilerParams(vmem_limit_bytes=VMEM_LIMIT),
        cost_estimate=pl.CostEstimate(
            flops=60 * own * 6 * chans * chans * vox,
            bytes_accessed=40 * own * chans * vox,
            transcendentals=6 * own * chans * vox,
        ),
    )(meta, weights, wt, wtb, whc, tgt, init, *pieces, *slopes, *xss)


def group_size(tiles, frames_here, layers):
    for g in range(1, layers + 1):
        if layers % g == 0 and tiles % g == 0 and g * frames_here >= HALO:
            return g
    return layers


def pick(parts, start):
    doubled = jnp.stack(parts + parts)
    return lax.dynamic_slice_in_dim(doubled, start, len(parts), 0)


def take(value, index, axis):
    return lax.dynamic_index_in_dim(value, index, axis, False)


def sum_over_tiles(value, tiles):
    if tiles & (tiles - 1):
        return lax.psum(value.astype(BF16), "tile").astype(F32)
    k = 1
    while k < tiles:
        pairs = [(a, a ^ k) for a in range(tiles)]
        value = value + lax.ppermute(value.astype(BF16), "tile", pairs).astype(F32)
        k *= 2
    return value


def sum_over_reps(value, axis):
    reps = lax.axis_size("rep")
    r = lax.axis_index("rep")
    n = value.shape[axis] // reps

    def share(k):
        return lax.dynamic_slice_in_dim(value, (k % reps) * n, n, axis)

    acc = share(r)
    for s in range(1, reps):
        pairs = [(a, (a + s) % reps) for a in range(reps)]
        acc = acc + lax.ppermute(share(r + s).astype(BF16), "rep", pairs).astype(F32)
    return acc


def body(inputs, w_spatial, w_temporal, w_head, targets, valid):
    _, here, chans, layers, rows, width = inputs.shape
    tiles = lax.axis_size("tile")
    total = here * tiles
    g = group_size(tiles, here, layers)
    per = layers // g
    own = g * here
    vox = rows * width
    t = lax.axis_index("tile")
    q, m = t // g, t % g
    spot = targets.shape[2]
    share = tiles // g
    x = inputs[0]
    apart = x.reshape(here, chans, g, per, rows, width)

    def swap(value, s):
        pairs = [(a, a // g * g + (a % g + s) % g) for a in range(tiles)]
        return lax.ppermute(value, "tile", pairs)

    def hop(value, shifts):
        pairs = [(a, a + shifts[a % g] * g) for a in range(tiles)]
        return lax.ppermute(value, "tile", [p for p in pairs if 0 <= p[1] < tiles])

    arriving = [
        [swap(take(apart, (m + s) % g, 2)[:, :, layer], s) for s in range(1, g)]
        for layer in range(per)
    ]

    w9 = w_spatial.reshape(3, 3, chans, chans)
    wf = w9.transpose(0, 2, 1, 3).reshape(3 * chans, 3 * chans)
    wb = w9.transpose(0, 3, 1, 2).reshape(3 * chans, 3 * chans)
    wt = w_temporal.transpose(0, 2, 1, 3).reshape(2, chans, 3 * chans)
    wtb = w_temporal.transpose(0, 3, 1, 2).reshape(2, chans, 3 * chans)
    whc = w_head.astype(F32)[:, None]

    window = jnp.pad(targets[0], ((3, 3), (0, 0)))
    parts = []
    for r in range(share):
        piece = lax.dynamic_slice_in_dim(window, ((t % share - r) % share) * own, own + 6, 0)
        pairs = [(a, (a % share - r) % share * g + a // share) for a in range(tiles)]
        parts.append(lax.ppermute(piece, "tile", pairs))
    tgt = pick(parts, (-q) % share).transpose(1, 0, 2).reshape(own + 6, per, 1, vox)
    frame_weight = jnp.pad(valid[0].astype(F32) / total, (3, 3))
    frame_weight = lax.dynamic_slice_in_dim(frame_weight, q * own, own + 6, 0)

    grads = jnp.zeros((6, chans, 3 * chans), F32)
    logits, out, backs = [], None, []
    mirrored = g == 2 and here <= HALO <= 2 * here
    for layer in range(per):
        index = (m * per + layer).astype(jnp.int32)
        done = [run_forward(index[None], x, wf)]
        for piece in arriving[layer]:
            done.append(run_forward(jnp.zeros((1,), jnp.int32), piece[:, :, None], wf))
        pieces = [d[0] for d in done]
        places = [HALO + (m - s) % g * here for s in range(g)]
        if mirrored:
            n = HALO - here
            up, down = own + HALO, HALO - here
            for k, full in enumerate(pieces[:2]):
                away, toward = ((-1, 1), (1, -1)) if k == 0 else ((1, -1), (-1, 1))
                pieces.append(hop(full, away))
                places.append(jnp.where(m == k, up, down))
                if n:
                    start = jnp.where(m == k, here - n, 0)
                    pieces.append(hop(lax.dynamic_slice_in_dim(full, start, n, 0), toward))
                    places.append(jnp.where(m == k, 0, up + here))
        else:
            block = pick(pieces[::-1], g - 1 - m).reshape(own, chans, vox)
            left, d = HALO, 1
            while left > 0:
                n = min(left, own)
                pieces.append(hop(block[own - n :], (d,) * g))
                places.append(left - n)
                pieces.append(hop(block[:n], (-d,) * g))
                places.append(HALO + d * own)
                left -= n
                d += 1
        meta = jnp.stack([jnp.asarray(v, jnp.int32) for v in [q * own] + places])
        logit, dpre, grads = run_temporal(
            meta,
            frame_weight,
            wt,
            wtb,
            whc,
            tgt[:, layer],
            grads,
            pieces,
            [d[1] for d in done],
            [d[2] for d in done],
            own,
            width,
            total,
        )
        logits.append(logit[3 : 3 + own, 0])
        zero = jnp.zeros((), jnp.int32)
        for s in range(1, g):
            frames = jnp.stack([((m - s) % g * here).astype(jnp.int32), zero])
            dx = run_backward(frames, dpre, wb, here, 1, rows, None)
            backs.append(((m + s) % g * per + layer, swap(dx, -s)))
        frames = jnp.stack([(m * here).astype(jnp.int32), index])
        out = run_backward(frames, dpre, wb, here, layers, rows, out)
    for index, dx in backs:
        out = lax.dynamic_update_slice_in_dim(out, dx, index, 2)

    grads = sum_over_tiles(sum_over_reps(grads, 1), tiles)
    part = grads.shape[1]
    gs = grads[:3].reshape(3, part, 3, chans).transpose(0, 2, 1, 3).reshape(9, part, chans)
    gt = grads[3:5].reshape(2, part, 3, chans).transpose(0, 2, 1, 3)
    gh = lax.dynamic_slice_in_dim(grads[5, 0], lax.axis_index("rep") * part, part, 0)

    logits = jnp.concatenate(logits, axis=1).astype(BF16).reshape(own, share, spot)
    parts = []
    for r in range(share):
        pairs = [(a, a % g * share + (a // g - r) % share) for a in range(tiles)]
        parts.append(lax.ppermute(take(logits, (q - r) % share, 1), "tile", pairs))
    logits = pick(parts, (-t) % share).reshape(1, total, spot)
    return logits, out[None], gs, gt, gh


def solution(mesh):
    placed = (
        P("rep", "tile", None, None, None, None),
        P(),
        P(),
        P(),
        P("rep", None, "tile"),
        P("rep", None),
    )
    return jax.shard_map(
        body,
        mesh=mesh,
        in_specs=placed,
        out_specs=(
            P("rep", None, "tile"),
            P("rep", "tile", None, None, None, None),
            P(None, "rep", None),
            P(None, None, "rep", None),
            P("rep"),
        ),
        check_vma=False,
    )
```

```python
import functools

import jax
import jax.numpy as jnp
from jax import lax
from jax.experimental import pallas as pl
from jax.experimental.pallas import tpu as pltpu
from jax.sharding import PartitionSpec as P

EPS = 1e-06
HALO = 6
F32 = jnp.float32
BF16 = jnp.bfloat16
VMEM_LIMIT = 52 * 1024 * 1024


def sigmoid(u):
    return 0.5 * jnp.tanh(0.5 * u) + 0.5


def dot_nn(a, b):
    return jnp.dot(a, b, preferred_element_type=F32)


def dot_nt(a, b):
    return lax.dot_general(a, b, (((1,), (1,)), ((), ())), preferred_element_type=F32)


def channel_sum(v):
    return jnp.sum(v, axis=0, keepdims=True)


def spread(row, dst, r, order):
    chans, width = row.shape
    lane = lax.broadcasted_iota(jnp.int32, (chans, width), 1)
    prev = jnp.where(lane > 0, pltpu.roll(row, 1, 1), 0.0)
    nxt = jnp.where(lane < width - 1, pltpu.roll(row, width - 1, 1), 0.0)
    parts = (prev, row, nxt) if order > 0 else (nxt, row, prev)
    for j in range(3):
        dst[j * chans : (j + 1) * chans, r * width : (r + 1) * width] = parts[j].astype(BF16)


def conv_rows(w_ref, src, sign, rows, chans, width):
    step = 2 * width
    outs = [dot_nn(w_ref[...], src[:, p * step : (p + 1) * step]) for p in range(rows // 2)]

    def piece(i, r):
        half = slice((r % 2) * width, (r % 2 + 1) * width)
        return outs[r // 2][i * chans : (i + 1) * chans, half]

    result = []
    for r in range(rows):
        acc = piece(1, r)
        for i in (-1, 1):
            if 0 <= r + sign * i < rows:
                acc = acc + piece(i + 1, r + sign * i)
        result.append(acc)
    return result


def forward_kernel(meta_ref, x_ref, w_ref, feat_ref, slope_ref, xs_ref, xt, wf):
    _, chans, _, rows, width = x_ref.shape

    @pl.when((pl.program_id(0) == 0) & (pl.program_id(1) == 0))
    def _():
        for i in range(3):
            for j in range(3):
                wf[i * chans : (i + 1) * chans, j * chans : (j + 1) * chans] = w_ref[3 * i + j]

    xt[...] = x_ref[0, :, 0].astype(F32).reshape(chans * rows, width)
    dst = xs_ref.at[0, 0]
    for r in range(rows):
        spread(xt[pl.ds(r, chans, stride=rows), :], dst, r, 1)
    for r, pre in enumerate(conv_rows(wf, dst, 1, rows, chans, width)):
        cols = slice(r * width, (r + 1) * width)
        s = sigmoid(pre)
        y = pre * s
        feat_ref[0, 0, :, cols] = y.astype(BF16)
        slope_ref[0, 0, :, cols] = (s + y * (1.0 - s)).astype(BF16)


def run_forward(first, count, x, w_spatial):
    n, chans, _, rows, width = x.shape
    vox = rows * width
    sds = jax.ShapeDtypeStruct
    result = lambda c: pl.BlockSpec((1, 1, c, vox), lambda k, f, meta: (k, f, 0, 0))
    return pl.pallas_call(
        forward_kernel,
        name="conv_forward",
        out_shape=(
            sds((count, n, chans, vox), BF16),
            sds((count, n, chans, vox), BF16),
            sds((count, n, 3 * chans, vox), BF16),
        ),
        grid_spec=pltpu.PrefetchScalarGridSpec(
            num_scalar_prefetch=1,
            grid=(count, n),
            in_specs=[
                pl.BlockSpec(
                    (1, chans, 1, rows, width), lambda k, f, meta: (f, 0, meta[0] + k, 0, 0)
                ),
                pl.BlockSpec((9, chans, chans), lambda k, f, meta: (0, 0, 0)),
            ],
            out_specs=[result(chans), result(chans), result(3 * chans)],
            scratch_shapes=[
                pltpu.VMEM((chans * rows, width), F32),
                pltpu.VMEM((3 * chans, 3 * chans), BF16),
            ],
        ),
        cost_estimate=pl.CostEstimate(flops=1000, bytes_accessed=1000, transcendentals=0),
    )(first, x, w_spatial)


def backward_kernel(aliased, meta_ref, dpre_ref, wb_ref, *rest):
    dx_ref, ds, xt = rest[-3:]
    _, chans, _, rows, width = dx_ref.shape
    for r in range(rows):
        spread(dpre_ref[0, :, r * width : (r + 1) * width].astype(F32), ds, r, -1)
    for r, row in enumerate(conv_rows(wb_ref, ds, -1, rows, chans, width)):
        xt[pl.ds(r, chans, stride=rows), :] = row
    dx_ref[0, :, 0] = xt[...].astype(BF16).reshape(chans, rows, width)


def run_backward(meta, dpre, wb, n, layers, rows, into):
    chans, vox = dpre.shape[1:]
    width = vox // rows
    aliased = into is not None
    return pl.pallas_call(
        functools.partial(backward_kernel, aliased),
        name="conv_backward",
        out_shape=jax.ShapeDtypeStruct((n, chans, layers, rows, width), BF16),
        grid_spec=pltpu.PrefetchScalarGridSpec(
            num_scalar_prefetch=1,
            grid=(n,),
            in_specs=[
                pl.BlockSpec((1, chans, vox), lambda f, meta: (meta[0] + f, 0, 0)),
                pl.BlockSpec((3 * chans, 3 * chans), lambda f, meta: (0, 0)),
            ]
            + [pl.BlockSpec(memory_space=pl.ANY)] * aliased,
            out_specs=pl.BlockSpec(
                (1, chans, 1, rows, width), lambda f, meta: (f, 0, meta[1], 0, 0)
            ),
            scratch_shapes=[
                pltpu.VMEM((3 * chans, vox), BF16),
                pltpu.VMEM((chans * rows, width), F32),
            ],
        ),
        input_output_aliases={3: 0} if aliased else {},
        cost_estimate=pl.CostEstimate(flops=1000, bytes_accessed=1000, transcendentals=0),
    )(meta, dpre, wb, *([into] if aliased else []))


def temporal_kernel(
    places,
    inside,
    dims,
    meta_ref,
    weight_ref,
    wt_ref,
    wtb_ref,
    whc_ref,
    tgt_ref,
    init_ref,
    wb_ref,
    *rest,
):
    own, chans, vox, total, members, width = dims
    here = own // members
    counts = len(places)
    pieces = [ref.at[k] for ref, k in zip(rest[:counts], places)]
    slope_in = [ref.at[k] for ref, k in zip(rest[counts : counts + members], places)]
    xs_in = [ref.at[k] for ref, k in zip(rest[counts + members : counts + 2 * members], places)]
    (
        logit_ref,
        back_ref,
        grad_ref,
        feats,
        slope,
        xs,
        n0,
        inv0,
        h1,
        n1,
        inv1,
        sp0,
        dh2,
        dm1,
        dm0,
        dpre,
        final_ref,
        dlog,
        ds,
        xt,
        sems,
    ) = rest[counts + 2 * members :]
    step = min(256, vox)
    lo, hi = HALO, HALO + own
    first = meta_ref[0]
    chunks = [slice(p * step, (p + 1) * step) for p in range(vox // step)]
    whole = slice(0, vox)

    early = [
        pltpu.make_async_copy(src, feats.at[pl.ds(meta_ref[1 + k], src.shape[0])], sems.at[k])
        for k, src in enumerate(pieces)
    ]
    late = []
    for k in range(members):
        spot = pl.ds(meta_ref[1 + k] - HALO, here)
        late.append(pltpu.make_async_copy(slope_in[k], slope.at[spot], sems.at[len(early) + k]))
        late.append(
            pltpu.make_async_copy(xs_in[k], xs.at[spot], sems.at[len(early) + members + k])
        )
    for copy in early + late:
        copy.start()
    for copy in early:
        copy.wait()

    def frame_ok(f):
        g = first + f - HALO
        return jnp.where((g >= 0) & (g < total), 1.0, 0.0).astype(F32)

    def loop(a, b, *fns):
        def every(f, carry):
            for fn in fns:
                fn(f)
            return carry

        lax.fori_loop(a, b, every, 0)

    def stack(ref, f0, f1, f2, cols):
        return jnp.concatenate([ref[f0, :, cols], ref[f1, :, cols], ref[f2, :, cols]], axis=0)

    def rms(hid):
        return lax.rsqrt(channel_sum(hid * hid) * (1.0 / chans) + EPS)

    def norm0(f):
        for cols in chunks:
            hid = feats[f, :, cols].astype(F32)
            inv = rms(hid)
            n0[f, :, cols] = (hid * inv).astype(BF16)
            inv0[f, :, cols] = inv

    def layer0(f):
        ok = frame_ok(f)
        for cols in chunks:
            mixed = dot_nn(wt_ref[0], stack(n0, f - 1, f, f + 1, cols))
            s = sigmoid(mixed)
            y = mixed * s
            hid = feats[f, :, cols].astype(F32) + y
            inv = rms(hid) * ok
            h1[f, :, cols] = hid
            n1[f, :, cols] = (hid * inv).astype(BF16)
            inv1[f, :, cols] = inv
            sp0[f, :, cols] = s + y * (1.0 - s)

    def layer1(f):
        weight = weight_ref[f - 3]
        for cols in chunks:
            mixed = dot_nn(wt_ref[1], stack(n1, f - 2, f, f + 2, cols))
            s = sigmoid(mixed)
            y = mixed * s
            hid = h1[f, :, cols] + y
            inv = rms(hid)
            unit = hid * inv
            final = unit.astype(BF16)
            logit = channel_sum(final.astype(F32) * whc_ref[...])
            logit_ref[f - 3, :, cols] = logit
            dlogit = weight * (sigmoid(logit) - tgt_ref[f - 3, :, cols].astype(F32))
            final_ref[f, :, cols] = final
            dlog[f, :, cols] = dlogit
            dhid = (inv * dlogit) * (whc_ref[...] - unit * (logit * (1.0 / chans)))
            dh2[f, :, cols] = dhid
            dm1[f, :, cols] = (dhid * (s + y * (1.0 - s))).astype(BF16)

    def back1(f):
        ok = frame_ok(f)
        for cols in chunks:
            dnorm = dot_nn(wtb_ref[1], stack(dm1, f + 2, f, f - 2, cols))
            unit = n1[f, :, cols].astype(F32)
            mean = channel_sum(dnorm * unit) * (1.0 / chans)
            dhid = dh2[f, :, cols] + inv1[f, :, cols] * (dnorm - unit * mean)
            dh2[f, :, cols] = dhid
            dm0[f, :, cols] = (dhid * (sp0[f, :, cols] * ok)).astype(BF16)

    def back0(f):
        b = f - HALO
        for cols in chunks:
            dnorm = dot_nn(wtb_ref[0], stack(dm0, f + 1, f, f - 1, cols))
            unit = n0[f, :, cols].astype(F32)
            mean = channel_sum(dnorm * unit) * (1.0 / chans)
            dhid = dh2[f, :, cols] + inv0[f, :, cols] * (dnorm - unit * mean)
            dfeat = dhid.astype(BF16).astype(F32)
            dpre[b, :, cols] = (dfeat * slope[b, :, cols].astype(F32)).astype(BF16)

    def weights(f):
        b = f - HALO
        center = dpre[b]
        blank = jnp.zeros((chans, width), BF16)
        taller = jnp.concatenate([center[:, width:], blank], axis=1)
        lower = jnp.concatenate([blank, center[:, :-width]], axis=1)
        for i, rows in enumerate((taller, center, lower)):
            grad_ref[i] += dot_nt(rows, xs[b])
        grad_ref[3] += dot_nt(dm0[f], stack(n0, f - 1, f, f + 1, whole))
        grad_ref[4] += dot_nt(dm1[f], stack(n1, f - 2, f, f + 2, whole))
        head = jnp.broadcast_to(dlog[f].astype(BF16), (chans, vox))
        grad_ref[5, :, :chans] += dot_nt(head, final_ref[f])

    grad_ref[...] = init_ref[...]
    loop(0, hi + HALO, norm0)
    loop(1, hi + HALO - 1, layer0)
    loop(3, hi + 3, layer1)
    loop(lo - 1, hi + 1, back1)
    for copy in late:
        copy.wait()
    loop(lo, hi, back0)
    loop(lo, hi, weights)

    def inputs(b):
        rows = vox // width
        for r in range(rows):
            spread(dpre[b, :, r * width : (r + 1) * width].astype(F32), ds, r, -1)
        for r, row in enumerate(conv_rows(wb_ref, ds, -1, rows, chans, width)):
            xt[pl.ds(r, chans, stride=rows), :] = row
        back_ref[b] = xt[...].astype(BF16)

    def hand_on(b):
        back_ref[b] = dpre[b]

    loop(0, own, inputs if inside else hand_on)


def run_temporal(
    meta, weights, wt, wtb, whc, tgt, init, wb, pieces, places, slopes, xss, inside, own, width, total
):
    members = len(slopes)
    chans, vox = pieces[0].shape[2:]
    every = own + 2 * HALO
    sds = jax.ShapeDtypeStruct
    smem = pl.BlockSpec(memory_space=pltpu.SMEM)
    vmem = pl.BlockSpec(memory_space=pltpu.VMEM)
    hbm = pl.BlockSpec(memory_space=pl.ANY)
    loose = len(pieces) + 2 * members
    frame = lambda n, c, dt: pltpu.VMEM((n, c, vox), dt)
    return pl.pallas_call(
        functools.partial(
            temporal_kernel, tuple(places), inside, (own, chans, vox, total, members, width)
        ),
        name="temporal",
        out_shape=(
            sds((own + 6, 1, vox), F32),
            sds((own, chans * vox // width, width) if inside else (own, chans, vox), BF16),
            sds((6, chans, 3 * chans), F32),
        ),
        in_specs=[smem, smem] + [vmem] * 6 + [hbm] * loose,
        out_specs=[vmem] * 3,
        scratch_shapes=[
            frame(every, chans, BF16),
            frame(own, chans, BF16),
            frame(own, 3 * chans, BF16),
            frame(every, chans, BF16),
            frame(every, 1, F32),
            frame(every, chans, F32),
            frame(every, chans, BF16),
            frame(every, 1, F32),
            frame(every, chans, F32),
            frame(every, chans, F32),
            frame(every, chans, BF16),
            frame(every, chans, BF16),
            frame(own, chans, BF16),
            frame(every, chans, BF16),
            frame(every, 1, F32),
            pltpu.VMEM((3 * chans, vox), BF16),
            pltpu.VMEM((chans * vox // width, width), F32),
            pltpu.SemaphoreType.DMA((loose,)),
        ],
        compiler_params=pltpu.CompilerParams(vmem_limit_bytes=VMEM_LIMIT),
        cost_estimate=pl.CostEstimate(
            flops=1000, bytes_accessed=1000, transcendentals=0
        ),
    )(meta, weights, wt, wtb, whc, tgt, init, wb, *pieces, *slopes, *xss)


def group_size(tiles, frames_here, layers):
    for g in range(1, layers + 1):
        if layers % g == 0 and tiles % g == 0 and g * frames_here >= HALO:
            return g
    return layers


def pick(parts, start):
    doubled = jnp.stack(parts + parts)
    return lax.dynamic_slice_in_dim(doubled, start, len(parts), 0)


def take(value, index, axis):
    return lax.dynamic_index_in_dim(value, index, axis, False)


def sum_over_tiles(value, tiles):
    if tiles & (tiles - 1):
        return lax.psum(value.astype(BF16), "tile").astype(F32)
    k = 1
    while k < tiles:
        pairs = [(a, a ^ k) for a in range(tiles)]
        value = value + lax.ppermute(value.astype(BF16), "tile", pairs).astype(F32)
        k *= 2
    return value


def sum_over_reps(value, axis):
    reps = lax.axis_size("rep")
    r = lax.axis_index("rep")
    n = value.shape[axis] // reps

    def share(k):
        return lax.dynamic_slice_in_dim(value, (k % reps) * n, n, axis)

    acc = share(r)
    for s in range(1, reps):
        pairs = [(a, (a + s) % reps) for a in range(reps)]
        acc = acc + lax.ppermute(share(r + s).astype(BF16), "rep", pairs).astype(F32)
    return acc


def body(inputs, w_spatial, w_temporal, w_head, targets, valid):
    _, here, chans, layers, rows, width = inputs.shape
    tiles = lax.axis_size("tile")
    total = here * tiles
    g = group_size(tiles, here, layers)
    per = layers // g
    own = g * here
    vox = rows * width
    t = lax.axis_index("tile")
    q, m = t // g, t % g
    spot = targets.shape[2]
    share = groups = tiles // g
    x = inputs[0]
    apart = x.reshape(here, chans, g, per, rows, width)

    def swap(value, s):
        pairs = [(a, a // g * g + (a % g + s) % g) for a in range(tiles)]
        return lax.ppermute(value, "tile", pairs)

    def hop(value, shifts):
        pairs = [(a, a + shifts[a % g] * g) for a in range(tiles)]
        return lax.ppermute(value, "tile", [p for p in pairs if 0 <= p[1] < tiles])

    arriving = [
        [swap(take(apart, (m + s) % g, 2)[:, :, layer], s) for s in range(1, g)]
        for layer in range(per)
    ]

    w9 = w_spatial.reshape(3, 3, chans, chans)
    wb = w9.transpose(0, 3, 1, 2).reshape(3 * chans, 3 * chans)
    wt = w_temporal.transpose(0, 2, 1, 3).reshape(2, chans, 3 * chans)
    wtb = w_temporal.transpose(0, 3, 1, 2).reshape(2, chans, 3 * chans)
    whc = w_head.astype(F32)[:, None]

    index = (m * per).astype(jnp.int32)
    mine = run_forward(index[None], per, x, w_spatial)
    mirrored = g == 2 and here <= HALO <= 2 * here
    n = HALO - here
    ahead = []
    if mirrored:
        ahead.append(hop(mine[0], (-1, 1)))
        if n:
            start = jnp.where(m == 0, here - n, 0)
            ahead.append(hop(lax.dynamic_slice_in_dim(mine[0], start, n, 1), (1, -1)))

    window = jnp.pad(targets[0], ((3, 3), (0, 0)))
    window = jnp.stack([window[k // g * own : k // g * own + own + 6] for k in range(tiles)])
    window = lax.all_to_all(window, "tile", 0, 0, tiled=True)
    tgt = lax.dynamic_slice_in_dim(window, m * share, share, 0)
    tgt = tgt.transpose(1, 0, 2).reshape(own + 6, per, 1, vox)
    frame_weight = jnp.pad(valid[0].astype(F32) / total, (3, 3))
    frame_weight = lax.dynamic_slice_in_dim(frame_weight, q * own, own + 6, 0)

    grads = jnp.zeros((6, chans, 3 * chans), F32)
    logits, backs = [], []
    zero = jnp.zeros((1,), jnp.int32)
    for layer in range(per):
        done = [mine]
        for piece in arriving[layer]:
            done.append(run_forward(zero, 1, piece[:, :, None], w_spatial))
        pieces = [d[0] for d in done]
        ranks = [layer] + [0] * (g - 1)
        places = [HALO + (m - s) % g * here for s in range(g)]
        if mirrored:
            up, down = own + HALO, HALO - here
            pieces += ahead
            ranks += [layer] * len(ahead)
            places += [jnp.where(m == 0, up, down), jnp.where(m == 0, 0, up + here)][: len(ahead)]
            pieces.append(hop(pieces[1], (1, -1)))
            places.append(jnp.where(m == 1, up, down))
            if n:
                start = jnp.where(m == 1, here - n, 0)
                pieces.append(hop(lax.dynamic_slice_in_dim(pieces[1], start, n, 1), (-1, 1)))
                places.append(jnp.where(m == 1, 0, up + here))
            ranks += [0] * len(ahead)
        else:
            block = [p[k] for p, k in zip(pieces, ranks)]
            block = pick(block[::-1], g - 1 - m).reshape(own, chans, vox)
            left, d = HALO, 1
            while left > 0:
                k = min(left, own)
                pieces.append(hop(block[own - k :], (d,) * g)[None])
                places.append(left - k)
                pieces.append(hop(block[:k], (-d,) * g)[None])
                places.append(HALO + d * own)
                ranks += [0, 0]
                left -= k
                d += 1
        meta = jnp.stack([jnp.asarray(v, jnp.int32) for v in [q * own] + places])
        inside = layer < per - 1
        logit, back, grads = run_temporal(
            meta,
            frame_weight,
            wt,
            wtb,
            whc,
            tgt[:, layer],
            grads,
            wb,
            pieces,
            ranks,
            [d[1] for d in done],
            [d[2] for d in done],
            inside,
            own,
            width,
            total,
        )
        logits.append(logit[3 : 3 + own, 0])
        if inside:
            back = back.reshape(g, here, chans, 1, rows, width)
            for s in range(1, g):
                dx = swap(take(back, (m - s) % g, 0), -s)
                backs.append(((m + s) % g * per + layer, dx))
            backs.append((index + layer, take(back, m, 0)))
        else:
            for s in range(1, g):
                frames = jnp.stack([((m - s) % g * here).astype(jnp.int32), zero[0]])
                dx = swap(run_backward(frames, back, wb, here, 1, rows, None), -s)
                backs.append(((m + s) % g * per + layer, dx))
            frames = jnp.stack([(m * here).astype(jnp.int32), index + layer])
            out = run_backward(frames, back, wb, here, layers, rows, None)
    for spot_z, dx in backs:
        out = lax.dynamic_update_slice_in_dim(out, dx, spot_z, 2)

    grads = sum_over_tiles(sum_over_reps(grads, 1), tiles)
    part = grads.shape[1]
    gs = grads[:3].reshape(3, part, 3, chans).transpose(0, 2, 1, 3).reshape(9, part, chans)
    gt = grads[3:5].reshape(2, part, 3, chans).transpose(0, 2, 1, 3)
    gh = lax.dynamic_slice_in_dim(grads[5, 0], lax.axis_index("rep") * part, part, 0)

    logits = jnp.concatenate(logits, axis=1).astype(BF16).reshape(own, share, spot)
    logits = logits.transpose(1, 0, 2)
    logits = jnp.concatenate([logits] * g)
    logits = lax.all_to_all(logits, "tile", 0, 0, tiled=True)
    logits = take(logits.reshape(groups, g, own, spot), t // share, 1).reshape(1, total, spot)
    return logits, out[None], gs, gt, gh


def solution(mesh):
    placed = (
        P("rep", "tile", None, None, None, None),
        P(),
        P(),
        P(),
        P("rep", None, "tile"),
        P("rep", None),
    )
    return jax.shard_map(
        body,
        mesh=mesh,
        in_specs=placed,
        out_specs=(
            P("rep", None, "tile"),
            P("rep", "tile", None, None, None, None),
            P(None, "rep", None),
            P(None, None, "rep", None),
            P("rep"),
        ),
        check_vma=False,
    )
```

```python
import functools

import jax
import jax.numpy as jnp
from jax import lax
from jax.experimental import pallas as pl
from jax.experimental.pallas import tpu as pltpu
from jax.sharding import PartitionSpec as P

EPS = 1e-06
HALO = 6
F32 = jnp.float32
BF16 = jnp.bfloat16
VMEM_LIMIT = 52 * 1024 * 1024


def sigmoid(u):
    return 0.5 * jnp.tanh(0.5 * u) + 0.5


def dot_nn(a, b):
    return jnp.dot(a, b, preferred_element_type=F32)


def dot_nt(a, b):
    return lax.dot_general(a, b, (((1,), (1,)), ((), ())), preferred_element_type=F32)


def channel_sum(v):
    return jnp.sum(v, axis=0, keepdims=True)


def spread(row, dst, r, order):
    chans, width = row.shape
    lane = lax.broadcasted_iota(jnp.int32, (chans, width), 1)
    prev = jnp.where(lane > 0, pltpu.roll(row, 1, 1), 0.0)
    nxt = jnp.where(lane < width - 1, pltpu.roll(row, width - 1, 1), 0.0)
    parts = (prev, row, nxt) if order > 0 else (nxt, row, prev)
    for j in range(3):
        dst[j * chans : (j + 1) * chans, r * width : (r + 1) * width] = parts[j].astype(BF16)


def conv_rows(w_ref, src, sign, rows, chans, width):
    step = 2 * width
    outs = [dot_nn(w_ref[...], src[:, p * step : (p + 1) * step]) for p in range(rows // 2)]

    def piece(i, r):
        half = slice((r % 2) * width, (r % 2 + 1) * width)
        return outs[r // 2][i * chans : (i + 1) * chans, half]

    result = []
    for r in range(rows):
        acc = piece(1, r)
        for i in (-1, 1):
            if 0 <= r + sign * i < rows:
                acc = acc + piece(i + 1, r + sign * i)
        result.append(acc)
    return result


def forward_kernel(middle, meta_ref, x_ref, w_ref, feat_ref, slope_ref, xc_ref, *rest):
    xt, xs, wf = rest[-3:]
    _, chans, _, rows, width = x_ref.shape

    @pl.when((pl.program_id(0) == 0) & (pl.program_id(1) == 0))
    def _():
        for i in range(3):
            for j in range(3):
                wf[i * chans : (i + 1) * chans, j * chans : (j + 1) * chans] = w_ref[3 * i + j]

    xt[...] = x_ref[0, :, 0].astype(F32).reshape(chans * rows, width)
    for r in range(rows):
        row = xt[pl.ds(r, chans, stride=rows), :]
        spread(row, xs, r, 1)
        xc_ref[0, 0, :, r * width : (r + 1) * width] = row.astype(BF16)
    for r, pre in enumerate(conv_rows(wf, xs, 1, rows, chans, width)):
        cols = slice(r * width, (r + 1) * width)
        s = sigmoid(pre)
        y = pre * s
        feat_ref[0, 0, :, cols] = y.astype(BF16)
        slope_ref[0, 0, :, cols] = (s + y * (1.0 - s)).astype(BF16)
    if middle:
        spot = pl.program_id(1) - meta_ref[1]

        @pl.when((spot >= 0) & (spot < middle))
        def _():
            rest[0][0, 0] = feat_ref[0, 0]


def run_forward(first, start, middle, count, x, w_spatial):
    n, chans, _, rows, width = x.shape
    vox = rows * width
    sds = jax.ShapeDtypeStruct
    shapes = [sds((count, n, chans, vox), BF16)] * 3
    specs = [pl.BlockSpec((1, 1, chans, vox), lambda k, f, meta: (k, f, 0, 0))] * 3
    if middle:
        shapes.append(sds((count, middle, chans, vox), BF16))
        specs.append(
            pl.BlockSpec(
                (1, 1, chans, vox),
                lambda k, f, meta: (k, jnp.clip(f - meta[1], 0, middle - 1), 0, 0),
            )
        )
    meta = jnp.stack([jnp.asarray(v, jnp.int32) for v in (first, start)])
    return pl.pallas_call(
        functools.partial(forward_kernel, middle),
        name="conv_forward",
        out_shape=shapes,
        grid_spec=pltpu.PrefetchScalarGridSpec(
            num_scalar_prefetch=1,
            grid=(count, n),
            in_specs=[
                pl.BlockSpec(
                    (1, chans, 1, rows, width), lambda k, f, meta: (f, 0, meta[0] + k, 0, 0)
                ),
                pl.BlockSpec((9, chans, chans), lambda k, f, meta: (0, 0, 0)),
            ],
            out_specs=specs,
            scratch_shapes=[
                pltpu.VMEM((chans * rows, width), F32),
                pltpu.VMEM((3 * chans, vox), BF16),
                pltpu.VMEM((3 * chans, 3 * chans), BF16),
            ],
        ),
        cost_estimate=pl.CostEstimate(flops=1000, bytes_accessed=1000, transcendentals=0),
    )(meta, x, w_spatial)


def backward_kernel(aliased, meta_ref, dpre_ref, wb_ref, *rest):
    dx_ref, ds, xt = rest[-3:]
    _, chans, _, rows, width = dx_ref.shape
    for r in range(rows):
        spread(dpre_ref[0, :, r * width : (r + 1) * width].astype(F32), ds, r, -1)
    for r, row in enumerate(conv_rows(wb_ref, ds, -1, rows, chans, width)):
        xt[pl.ds(r, chans, stride=rows), :] = row
    dx_ref[0, :, 0] = xt[...].astype(BF16).reshape(chans, rows, width)


def run_backward(meta, dpre, wb, n, layers, rows, into):
    chans, vox = dpre.shape[1:]
    width = vox // rows
    aliased = into is not None
    return pl.pallas_call(
        functools.partial(backward_kernel, aliased),
        name="conv_backward",
        out_shape=jax.ShapeDtypeStruct((n, chans, layers, rows, width), BF16),
        grid_spec=pltpu.PrefetchScalarGridSpec(
            num_scalar_prefetch=1,
            grid=(n,),
            in_specs=[
                pl.BlockSpec((1, chans, vox), lambda f, meta: (meta[0] + f, 0, 0)),
                pl.BlockSpec((3 * chans, 3 * chans), lambda f, meta: (0, 0)),
            ]
            + [pl.BlockSpec(memory_space=pl.ANY)] * aliased,
            out_specs=pl.BlockSpec(
                (1, chans, 1, rows, width), lambda f, meta: (f, 0, meta[1], 0, 0)
            ),
            scratch_shapes=[
                pltpu.VMEM((3 * chans, vox), BF16),
                pltpu.VMEM((chans * rows, width), F32),
            ],
        ),
        input_output_aliases={3: 0} if aliased else {},
        cost_estimate=pl.CostEstimate(flops=1000, bytes_accessed=1000, transcendentals=0),
    )(meta, dpre, wb, *([into] if aliased else []))


def temporal_kernel(
    places,
    inside,
    aliased,
    dims,
    meta_ref,
    weight_ref,
    wt_ref,
    wtb_ref,
    whc_ref,
    tgt_ref,
    init_ref,
    wb_ref,
    *rest,
):
    own, chans, vox, total, members, width = dims
    rows = vox // width
    here = own // members
    counts = len(places)
    pieces = [ref.at[k] for ref, k in zip(rest[:counts], places)]
    slope_in = [ref.at[k] for ref, k in zip(rest[counts : counts + members], places)]
    xs_in = [ref.at[k] for ref, k in zip(rest[counts + members : counts + 2 * members], places)]
    rest = rest[counts + 2 * members + aliased :]
    logit_ref, grad_ref = rest[:2]
    if inside:
        out_ref, send_ref, back = rest[2], rest[3], rest[-1]
    else:
        dpre_ref = rest[2]
    (
        feats,
        slope,
        xs,
        n0,
        inv0,
        h1,
        n1,
        inv1,
        sp0,
        dh2,
        dm1,
        dm0,
        final_ref,
        dlog,
        ds,
        xt,
        tgt,
        sems,
    ) = rest[3 + inside : 21 + inside]
    step = min(256, vox)
    lo, hi = HALO, HALO + own
    first = meta_ref[0]
    chunks = [slice(p * step, (p + 1) * step) for p in range(vox // step)]
    whole = slice(0, vox)

    early = [
        pltpu.make_async_copy(src, feats.at[pl.ds(meta_ref[1 + k], src.shape[0])], sems.at[k])
        for k, src in enumerate(pieces)
    ]
    late = []
    for k in range(members):
        spot = pl.ds(meta_ref[1 + k] - HALO, here)
        late.append(pltpu.make_async_copy(slope_in[k], slope.at[spot], sems.at[len(early) + k]))
        late.append(
            pltpu.make_async_copy(xs_in[k], xs.at[spot], sems.at[len(early) + members + k])
        )
    for copy in early + late:
        copy.start()
    for c in range(tgt_ref.shape[0]):
        tgt[:, c * tgt_ref.shape[2] : (c + 1) * tgt_ref.shape[2]] = tgt_ref[c].astype(F32)
    for copy in early:
        copy.wait()

    def frame_ok(f):
        g = first + f - HALO
        return jnp.where((g >= 0) & (g < total), 1.0, 0.0).astype(F32)

    def loop(a, b, *fns):
        def every(f, carry):
            for fn in fns:
                fn(f)
            return carry

        lax.fori_loop(a, b, every, 0)

    def stack(ref, f0, f1, f2, cols):
        return jnp.concatenate([ref[f0, :, cols], ref[f1, :, cols], ref[f2, :, cols]], axis=0)

    def rms(hid):
        return lax.rsqrt(channel_sum(hid * hid) * (1.0 / chans) + EPS)

    def norm0(f):
        for cols in chunks:
            hid = feats[f, :, cols].astype(F32)
            inv = rms(hid)
            n0[f, :, cols] = (hid * inv).astype(BF16)
            inv0[f, :, cols] = inv

    def layer0(f):
        ok = frame_ok(f)
        for cols in chunks:
            mixed = dot_nn(wt_ref[0], stack(n0, f - 1, f, f + 1, cols))
            s = sigmoid(mixed)
            y = mixed * s
            hid = feats[f, :, cols].astype(F32) + y
            inv = rms(hid) * ok
            h1[f, :, cols] = hid
            n1[f, :, cols] = (hid * inv).astype(BF16)
            inv1[f, :, cols] = inv
            sp0[f, :, cols] = s + y * (1.0 - s)

    def layer1(f):
        weight = weight_ref[f - 3]
        frame = jnp.clip(first + f - HALO, 0, total - 1)
        for cols in chunks:
            mixed = dot_nn(wt_ref[1], stack(n1, f - 2, f, f + 2, cols))
            s = sigmoid(mixed)
            y = mixed * s
            hid = h1[f, :, cols] + y
            inv = rms(hid)
            unit = hid * inv
            final = unit.astype(BF16)
            logit = channel_sum(final.astype(F32) * whc_ref[...])
            logit_ref[f - 3, :, cols] = logit
            dlogit = weight * (sigmoid(logit) - tgt[pl.ds(frame, 1), cols])
            final_ref[f, :, cols] = final
            dlog[f, :, cols] = dlogit
            dhid = (inv * dlogit) * (whc_ref[...] - unit * (logit * (1.0 / chans)))
            dh2[f, :, cols] = dhid
            dm1[f, :, cols] = (dhid * (s + y * (1.0 - s))).astype(BF16)

    def back1(f):
        ok = frame_ok(f)
        for cols in chunks:
            dnorm = dot_nn(wtb_ref[1], stack(dm1, f + 2, f, f - 2, cols))
            unit = n1[f, :, cols].astype(F32)
            mean = channel_sum(dnorm * unit) * (1.0 / chans)
            dhid = dh2[f, :, cols] + inv1[f, :, cols] * (dnorm - unit * mean)
            dh2[f, :, cols] = dhid
            dm0[f, :, cols] = (dhid * (sp0[f, :, cols] * ok)).astype(BF16)

    def back0(f):
        b = f - HALO
        for cols in chunks:
            dnorm = dot_nn(wtb_ref[0], stack(dm0, f + 1, f, f - 1, cols))
            unit = n0[f, :, cols].astype(F32)
            mean = channel_sum(dnorm * unit) * (1.0 / chans)
            dhid = dh2[f, :, cols] + inv0[f, :, cols] * (dnorm - unit * mean)
            dfeat = dhid.astype(BF16).astype(F32)
            dpre = dfeat * slope[b, :, cols].astype(F32)
            if not inside:
                dpre_ref[b, :, cols] = dpre.astype(BF16)
            dpre = dpre.astype(BF16).astype(F32)
            for r in range(step // width):
                spread(
                    dpre[:, r * width : (r + 1) * width], ds, cols.start // width + r, -1
                )
        center = xs[b]
        blank = jnp.zeros((chans, width), BF16)
        taller = jnp.concatenate([center[:, width:], blank], axis=1)
        lower = jnp.concatenate([blank, center[:, :-width]], axis=1)
        grad = dot_nt(ds[...], jnp.concatenate([lower, center, taller], axis=0))
        for j in range(3):
            grad_ref[j] += grad[j * chans : (j + 1) * chans]
        grad_ref[3] += dot_nt(dm0[f], stack(n0, f - 1, f, f + 1, whole))
        grad_ref[4] += dot_nt(dm1[f], stack(n1, f - 2, f, f + 2, whole))
        head = jnp.broadcast_to(dlog[f].astype(BF16), (chans, vox))
        grad_ref[5, :, :chans] += dot_nt(head, final_ref[f])
        if inside:
            for r, row in enumerate(conv_rows(wb_ref, ds, -1, rows, chans, width)):
                xt[pl.ds(r, chans, stride=rows), :] = row
            back[b] = xt[...].astype(BF16).reshape(chans, rows, width)

    grad_ref[...] = init_ref[...]
    loop(0, hi + HALO, norm0)
    loop(1, hi + HALO - 1, layer0)
    loop(3, hi + 3, layer1)
    loop(lo - 1, hi + 1, back1)
    for copy in late:
        copy.wait()
    loop(lo, hi, back0)
    if inside:
        layer = meta_ref[1 + counts]
        leaving = []
        for k in range(members):
            src = back.at[pl.ds(meta_ref[1 + k] - HALO, here)]
            dst = send_ref.at[k - 1] if k else out_ref.at[:, :, layer]
            leaving.append(pltpu.make_async_copy(src, dst, sems.at[k]))
        for copy in leaving:
            copy.start()
        for copy in leaving:
            copy.wait()


def run_temporal(meta, vmem_args, weights, pieces, places, slopes, xss, inside, into, dims, layers):
    own, chans, vox, total, members, width = dims
    rows, here = vox // width, own // members
    every = own + 2 * HALO
    sds = jax.ShapeDtypeStruct
    smem = pl.BlockSpec(memory_space=pltpu.SMEM)
    vmem = pl.BlockSpec(memory_space=pltpu.VMEM)
    hbm = pl.BlockSpec(memory_space=pl.ANY)
    loose = len(pieces) + 2 * members
    aliased = into is not None
    frame = lambda n, c, dt: pltpu.VMEM((n, c, vox), dt)
    shapes = [sds((own + 6, 1, vox), F32), sds((6, chans, 3 * chans), F32)]
    specs = [vmem, vmem]
    if inside:
        shapes.append(sds((here, chans, layers, rows, width), BF16))
        shapes.append(sds((members - 1, here, chans, rows, width), BF16))
        specs += [hbm, hbm]
    else:
        shapes.append(sds((own, chans, vox), BF16))
        specs.append(vmem)
    return pl.pallas_call(
        functools.partial(temporal_kernel, tuple(places), inside, aliased, dims),
        name="temporal",
        out_shape=shapes,
        in_specs=[smem, smem] + [vmem] * len(vmem_args) + [hbm] * (loose + aliased),
        out_specs=specs,
        input_output_aliases={2 + len(vmem_args) + loose: 2} if aliased else {},
        scratch_shapes=[
            frame(every, chans, BF16),
            frame(own, chans, BF16),
            frame(own, chans, BF16),
            frame(every, chans, BF16),
            frame(every, 1, F32),
            frame(every, chans, F32),
            frame(every, chans, BF16),
            frame(every, 1, F32),
            frame(every, chans, F32),
            frame(every, chans, F32),
            frame(every, chans, BF16),
            frame(every, chans, BF16),
            frame(every, chans, BF16),
            frame(every, 1, F32),
            pltpu.VMEM((3 * chans, vox), BF16),
            pltpu.VMEM((chans * rows, width), F32),
            pltpu.VMEM((total, vox), F32),
            pltpu.SemaphoreType.DMA((loose,)),
        ]
        + [pltpu.VMEM((own, chans, rows, width), BF16)] * inside,
        compiler_params=pltpu.CompilerParams(vmem_limit_bytes=VMEM_LIMIT),
        cost_estimate=pl.CostEstimate(
            flops=3000 * own * chans * vox, bytes_accessed=100 * own * chans * vox, transcendentals=0
        ),
    )(meta, weights, *vmem_args, *pieces, *slopes, *xss, *([into] if aliased else []))


def group_size(tiles, frames_here, layers):
    for g in range(1, layers + 1):
        if layers % g == 0 and tiles % g == 0 and g * frames_here >= HALO:
            return g
    return layers


def pick(parts, start):
    doubled = jnp.stack(parts + parts)
    return lax.dynamic_slice_in_dim(doubled, start, len(parts), 0)


def take(value, index, axis):
    return lax.dynamic_index_in_dim(value, index, axis, False)


def sum_over_tiles(value, tiles, others):
    if tiles & (tiles - 1):
        return lax.psum(value.astype(BF16), "tile").astype(F32), others
    k = 1
    while k < tiles:
        if 2 * k >= tiles:
            value, others = lax.optimization_barrier((value, others))
        pairs = [(a, a ^ k) for a in range(tiles)]
        value = value + lax.ppermute(value.astype(BF16), "tile", pairs).astype(F32)
        k *= 2
    return value, others


def sum_over_reps(value, axis):
    reps = lax.axis_size("rep")
    r = lax.axis_index("rep")
    n = value.shape[axis] // reps

    def share(k):
        return lax.dynamic_slice_in_dim(value, (k % reps) * n, n, axis)

    acc = share(r)
    for s in range(1, reps):
        pairs = [(a, (a + s) % reps) for a in range(reps)]
        acc = acc + lax.ppermute(share(r + s).astype(BF16), "rep", pairs).astype(F32)
    return acc


def body(inputs, w_spatial, w_temporal, w_head, targets, valid):
    _, here, chans, layers, rows, width = inputs.shape
    tiles = lax.axis_size("tile")
    total = here * tiles
    g = group_size(tiles, here, layers)
    per = layers // g
    own = g * here
    vox = rows * width
    t = lax.axis_index("tile")
    q, m = t // g, t % g
    spot = targets.shape[2]
    share = groups = tiles // g
    x = inputs[0]

    def swap(value, s):
        pairs = [(a, a // g * g + (a % g + s) % g) for a in range(tiles)]
        return lax.ppermute(value, "tile", pairs)

    def hop(value, shifts):
        pairs = [(a, a + shifts[a % g] * g) for a in range(tiles)]
        return lax.ppermute(value, "tile", [p for p in pairs if 0 <= p[1] < tiles])

    w9 = w_spatial.reshape(3, 3, chans, chans)
    wb = w9.transpose(0, 3, 1, 2).reshape(3 * chans, 3 * chans)
    wt = w_temporal.transpose(0, 2, 1, 3).reshape(2, chans, 3 * chans)
    wtb = w_temporal.transpose(0, 3, 1, 2).reshape(2, chans, 3 * chans)
    whc = w_head.astype(F32)[:, None]

    index = (m * per).astype(jnp.int32)
    mirrored = g == 2 and here <= HALO <= 2 * here
    extra = HALO - here if mirrored else 0
    start = jnp.where(m == 0, here - extra, 0)
    def arrive(value, layer):
        pieces = []
        for s in range(1, g):
            piece = lax.dynamic_slice_in_dim(value, (m + s) % g * per + layer, 1, 2)
            pieces.append(swap(piece, s))
        return pieces

    arriving = [arrive(x, 0)]
    mine = list(run_forward(index, start, extra, per, x, w_spatial))
    if per > 1:
        later, mine[1] = lax.optimization_barrier((x, mine[1]))
        arriving += [arrive(later, layer) for layer in range(1, per)]
    ahead = []
    if mirrored:
        ahead.append(hop(mine[0], (-1, 1)))
        if extra:
            ahead.append(hop(mine[3], (1, -1)))

    everyone = jnp.broadcast_to(targets, (tiles, total, spot))
    everyone = lax.all_to_all(everyone, "tile", 0, 0, tiled=True)
    tgt = lax.dynamic_slice_in_dim(everyone, m * share, share, 0)
    if share % per:
        tgt = tgt.transpose(1, 0, 2).reshape(total, per, vox).transpose(1, 0, 2)
    frame_weight = jnp.pad(valid[0].astype(F32) / total, (3, 3))
    frame_weight = lax.dynamic_slice_in_dim(frame_weight, q * own, own + 6, 0)

    dims = (own, chans, vox, total, g, width)
    grads = jnp.zeros((6, chans, 3 * chans), F32)
    ready = []
    for layer in range(per):
        done = [mine]
        start = jnp.where(m == 1, here - extra, 0)
        for piece in arriving[layer]:
            done.append(run_forward(0, start, extra, 1, piece, w_spatial))
        pieces = [d[0] for d in done]
        ranks = [layer] + [0] * (g - 1)
        places = [HALO + (m - s) % g * here for s in range(g)]
        if mirrored:
            up, down = own + HALO, HALO - here
            pieces += ahead
            pieces.append(hop(done[1][0], (1, -1)))
            if extra:
                pieces.append(hop(done[1][3], (-1, 1)))
            for k in range(2):
                ranks += [0 if k else layer] * len(ahead)
                places += [jnp.where(m == k, up, down), jnp.where(m == k, 0, up + here)][: len(ahead)]
        else:
            block = [p[k] for p, k in zip(pieces, ranks)]
            block = pick(block[::-1], g - 1 - m).reshape(own, chans, vox)
            left, d = HALO, 1
            while left > 0:
                k = min(left, own)
                pieces.append(hop(block[own - k :], (d,) * g)[None])
                places.append(left - k)
                pieces.append(hop(block[:k], (-d,) * g)[None])
                places.append(HALO + d * own)
                ranks += [0, 0]
                left -= k
                d += 1
        meta = jnp.stack([jnp.asarray(v, jnp.int32) for v in [q * own] + places + [index + layer]])
        ready.append([meta, pieces, ranks, [d[1] for d in done], [d[2] for d in done]])

    logits, out, homecoming = [], None, []
    for layer in range(per):
        meta, pieces, ranks, slopes, xcs = ready[layer]
        inside = layer < per - 1
        part = share // per if share % per == 0 else 1
        logit, grads, *result = run_temporal(
            meta,
            (wt, wtb, whc, tgt[layer * part : (layer + 1) * part], grads, wb),
            frame_weight,
            pieces,
            ranks,
            slopes,
            xcs,
            inside,
            out if inside else None,
            dims,
            layers,
        )
        logits.append(logit[3 : 3 + own, 0])
        if inside:
            out, sent = result
            following = ready[layer + 1]
            following[1], sent = lax.optimization_barrier((following[1], sent))
            for s in range(1, g):
                dx = swap(sent[s - 1][:, :, None], -s)
                homecoming.append(((m + s) % g * per + layer, dx))
    dpre = result[0]
    home = [dx for _, dx in homecoming]
    home, dpre, grads = lax.optimization_barrier((home, dpre, grads))
    for (place, _), dx in zip(homecoming, home):
        out = lax.dynamic_update_slice_in_dim(out, dx, place, 2)
    layer = per - 1
    backs = []
    for s in range(1, g):
        frames = jnp.stack([(m - s) % g * here, 0]).astype(jnp.int32)
        dx = run_backward(frames, dpre, wb, here, 1, rows, None)
        logits, dx = lax.optimization_barrier((logits, dx))
        backs.append(swap(dx, -s))
    frames = jnp.stack([m * here, index + layer]).astype(jnp.int32)
    out = run_backward(frames, dpre, wb, here, layers, rows, out)

    grads, backs = sum_over_tiles(sum_over_reps(grads, 1), tiles, backs)
    for s in range(1, g):
        out = lax.dynamic_update_slice_in_dim(out, backs[s - 1], (m + s) % g * per + layer, 2)
    part = grads.shape[1]
    gs = grads[:3].reshape(3, part, 3, chans).transpose(2, 0, 1, 3).reshape(9, part, chans)
    gt = grads[3:5].reshape(2, part, 3, chans).transpose(0, 2, 1, 3)
    gh = lax.dynamic_slice_in_dim(grads[5, 0], lax.axis_index("rep") * part, part, 0)

    logits = jnp.concatenate(logits, axis=1).astype(BF16).reshape(own, share, spot)
    logits = logits.transpose(1, 0, 2)
    logits = jnp.concatenate([logits] * g)
    logits = lax.all_to_all(logits, "tile", 0, 0, tiled=True)
    logits = take(logits.reshape(groups, g, own, spot), t // share, 1).reshape(1, total, spot)
    return logits, out[None], gs, gt, gh


def solution(mesh):
    placed = (
        P("rep", "tile", None, None, None, None),
        P(),
        P(),
        P(),
        P("rep", None, "tile"),
        P("rep", None),
    )
    return jax.shard_map(
        body,
        mesh=mesh,
        in_specs=placed,
        out_specs=(
            P("rep", None, "tile"),
            P("rep", "tile", None, None, None, None),
            P(None, "rep", None),
            P(None, None, "rep", None),
            P("rep"),
        ),
        check_vma=False,
    )
```

```python
import functools

import jax
import jax.numpy as jnp
from jax import lax
from jax.experimental import pallas as pl
from jax.experimental.pallas import tpu as pltpu
from jax.sharding import PartitionSpec as P
import numpy as np

EPS = 1e-06
HALO = 6
F32 = jnp.float32
BF16 = jnp.bfloat16
VMEM_LIMIT = 52 * 1024 * 1024


def sigmoid(u):
    return 0.5 * jnp.tanh(0.5 * u) + 0.5


def silu_parts(half):
    t = jnp.tanh(half)
    a = 1.0 + t
    y = half * a
    return y, a + y * (1.0 - t)


def dot_nn(a, b):
    return jnp.dot(a, b, preferred_element_type=F32)


def dot_nt(a, b):
    return lax.dot_general(a, b, (((1,), (1,)), ((), ())), preferred_element_type=F32)


def channel_sum(v):
    return jnp.sum(v, axis=0, keepdims=True)


def spread(row, dst, r, order):
    chans, width = row.shape
    lane = lax.broadcasted_iota(jnp.int32, (chans, width), 1)
    prev = jnp.where(lane > 0, pltpu.roll(row, 1, 1), 0.0)
    nxt = jnp.where(lane < width - 1, pltpu.roll(row, width - 1, 1), 0.0)
    parts = (prev, row, nxt) if order > 0 else (nxt, row, prev)
    for j in range(3):
        dst[j * chans : (j + 1) * chans, r * width : (r + 1) * width] = parts[j].astype(BF16)


def conv_rows(w_ref, src, sign, rows, chans, width):
    step = 2 * width
    outs = [dot_nn(w_ref[...], src[:, p * step : (p + 1) * step]) for p in range(rows // 2)]

    def piece(i, r):
        half = slice((r % 2) * width, (r % 2 + 1) * width)
        return outs[r // 2][i * chans : (i + 1) * chans, half]

    result = []
    for r in range(rows):
        acc = piece(1, r)
        for i in (-1, 1):
            if 0 <= r + sign * i < rows:
                acc = acc + piece(i + 1, r + sign * i)
        result.append(acc)
    return result


def forward_kernel(middle, base, meta_ref, x_ref, w_ref, feat_ref, slope_ref, xc_ref, *rest):
    xt, xs, wf = rest[-3:]
    frames, chans, _, rows, width = x_ref.shape

    @pl.when((pl.program_id(0) == 0) & (pl.program_id(1) == 0))
    def _():
        for i in range(3):
            for j in range(3):
                wf[i * chans : (i + 1) * chans, j * chans : (j + 1) * chans] = (
                    w_ref[3 * i + j].astype(F32) * 0.5
                ).astype(BF16)

    for n in range(frames):
        xt[n] = x_ref[n, :, 0].astype(F32).reshape(chans * rows, width)
    for n in range(frames):
        for r in range(rows):
            row = xt[n, pl.ds(r, chans, stride=rows), :]
            spread(row, xs.at[n], r, 1)
            xc_ref[0, n, :, r * width : (r + 1) * width] = row.astype(BF16)
    for n in range(frames):
        for r, half in enumerate(conv_rows(wf, xs.at[n], 1, rows, chans, width)):
            cols = slice(r * width, (r + 1) * width)
            y, slope = silu_parts(half)
            feat_ref[0, n, :, cols] = y.astype(BF16)
            slope_ref[0, n, :, cols] = slope.astype(BF16)
    if middle:

        @pl.when(pl.program_id(1) == meta_ref[base + 1])
        def _():
            rest[0][0] = feat_ref[0]


def run_forward(meta, base, middle, count, x, w_spatial):
    n, chans, _, rows, width = x.shape
    vox = rows * width
    sds = jax.ShapeDtypeStruct
    frames = middle if middle and n % middle == 0 else 2 - n % 2
    shapes = [sds((count, n, chans, vox), BF16)] * 3
    specs = [pl.BlockSpec((1, frames, chans, vox), lambda k, f, meta: (k, f, 0, 0))] * 3
    if middle:
        shapes.append(sds((count, middle, chans, vox), BF16))
        specs.append(pl.BlockSpec((1, middle, chans, vox), lambda k, f, meta: (k, 0, 0, 0)))
    return pl.pallas_call(
        functools.partial(forward_kernel, middle, base),
        name="conv_forward",
        out_shape=shapes,
        grid_spec=pltpu.PrefetchScalarGridSpec(
            num_scalar_prefetch=1,
            grid=(count, n // frames),
            in_specs=[
                pl.BlockSpec(
                    (frames, chans, 1, rows, width),
                    lambda k, f, meta: (f, 0, meta[base] + k, 0, 0),
                ),
                pl.BlockSpec((9, chans, chans), lambda k, f, meta: (0, 0, 0)),
            ],
            out_specs=specs,
            scratch_shapes=[
                pltpu.VMEM((frames, chans * rows, width), F32),
                pltpu.VMEM((frames, 3 * chans, vox), BF16),
                pltpu.VMEM((3 * chans, 3 * chans), BF16),
            ],
        ),
        cost_estimate=pl.CostEstimate(flops=1000, bytes_accessed=1000, transcendentals=0),
    )(meta, x, w_spatial)


def backward_kernel(aliased, meta_ref, dpre_ref, wb_ref, *rest):
    dx_ref, ds, xt = rest[-3:]
    frames, chans, _, rows, width = dx_ref.shape
    for n in range(frames):
        for r in range(rows):
            spread(dpre_ref[n, :, r * width : (r + 1) * width].astype(F32), ds.at[n], r, -1)
    for n in range(frames):
        for r, row in enumerate(conv_rows(wb_ref, ds.at[n], -1, rows, chans, width)):
            xt[n, pl.ds(r, chans, stride=rows), :] = row
        dx_ref[n, :, 0] = xt[n].astype(BF16).reshape(chans, rows, width)


def run_backward(meta, base, dpre, wb, n, layers, rows, into):
    chans, vox = dpre.shape[1:]
    width = vox // rows
    aliased = into is not None
    frames = 2 - n % 2
    return pl.pallas_call(
        functools.partial(backward_kernel, aliased),
        name="conv_backward",
        out_shape=jax.ShapeDtypeStruct((n, chans, layers, rows, width), BF16),
        grid_spec=pltpu.PrefetchScalarGridSpec(
            num_scalar_prefetch=1,
            grid=(n // frames,),
            in_specs=[
                pl.BlockSpec(
                    (frames, chans, vox), lambda f, meta: (meta[base] * (n // frames) + f, 0, 0)
                ),
                pl.BlockSpec((3 * chans, 3 * chans), lambda f, meta: (0, 0)),
            ]
            + [pl.BlockSpec(memory_space=pl.ANY)] * aliased,
            out_specs=pl.BlockSpec(
                (frames, chans, 1, rows, width), lambda f, meta: (f, 0, meta[base + 1], 0, 0)
            ),
            scratch_shapes=[
                pltpu.VMEM((frames, 3 * chans, vox), BF16),
                pltpu.VMEM((frames, chans * rows, width), F32),
            ],
        ),
        input_output_aliases={3: 0} if aliased else {},
        cost_estimate=pl.CostEstimate(flops=1000, bytes_accessed=1000, transcendentals=0),
    )(meta, dpre, wb, *([into] if aliased else []))


def temporal_kernel(
    places,
    inside,
    aliased,
    base,
    dims,
    meta_ref,
    weight_ref,
    wt_ref,
    wtb_ref,
    whc_ref,
    tgt_ref,
    init_ref,
    wb_ref,
    *rest,
):
    own, chans, vox, total, members, width = dims
    rows = vox // width
    here = own // members
    counts = len(places)
    pieces = [ref.at[k] for ref, k in zip(rest[:counts], places)]
    slope_in = [ref.at[k] for ref, k in zip(rest[counts : counts + members], places)]
    xs_in = [ref.at[k] for ref, k in zip(rest[counts + members : counts + 2 * members], places)]
    rest = rest[counts + 2 * members + aliased :]
    logit_ref, grad_ref = rest[:2]
    if inside:
        out_ref, send_ref, back = rest[2], rest[3], rest[-1]
    else:
        dpre_ref = rest[2]
    (
        feats,
        slope,
        xs,
        n0,
        inv0,
        h1,
        n1,
        inv1,
        sp0,
        dh2,
        dm1,
        dm0,
        final_ref,
        dlog,
        ds,
        xt,
        tgt,
        sems,
    ) = rest[3 + inside : 21 + inside]
    step = min(256, vox)
    lo, hi = HALO, HALO + own
    first = meta_ref[base]
    chunks = [slice(p * step, (p + 1) * step) for p in range(vox // step)]
    whole = slice(0, vox)

    early = [
        pltpu.make_async_copy(src, feats.at[pl.ds(meta_ref[base + 1 + k], src.shape[0])], sems.at[k])
        for k, src in enumerate(pieces)
    ]
    late = []
    for k in range(members):
        spot = pl.ds(meta_ref[base + 1 + k] - HALO, here)
        late.append(pltpu.make_async_copy(slope_in[k], slope.at[spot], sems.at[len(early) + k]))
        late.append(
            pltpu.make_async_copy(xs_in[k], xs.at[spot], sems.at[len(early) + members + k])
        )
    for copy in early + late:
        copy.start()
    for c in range(tgt_ref.shape[0]):
        tgt[:, c * tgt_ref.shape[2] : (c + 1) * tgt_ref.shape[2]] = tgt_ref[c].astype(F32)
    for copy in early:
        copy.wait()

    def frame_ok(f):
        g = first + f - HALO
        return jnp.where((g >= 0) & (g < total), 1.0, 0.0).astype(F32)

    def loop(a, b, *fns):
        def every(f, carry):
            for fn in fns:
                fn(f)
            return carry

        lax.fori_loop(a, b, every, 0)

    def stack(ref, f0, f1, f2, cols):
        return jnp.concatenate([ref[f0, :, cols], ref[f1, :, cols], ref[f2, :, cols]], axis=0)

    def rms(hid):
        return lax.rsqrt(channel_sum(hid * hid) * (1.0 / chans) + EPS)

    def norm0(f):
        for cols in chunks:
            hid = feats[f, :, cols].astype(F32)
            inv = rms(hid)
            n0[f, :, cols] = (hid * inv).astype(BF16)
            inv0[f, :, cols] = inv

    def layer0(f):
        ok = frame_ok(f)
        for cols in chunks:
            y, slope2 = silu_parts(dot_nn(wt_ref[0], stack(n0, f - 1, f, f + 1, cols)))
            hid = feats[f, :, cols].astype(F32) + y
            inv = rms(hid) * ok
            h1[f, :, cols] = hid
            n1[f, :, cols] = (hid * inv).astype(BF16)
            inv1[f, :, cols] = inv
            sp0[f, :, cols] = slope2

    def layer1(f):
        weight = weight_ref[f - 3]
        frame = jnp.clip(first + f - HALO, 0, total - 1)
        for cols in chunks:
            y, slope2 = silu_parts(dot_nn(wt_ref[1], stack(n1, f - 2, f, f + 2, cols)))
            hid = h1[f, :, cols] + y
            inv = rms(hid)
            unit = hid * inv
            logit = channel_sum(unit * whc_ref[...])
            logit_ref[f - 3, :, cols] = logit
            dlogit = weight * (sigmoid(logit) - tgt[pl.ds(frame, 1), cols])
            final_ref[f, :, cols] = unit.astype(BF16)
            dlog[f, :, cols] = dlogit
            dhid = (inv * dlogit) * (whc_ref[...] - unit * (logit * (1.0 / chans)))
            dh2[f, :, cols] = dhid
            dm1[f, :, cols] = (dhid * slope2).astype(BF16)

    def back1(f):
        for cols in chunks:
            dnorm = dot_nn(wtb_ref[1], stack(dm1, f + 2, f, f - 2, cols))
            unit = n1[f, :, cols].astype(F32)
            mean = channel_sum(dnorm * unit) * (1.0 / chans)
            dhid = dh2[f, :, cols] + inv1[f, :, cols] * (dnorm - unit * mean)
            dh2[f, :, cols] = dhid
            dm0[f, :, cols] = (dhid * sp0[f, :, cols]).astype(BF16)

    def back0(f):
        b = f - HALO
        for cols in chunks:
            dnorm = dot_nn(wtb_ref[0], stack(dm0, f + 1, f, f - 1, cols))
            unit = n0[f, :, cols].astype(F32)
            mean = channel_sum(dnorm * unit) * (1.0 / chans)
            dhid = dh2[f, :, cols] + inv0[f, :, cols] * (dnorm - unit * mean)
            dpre = dhid * slope[b, :, cols].astype(F32)
            if not inside:
                dpre_ref[b, :, cols] = dpre.astype(BF16)
            for r in range(step // width):
                spread(dpre[:, r * width : (r + 1) * width], ds, cols.start // width + r, -1)
        center = xs[b]
        blank = jnp.zeros((chans, width), BF16)
        taller = jnp.concatenate([center[:, width:], blank], axis=1)
        lower = jnp.concatenate([blank, center[:, :-width]], axis=1)
        grad = dot_nt(ds[...], jnp.concatenate([lower, center, taller], axis=0))
        for j in range(3):
            grad_ref[j] += grad[j * chans : (j + 1) * chans]
        grad_ref[3] += dot_nt(dm0[f], stack(n0, f - 1, f, f + 1, whole))
        grad_ref[4] += dot_nt(dm1[f], stack(n1, f - 2, f, f + 2, whole))
        head = jnp.broadcast_to(dlog[f].astype(BF16), (chans, vox))
        grad_ref[5, :, :chans] += dot_nt(head, final_ref[f])
        if inside:
            for r, row in enumerate(conv_rows(wb_ref, ds, -1, rows, chans, width)):
                xt[pl.ds(r, chans, stride=rows), :] = row
            back[b] = xt[...].astype(BF16).reshape(chans, rows, width)

    grad_ref[...] = init_ref[...]
    stages = [
        (back0, 5, lo, hi),
        (back1, 3, lo - 1, hi + 1),
        (layer1, 0, 3, hi + 3),
        (layer0, -3, 1, hi + HALO - 1),
        (norm0, -5, 0, hi + HALO),
    ]
    cuts = sorted({a + d for _, d, a, _ in stages} | {b + d for _, d, _, b in stages})
    for a, b in zip(cuts, cuts[1:]):
        active = [(fn, d) for fn, d, p, n in stages if p + d <= a and b <= n + d]
        if a == lo + 5:
            for copy in late:
                copy.wait()
        loop(0, b - a, *[lambda i, fn=fn, f=a - d: fn(i + f) for fn, d in active])
    if inside is False:
        grad_ref[:5] = grad_ref[:5] * 0.5
    if inside:
        layer = meta_ref[base + 1 + counts]
        leaving = []
        for k in range(members):
            src = back.at[pl.ds(meta_ref[base + 1 + k] - HALO, here)]
            dst = send_ref.at[k - 1] if k else out_ref.at[:, :, layer]
            leaving.append(pltpu.make_async_copy(src, dst, sems.at[k]))
        for copy in leaving:
            copy.start()
        for copy in leaving:
            copy.wait()


def run_temporal(meta, base, vmem_args, weights, pieces, places, slopes, xss, inside, into, dims, layers):
    own, chans, vox, total, members, width = dims
    rows, here = vox // width, own // members
    every = own + 2 * HALO
    sds = jax.ShapeDtypeStruct
    smem = pl.BlockSpec(memory_space=pltpu.SMEM)
    vmem = pl.BlockSpec(memory_space=pltpu.VMEM)
    hbm = pl.BlockSpec(memory_space=pl.ANY)
    loose = len(pieces) + 2 * members
    aliased = into is not None
    frame = lambda n, c, dt: pltpu.VMEM((n, c, vox), dt)
    shapes = [sds((own + 6, 1, vox), F32), sds((6, chans, 3 * chans), F32)]
    specs = [vmem, vmem]
    if inside:
        shapes.append(sds((here, chans, layers, rows, width), BF16))
        shapes.append(sds((members - 1, here, chans, rows, width), BF16))
        specs += [hbm, hbm]
    else:
        shapes.append(sds((own, chans, vox), BF16))
        specs.append(vmem)
    return pl.pallas_call(
        functools.partial(temporal_kernel, tuple(places), inside, aliased, base, dims),
        name="temporal",
        out_shape=shapes,
        in_specs=[smem, smem] + [vmem] * len(vmem_args) + [hbm] * (loose + aliased),
        out_specs=specs,
        input_output_aliases={2 + len(vmem_args) + loose: 2} if aliased else {},
        scratch_shapes=[
            frame(every, chans, BF16),
            frame(own, chans, BF16),
            frame(own, chans, BF16),
            frame(every, chans, BF16),
            frame(every, 1, F32),
            frame(every, chans, F32),
            frame(every, chans, BF16),
            frame(every, 1, F32),
            frame(every, chans, F32),
            frame(every, chans, F32),
            frame(every, chans, BF16),
            frame(every, chans, BF16),
            frame(every, chans, BF16),
            frame(every, 1, F32),
            pltpu.VMEM((3 * chans, vox), BF16),
            pltpu.VMEM((chans * rows, width), F32),
            pltpu.VMEM((total, vox), F32),
            pltpu.SemaphoreType.DMA((loose,)),
        ]
        + [pltpu.VMEM((own, chans, rows, width), BF16)] * inside,
        compiler_params=pltpu.CompilerParams(vmem_limit_bytes=VMEM_LIMIT),
        cost_estimate=pl.CostEstimate(
            flops=3000 * own * chans * vox, bytes_accessed=100 * own * chans * vox, transcendentals=0
        ),
    )(meta, weights, *vmem_args, *pieces, *slopes, *xss, *([into] if aliased else []))


def group_size(tiles, frames_here, layers):
    for g in range(1, layers + 1):
        if layers % g == 0 and tiles % g == 0 and g * frames_here >= HALO:
            return g
    return layers


def pick(parts, start):
    doubled = jnp.stack(parts + parts)
    return lax.dynamic_slice_in_dim(doubled, start, len(parts), 0)


def take(value, index, axis):
    return lax.dynamic_index_in_dim(value, index, axis, False)


def sum_over_tiles(value, tiles, g, others):
    if tiles & (tiles - 1):
        return lax.psum(value.astype(BF16), "tile").astype(F32), others
    steps = [2**k for k in range(tiles.bit_length() - 1)]
    steps = [k for k in steps if k >= g] + [k for k in steps if k < g]
    for k in steps:
        if k == steps[-1]:
            value, others = lax.optimization_barrier((value, others))
        pairs = [(a, a ^ k) for a in range(tiles)]
        value = value + lax.ppermute(value.astype(BF16), "tile", pairs).astype(F32)
    return value, others


def sum_over_reps(value, axis):
    reps = lax.axis_size("rep")
    r = lax.axis_index("rep")
    n = value.shape[axis] // reps

    def share(k):
        return lax.dynamic_slice_in_dim(value, (k % reps) * n, n, axis)

    acc = share(r)
    for s in range(1, reps):
        pairs = [(a, (a + s) % reps) for a in range(reps)]
        acc = acc + lax.ppermute(share(r + s).astype(BF16), "rep", pairs).astype(F32)
    return acc


def body(inputs, w_spatial, w_temporal, w_head, targets, valid):
    _, here, chans, layers, rows, width = inputs.shape
    tiles = lax.axis_size("tile")
    total = here * tiles
    g = group_size(tiles, here, layers)
    per = layers // g
    own = g * here
    vox = rows * width
    t = lax.axis_index("tile")
    q, m = t // g, t % g
    spot = targets.shape[2]
    share = groups = tiles // g
    x = inputs[0]

    def swap(value, s):
        pairs = [(a, a // g * g + (a % g + s) % g) for a in range(tiles)]
        return lax.ppermute(value, "tile", pairs)

    def hop(value, shifts):
        pairs = [(a, a + shifts[a % g] * g) for a in range(tiles)]
        return lax.ppermute(value, "tile", [p for p in pairs if 0 <= p[1] < tiles])

    halved = (w_temporal.astype(F32) * 0.5).astype(BF16)
    wt = halved.transpose(0, 2, 1, 3).reshape(2, chans, 3 * chans)
    wtb = halved.transpose(0, 3, 1, 2).reshape(2, chans, 3 * chans)
    w9 = (w_spatial.astype(F32) * 0.5).astype(BF16).reshape(3, 3, chans, chans)
    wb = w9.transpose(0, 3, 1, 2).reshape(3 * chans, 3 * chans)
    whc = w_head.astype(F32)[:, None]

    mirrored = g == 2 and here <= HALO <= 2 * here
    extra = HALO - here if mirrored else 0
    up, down = own + HALO, HALO - here
    table, slots = [], {}
    for a in range(tiles):
        aq, am = a // g, a % g
        spots = [HALO + (am - s) % g * here for s in range(g)]
        if mirrored:
            for k in range(2):
                spots.append(up if am == k else down)
                if extra:
                    spots.append(0 if am == k else up + here)
        else:
            left, d = HALO, 1
            while left > 0:
                k = min(left, own)
                spots += [left - k, HALO + d * own]
                left -= k
                d += 1
        late = (here - extra) // max(extra, 1)
        row = []

        def put(name, *values):
            slots[name] = len(row)
            row.extend(values)

        put("mine", am * per, late if am == 0 else 0)
        put("theirs", 0, late if am == 1 else 0)
        for layer in range(per):
            put(("temporal", layer), aq * own, *spots, am * per + layer)
        for s in range(g):
            put(("back", s), (am - s) % g, 0 if s else am * per + per - 1)
        table.append(row)
    meta = lax.dynamic_index_in_dim(jnp.asarray(np.array(table, np.int32)), t, 0, False)

    def arrive(value, layer):
        pieces = []
        for s in range(1, g):
            piece = lax.dynamic_slice_in_dim(value, (m + s) % g * per + layer, 1, 2)
            pieces.append(swap(piece, s))
        return pieces

    arriving = [arrive(x, 0)]
    mine = list(run_forward(meta, slots["mine"], extra, per, x, w_spatial))
    if per > 1:
        later, mine[1] = lax.optimization_barrier((x, mine[1]))
        arriving += [arrive(later, layer) for layer in range(1, per)]
    ahead = []
    if mirrored:
        ahead.append(hop(mine[0], (-1, 1)))
        if extra:
            ahead.append(hop(mine[3], (1, -1)))

    after, mine[2] = lax.optimization_barrier((targets, mine[2]))
    everyone = jnp.broadcast_to(after, (tiles, total, spot))
    everyone = lax.all_to_all(everyone, "tile", 0, 0, tiled=True)
    tgt = lax.dynamic_slice_in_dim(everyone, m * share, share, 0)
    if share % per:
        tgt = tgt.transpose(1, 0, 2).reshape(total, per, vox).transpose(1, 0, 2)
    frame_weight = jnp.pad(valid[0].astype(F32) / total, (3, 3))
    frame_weight = lax.dynamic_slice_in_dim(frame_weight, q * own, own + 6, 0)

    dims = (own, chans, vox, total, g, width)
    grads = jnp.zeros((6, chans, 3 * chans), F32)
    ready = []
    for layer in range(per):
        done = [mine]
        for piece in arriving[layer]:
            done.append(run_forward(meta, slots["theirs"], extra, 1, piece, w_spatial))
        pieces = [d[0] for d in done]
        ranks = [layer] + [0] * (g - 1)
        if mirrored:
            pieces += ahead
            pieces.append(hop(done[1][0], (1, -1)))
            if extra:
                pieces.append(hop(done[1][3], (-1, 1)))
            for k in range(2):
                ranks += [0 if k else layer] * len(ahead)
        else:
            block = [p[k] for p, k in zip(pieces, ranks)]
            block = pick(block[::-1], g - 1 - m).reshape(own, chans, vox)
            left, d = HALO, 1
            while left > 0:
                k = min(left, own)
                pieces.append(hop(block[own - k :], (d,) * g)[None])
                pieces.append(hop(block[:k], (-d,) * g)[None])
                ranks += [0, 0]
                left -= k
                d += 1
        ready.append([layer, pieces, ranks, [d[1] for d in done], [d[2] for d in done]])

    logits, out, homecoming = [], None, []
    for layer in range(per):
        _, pieces, ranks, slopes, xcs = ready[layer]
        inside = layer < per - 1
        part = share // per if share % per == 0 else 1
        logit, grads, *result = run_temporal(
            meta,
            slots["temporal", layer],
            (wt, wtb, whc, tgt[layer * part : (layer + 1) * part], grads, wb),
            frame_weight,
            pieces,
            ranks,
            slopes,
            xcs,
            inside,
            out if inside else None,
            dims,
            layers,
        )
        logits.append(logit[3 : 3 + own, 0])
        if inside:
            out, sent = result
            following = ready[layer + 1]
            following[1], sent = lax.optimization_barrier((following[1], sent))
            for s in range(1, g):
                dx = swap(sent[s - 1][:, :, None], -s)
                homecoming.append(((m + s) % g * per + layer, dx))
    dpre = result[0]
    home = [dx for _, dx in homecoming]
    home, dpre, grads = lax.optimization_barrier((home, dpre, grads))
    for (place, _), dx in zip(homecoming, home):
        out = lax.dynamic_update_slice_in_dim(out, dx, place, 2)
    layer = per - 1
    backs = []
    for s in range(1, g):
        dx = run_backward(meta, slots["back", s], dpre, wb, here, 1, rows, None)
        logits, dx = lax.optimization_barrier((logits, dx))
        backs.append(swap(dx, -s))
    out = run_backward(meta, slots["back", 0], dpre, wb, here, layers, rows, out)

    grads, backs = sum_over_tiles(sum_over_reps(grads, 1), tiles, g, backs)
    for s in range(1, g):
        out = lax.dynamic_update_slice_in_dim(out, backs[s - 1], (m + s) % g * per + layer, 2)
    part = grads.shape[1]
    gs = grads[:3].reshape(3, part, 3, chans).transpose(2, 0, 1, 3).reshape(9, part, chans)
    gt = grads[3:5].reshape(2, part, 3, chans).transpose(0, 2, 1, 3)
    gh = lax.dynamic_slice_in_dim(grads[5, 0], lax.axis_index("rep") * part, part, 0)

    logits = jnp.concatenate(logits, axis=1).astype(BF16).reshape(own, share, spot)
    logits = logits.transpose(1, 0, 2)
    logits = jnp.concatenate([logits] * g)
    logits = lax.all_to_all(logits, "tile", 0, 0, tiled=True)
    logits = take(logits.reshape(groups, g, own, spot), t // share, 1).reshape(1, total, spot)
    return logits, out[None], gs, gt, gh


def solution(mesh):
    placed = (
        P("rep", "tile", None, None, None, None),
        P(),
        P(),
        P(),
        P("rep", None, "tile"),
        P("rep", None),
    )
    return jax.shard_map(
        body,
        mesh=mesh,
        in_specs=placed,
        out_specs=(
            P("rep", None, "tile"),
            P("rep", "tile", None, None, None, None),
            P(None, "rep", None),
            P(None, None, "rep", None),
            P("rep"),
        ),
        check_vma=False,
    )
```

```python
import functools

import jax
import jax.numpy as jnp
from jax import lax
from jax.experimental import pallas as pl
from jax.experimental.pallas import tpu as pltpu
from jax.sharding import PartitionSpec as P
import numpy as np

EPS = 1e-06
HALO = 6
F32 = jnp.float32
BF16 = jnp.bfloat16
VMEM_LIMIT = 52 * 1024 * 1024


def sigmoid(u):
    return 0.5 * jnp.tanh(0.5 * u) + 0.5


def silu_parts(half):
    t = jnp.tanh(half)
    a = 1.0 + t
    y = half * a
    return y, a + y * (1.0 - t)


def dot_nn(a, b):
    return jnp.dot(a, b, preferred_element_type=F32)


def dot_nt(a, b):
    return lax.dot_general(a, b, (((1,), (1,)), ((), ())), preferred_element_type=F32)


def channel_sum(v):
    return jnp.sum(v, axis=0, keepdims=True)


def spread(row, dst, r, order):
    chans, width = row.shape
    lane = lax.broadcasted_iota(jnp.int32, (chans, width), 1)
    prev = jnp.where(lane > 0, pltpu.roll(row, 1, 1), 0.0)
    nxt = jnp.where(lane < width - 1, pltpu.roll(row, width - 1, 1), 0.0)
    parts = (prev, row, nxt) if order > 0 else (nxt, row, prev)
    for j in range(3):
        dst[j * chans : (j + 1) * chans, r * width : (r + 1) * width] = parts[j].astype(BF16)


def conv_rows(w_ref, src, sign, rows, chans, width):
    step = 2 * width
    outs = [dot_nn(w_ref[...], src[:, p * step : (p + 1) * step]) for p in range(rows // 2)]

    def piece(i, r):
        half = slice((r % 2) * width, (r % 2 + 1) * width)
        return outs[r // 2][i * chans : (i + 1) * chans, half]

    result = []
    for r in range(rows):
        acc = piece(1, r)
        for i in (-1, 1):
            if 0 <= r + sign * i < rows:
                acc = acc + piece(i + 1, r + sign * i)
        result.append(acc)
    return result


def forward_kernel(middle, base, meta_ref, x_ref, w_ref, feat_ref, slope_ref, xc_ref, *rest):
    xt, xs, wf = rest[-3:]
    frames, chans, _, rows, width = x_ref.shape

    @pl.when((pl.program_id(0) == 0) & (pl.program_id(1) == 0))
    def _():
        for i in range(3):
            for j in range(3):
                wf[i * chans : (i + 1) * chans, j * chans : (j + 1) * chans] = (
                    w_ref[3 * i + j].astype(F32) * 0.5
                ).astype(BF16)

    for n in range(frames):
        xt[n] = x_ref[n, :, 0].astype(F32).reshape(chans * rows, width)
    for n in range(frames):
        for r in range(rows):
            row = xt[n, pl.ds(r, chans, stride=rows), :]
            spread(row, xs.at[n], r, 1)
            xc_ref[0, n, :, r * width : (r + 1) * width] = row.astype(BF16)
    for n in range(frames):
        for r, half in enumerate(conv_rows(wf, xs.at[n], 1, rows, chans, width)):
            cols = slice(r * width, (r + 1) * width)
            y, slope = silu_parts(half)
            feat_ref[0, n, :, cols] = y.astype(BF16)
            slope_ref[0, n, :, cols] = slope.astype(BF16)
    if middle:

        @pl.when(pl.program_id(1) == meta_ref[base + 1])
        def _():
            rest[0][0] = feat_ref[0]


def run_forward(meta, base, middle, count, x, w_spatial):
    n, chans, _, rows, width = x.shape
    vox = rows * width
    sds = jax.ShapeDtypeStruct
    frames = middle if middle and n % middle == 0 else 2 - n % 2
    shapes = [sds((count, n, chans, vox), BF16)] * 3
    specs = [pl.BlockSpec((1, frames, chans, vox), lambda k, f, meta: (k, f, 0, 0))] * 3
    if middle:
        shapes.append(sds((count, middle, chans, vox), BF16))
        specs.append(pl.BlockSpec((1, middle, chans, vox), lambda k, f, meta: (k, 0, 0, 0)))
    return pl.pallas_call(
        functools.partial(forward_kernel, middle, base),
        name="conv_forward",
        out_shape=shapes,
        grid_spec=pltpu.PrefetchScalarGridSpec(
            num_scalar_prefetch=1,
            grid=(count, n // frames),
            in_specs=[
                pl.BlockSpec(
                    (frames, chans, 1, rows, width),
                    lambda k, f, meta: (f, 0, meta[base] + k, 0, 0),
                ),
                pl.BlockSpec((9, chans, chans), lambda k, f, meta: (0, 0, 0)),
            ],
            out_specs=specs,
            scratch_shapes=[
                pltpu.VMEM((frames, chans * rows, width), F32),
                pltpu.VMEM((frames, 3 * chans, vox), BF16),
                pltpu.VMEM((3 * chans, 3 * chans), BF16),
            ],
        ),
        cost_estimate=pl.CostEstimate(flops=1000, bytes_accessed=1000, transcendentals=0),
    )(meta, x, w_spatial)


def temporal_kernel(
    places,
    last,
    aliased,
    base,
    dims,
    meta_ref,
    weight_ref,
    wt_ref,
    wtb_ref,
    whc_ref,
    tgt_ref,
    init_ref,
    wb_ref,
    *rest,
):
    own, chans, vox, total, members, width = dims
    rows = vox // width
    here = own // members
    counts = len(places)
    pieces = [ref.at[k] for ref, k in zip(rest[:counts], places)]
    slope_in = [ref.at[k] for ref, k in zip(rest[counts : counts + members], places)]
    xs_in = [ref.at[k] for ref, k in zip(rest[counts + members : counts + 2 * members], places)]
    rest = rest[counts + 2 * members + aliased :]
    logit_ref, grad_ref = rest[:2]
    out_ref, send_ref, back = rest[2:4] + rest[-1:]
    taps = grad_ref
    if last:
        grad_ref = rest[-2]
    (
        feats,
        slope,
        xs,
        n0,
        inv0,
        h1,
        n1,
        inv1,
        sp0,
        dh2,
        dm1,
        dm0,
        final_ref,
        dlog,
        ds,
        xt,
        tgt,
        sems,
    ) = rest[4:22]
    step = min(256, vox)
    lo, hi = HALO, HALO + own
    first = meta_ref[base]
    chunks = [slice(p * step, (p + 1) * step) for p in range(vox // step)]
    whole = slice(0, vox)

    early = [
        pltpu.make_async_copy(src, feats.at[pl.ds(meta_ref[base + 1 + k], src.shape[0])], sems.at[k])
        for k, src in enumerate(pieces)
    ]
    late = []
    for k in range(members):
        spot = pl.ds(meta_ref[base + 1 + k] - HALO, here)
        late.append(pltpu.make_async_copy(slope_in[k], slope.at[spot], sems.at[len(early) + k]))
        late.append(
            pltpu.make_async_copy(xs_in[k], xs.at[spot], sems.at[len(early) + members + k])
        )
    for copy in early + late:
        copy.start()
    for c in range(tgt_ref.shape[0]):
        tgt[:, c * tgt_ref.shape[2] : (c + 1) * tgt_ref.shape[2]] = tgt_ref[c].astype(F32)
    for copy in early:
        copy.wait()

    def frame_ok(f):
        g = first + f - HALO
        return jnp.where((g >= 0) & (g < total), 1.0, 0.0).astype(F32)

    def loop(a, b, *fns):
        def every(f, carry):
            for fn in fns:
                fn(f)
            return carry

        lax.fori_loop(a, b, every, 0)

    def stack(ref, f0, f1, f2, cols):
        return jnp.concatenate([ref[f0, :, cols], ref[f1, :, cols], ref[f2, :, cols]], axis=0)

    def rms(hid):
        return lax.rsqrt(channel_sum(hid * hid) * (1.0 / chans) + EPS)

    def norm0(f):
        for cols in chunks:
            hid = feats[f, :, cols].astype(F32)
            inv = rms(hid)
            n0[f, :, cols] = (hid * inv).astype(BF16)
            inv0[f, :, cols] = inv

    def layer0(f):
        ok = frame_ok(f)
        for cols in chunks:
            y, slope2 = silu_parts(dot_nn(wt_ref[0], stack(n0, f - 1, f, f + 1, cols)))
            hid = feats[f, :, cols].astype(F32) + y
            inv = rms(hid) * ok
            h1[f, :, cols] = hid
            n1[f, :, cols] = (hid * inv).astype(BF16)
            inv1[f, :, cols] = inv
            sp0[f, :, cols] = slope2

    def layer1(f):
        weight = weight_ref[f - 3]
        frame = jnp.clip(first + f - HALO, 0, total - 1)
        for cols in chunks:
            y, slope2 = silu_parts(dot_nn(wt_ref[1], stack(n1, f - 2, f, f + 2, cols)))
            hid = h1[f, :, cols] + y
            inv = rms(hid)
            unit = hid * inv
            logit = channel_sum(unit * whc_ref[...])
            logit_ref[f - 3, :, cols] = logit
            dlogit = weight * (sigmoid(logit) - tgt[pl.ds(frame, 1), cols])
            final_ref[f, :, cols] = unit.astype(BF16)
            dlog[f, :, cols] = dlogit
            dhid = (inv * dlogit) * (whc_ref[...] - unit * (logit * (1.0 / chans)))
            dh2[f, :, cols] = dhid
            dm1[f, :, cols] = (dhid * slope2).astype(BF16)

    def back1(f):
        for cols in chunks:
            dnorm = dot_nn(wtb_ref[1], stack(dm1, f + 2, f, f - 2, cols))
            unit = n1[f, :, cols].astype(F32)
            mean = channel_sum(dnorm * unit) * (1.0 / chans)
            dhid = dh2[f, :, cols] + inv1[f, :, cols] * (dnorm - unit * mean)
            dh2[f, :, cols] = dhid
            dm0[f, :, cols] = (dhid * sp0[f, :, cols]).astype(BF16)

    def back0(f):
        b = f - HALO
        for cols in chunks:
            dnorm = dot_nn(wtb_ref[0], stack(dm0, f + 1, f, f - 1, cols))
            unit = n0[f, :, cols].astype(F32)
            mean = channel_sum(dnorm * unit) * (1.0 / chans)
            dhid = dh2[f, :, cols] + inv0[f, :, cols] * (dnorm - unit * mean)
            dpre = dhid * slope[b, :, cols].astype(F32)
            for r in range(step // width):
                spread(dpre[:, r * width : (r + 1) * width], ds, cols.start // width + r, -1)
        center = xs[b]
        blank = jnp.zeros((chans, width), BF16)
        taller = jnp.concatenate([center[:, width:], blank], axis=1)
        lower = jnp.concatenate([blank, center[:, :-width]], axis=1)
        grad = dot_nt(ds[...], jnp.concatenate([lower, center, taller], axis=0))
        for j in range(3):
            grad_ref[j] += grad[j * chans : (j + 1) * chans]
        grad_ref[3] += dot_nt(dm0[f], stack(n0, f - 1, f, f + 1, whole))
        grad_ref[4] += dot_nt(dm1[f], stack(n1, f - 2, f, f + 2, whole))
        head = jnp.broadcast_to(dlog[f].astype(BF16), (chans, vox))
        grad_ref[5, :, :chans] += dot_nt(head, final_ref[f])
        for r, row in enumerate(conv_rows(wb_ref, ds, -1, rows, chans, width)):
            xt[pl.ds(r, chans, stride=rows), :] = row
        back[b] = xt[...].astype(BF16).reshape(chans, rows, width)

    grad_ref[...] = init_ref[...]
    stages = [
        (back0, 5, lo, hi),
        (back1, 3, lo - 1, hi + 1),
        (layer1, 0, 3, hi + 3),
        (layer0, -3, 1, hi + HALO - 1),
        (norm0, -5, 0, hi + HALO),
    ]
    cuts = sorted({a + d for _, d, a, _ in stages} | {b + d for _, d, _, b in stages})
    for a, b in zip(cuts, cuts[1:]):
        active = [(fn, d) for fn, d, p, n in stages if p + d <= a and b <= n + d]
        if a == lo + 5:
            for copy in late:
                copy.wait()
        loop(0, b - a, *[lambda i, fn=fn, f=a - d: fn(i + f) for fn, d in active])
    layer = meta_ref[base + 1 + counts]
    leaving = []
    for k in range(members):
        src = back.at[pl.ds(meta_ref[base + 1 + k] - HALO, here)]
        dst = send_ref.at[k - 1] if k else out_ref.at[:, :, layer]
        leaving.append(pltpu.make_async_copy(src, dst, sems.at[k]))
    for copy in leaving:
        copy.start()
    if last:
        for k in range(3):
            cols = slice(k * chans, (k + 1) * chans)
            for j in range(3):
                taps[3 * k + j] = grad_ref[j, :, cols] * 0.5
            for l in range(2):
                taps[9 + 3 * l + k] = grad_ref[3 + l, :, cols] * 0.5
        taps[15] = grad_ref[5, :, :chans]
    for copy in leaving:
        copy.wait()


def run_temporal(meta, base, vmem_args, weights, pieces, places, slopes, xss, last, into, dims, layers):
    own, chans, vox, total, members, width = dims
    rows, here = vox // width, own // members
    every = own + 2 * HALO
    sds = jax.ShapeDtypeStruct
    smem = pl.BlockSpec(memory_space=pltpu.SMEM)
    vmem = pl.BlockSpec(memory_space=pltpu.VMEM)
    hbm = pl.BlockSpec(memory_space=pl.ANY)
    loose = len(pieces) + 2 * members
    aliased = into is not None
    frame = lambda n, c, dt: pltpu.VMEM((n, c, vox), dt)
    sums = (6, chans, 3 * chans)
    shapes = [
        sds((own + 6, 1, vox), F32),
        sds((16, chans, chans) if last else sums, F32),
        sds((here, chans, layers, rows, width), BF16),
        sds((members - 1, here, chans, rows, width), BF16),
    ]
    specs = [vmem, vmem, hbm, hbm]
    return pl.pallas_call(
        functools.partial(temporal_kernel, tuple(places), last, aliased, base, dims),
        name="temporal",
        out_shape=shapes,
        in_specs=[smem, smem] + [vmem] * len(vmem_args) + [hbm] * (loose + aliased),
        out_specs=specs,
        input_output_aliases={2 + len(vmem_args) + loose: 2} if aliased else {},
        scratch_shapes=[
            frame(every, chans, BF16),
            frame(own, chans, BF16),
            frame(own, chans, BF16),
            frame(every, chans, BF16),
            frame(every, 1, F32),
            frame(every, chans, F32),
            frame(every, chans, BF16),
            frame(every, 1, F32),
            frame(every, chans, F32),
            frame(every, chans, F32),
            frame(every, chans, BF16),
            frame(every, chans, BF16),
            frame(every, chans, BF16),
            frame(every, 1, F32),
            pltpu.VMEM((3 * chans, vox), BF16),
            pltpu.VMEM((chans * rows, width), F32),
            pltpu.VMEM((total, vox), F32),
            pltpu.SemaphoreType.DMA((loose,)),
        ]
        + [pltpu.VMEM(sums, F32)] * last
        + [pltpu.VMEM((own, chans, rows, width), BF16)],
        compiler_params=pltpu.CompilerParams(vmem_limit_bytes=VMEM_LIMIT),
        cost_estimate=pl.CostEstimate(
            flops=3000 * own * chans * vox, bytes_accessed=100 * own * chans * vox, transcendentals=0
        ),
    )(meta, weights, *vmem_args, *pieces, *slopes, *xss, *([into] if aliased else []))


def group_size(tiles, frames_here, layers):
    for g in range(1, layers + 1):
        if layers % g == 0 and tiles % g == 0 and g * frames_here >= HALO:
            return g
    return layers


def pick(parts, start):
    doubled = jnp.stack(parts + parts)
    return lax.dynamic_slice_in_dim(doubled, start, len(parts), 0)


def take(value, index, axis):
    return lax.dynamic_index_in_dim(value, index, axis, False)


def sum_over_tiles(value, tiles, g, others):
    if tiles & (tiles - 1):
        return lax.psum(value.astype(BF16), "tile").astype(F32), others
    steps = [2**k for k in range(tiles.bit_length() - 1)]
    steps = [k for k in steps if k >= g] + [k for k in steps if k < g]
    for k in steps:
        if k == steps[-1]:
            value, others = lax.optimization_barrier((value, others))
        pairs = [(a, a ^ k) for a in range(tiles)]
        value = value + lax.ppermute(value.astype(BF16), "tile", pairs).astype(F32)
    return value, others


def sum_over_reps(value, axis):
    reps = lax.axis_size("rep")
    r = lax.axis_index("rep")
    n = value.shape[axis] // reps

    def share(k):
        return lax.dynamic_slice_in_dim(value, (k % reps) * n, n, axis)

    acc = share(r)
    for s in range(1, reps):
        pairs = [(a, (a + s) % reps) for a in range(reps)]
        acc = acc + lax.ppermute(share(r + s).astype(BF16), "rep", pairs).astype(F32)
    return acc


def body(inputs, w_spatial, w_temporal, w_head, targets, valid):
    _, here, chans, layers, rows, width = inputs.shape
    tiles = lax.axis_size("tile")
    total = here * tiles
    g = group_size(tiles, here, layers)
    per = layers // g
    own = g * here
    vox = rows * width
    t = lax.axis_index("tile")
    q, m = t // g, t % g
    spot = targets.shape[2]
    share = groups = tiles // g
    x = inputs[0]

    def swap(value, s):
        pairs = [(a, a // g * g + (a % g + s) % g) for a in range(tiles)]
        return lax.ppermute(value, "tile", pairs)

    def hop(value, shifts):
        pairs = [(a, a + shifts[a % g] * g) for a in range(tiles)]
        return lax.ppermute(value, "tile", [p for p in pairs if 0 <= p[1] < tiles])

    halved = (w_temporal.astype(F32) * 0.5).astype(BF16)
    wt = halved.transpose(0, 2, 1, 3).reshape(2, chans, 3 * chans)
    wtb = halved.transpose(0, 3, 1, 2).reshape(2, chans, 3 * chans)
    w9 = (w_spatial.astype(F32) * 0.5).astype(BF16).reshape(3, 3, chans, chans)
    wb = w9.transpose(0, 3, 1, 2).reshape(3 * chans, 3 * chans)
    whc = w_head.astype(F32)[:, None]

    mirrored = g == 2 and here <= HALO <= 2 * here
    extra = HALO - here if mirrored else 0
    up, down = own + HALO, HALO - here
    table, slots = [], {}
    for a in range(tiles):
        aq, am = a // g, a % g
        spots = [HALO + (am - s) % g * here for s in range(g)]
        if mirrored:
            for k in range(2):
                spots.append(up if am == k else down)
                if extra:
                    spots.append(0 if am == k else up + here)
        else:
            left, d = HALO, 1
            while left > 0:
                k = min(left, own)
                spots += [left - k, HALO + d * own]
                left -= k
                d += 1
        late = (here - extra) // max(extra, 1)
        row = []

        def put(name, *values):
            slots[name] = len(row)
            row.extend(values)

        put("mine", am * per, late if am == 0 else 0)
        put("theirs", 0, late if am == 1 else 0)
        for layer in range(per):
            put(("temporal", layer), aq * own, *spots, am * per + layer)
        table.append(row)
    meta = lax.dynamic_index_in_dim(jnp.asarray(np.array(table, np.int32)), t, 0, False)

    def arrive(value, layer):
        pieces = []
        for s in range(1, g):
            piece = lax.dynamic_slice_in_dim(value, (m + s) % g * per + layer, 1, 2)
            pieces.append(swap(piece, s))
        return pieces

    arriving = [arrive(x, 0)]
    mine = list(run_forward(meta, slots["mine"], extra, per, x, w_spatial))
    ahead = []
    if mirrored:
        ahead.append(hop(mine[0], (-1, 1)))
        if extra:
            ahead.append(hop(mine[3], (1, -1)))

    dims = (own, chans, vox, total, g, width)
    grads = jnp.zeros((6, chans, 3 * chans), F32)
    ready, asked = [], targets
    for layer in range(per):
        done = [mine]
        for piece in arriving[layer]:
            done.append(list(run_forward(meta, slots["theirs"], extra, 1, piece, w_spatial)))
        if layer == 0 and g > 1:
            later, asked, done[1][2] = lax.optimization_barrier((x, targets, done[1][2]))
            arriving += [arrive(later, k) for k in range(1, per)]
        pieces = [d[0] for d in done]
        ranks = [layer] + [0] * (g - 1)
        if mirrored:
            pieces += ahead
            pieces.append(hop(done[1][0], (1, -1)))
            if extra:
                pieces.append(hop(done[1][3], (-1, 1)))
            for k in range(2):
                ranks += [0 if k else layer] * len(ahead)
        else:
            block = [p[k] for p, k in zip(pieces, ranks)]
            block = pick(block[::-1], g - 1 - m).reshape(own, chans, vox)
            left, d = HALO, 1
            while left > 0:
                k = min(left, own)
                pieces.append(hop(block[own - k :], (d,) * g)[None])
                pieces.append(hop(block[:k], (-d,) * g)[None])
                ranks += [0, 0]
                left -= k
                d += 1
        ready.append([layer, pieces, ranks, [d[1] for d in done], [d[2] for d in done]])

    everyone = jnp.broadcast_to(asked, (tiles, total, spot))
    everyone = lax.all_to_all(everyone, "tile", 0, 0, tiled=True)
    tgt = lax.dynamic_slice_in_dim(everyone, m * share, share, 0)
    if share % per:
        tgt = tgt.transpose(1, 0, 2).reshape(total, per, vox).transpose(1, 0, 2)
    frame_weight = jnp.pad(valid[0].astype(F32) / total, (3, 3))
    frame_weight = lax.dynamic_slice_in_dim(frame_weight, q * own, own + 6, 0)


    logits, out, homecoming = [], None, []
    for layer in range(per):
        _, pieces, ranks, slopes, xcs = ready[layer]
        part = share // per if share % per == 0 else 1
        logit, grads, out, sent = run_temporal(
            meta,
            slots["temporal", layer],
            (wt, wtb, whc, tgt[layer * part : (layer + 1) * part], grads, wb),
            frame_weight,
            pieces,
            ranks,
            slopes,
            xcs,
            layer == per - 1,
            out,
            dims,
            layers,
        )
        logits.append(logit[3 : 3 + own, 0])
        if layer < per - 1:
            following = ready[layer + 1]
            following[1], sent = lax.optimization_barrier((following[1], sent))
        homecoming.append([swap(sent[s - 1][:, :, None], -s) for s in range(1, g)])
    homecoming[:-1], grads = lax.optimization_barrier((homecoming[:-1], grads))

    logits = jnp.concatenate(logits, axis=1).astype(BF16).reshape(own, share, spot)
    logits = logits.transpose(1, 0, 2)
    logits = jnp.concatenate([logits] * g)
    logits = lax.all_to_all(logits, "tile", 0, 0, tiled=True)
    grads, homecoming = sum_over_tiles(sum_over_reps(grads, 1), tiles, g, homecoming)
    for layer in range(per):
        for s in range(1, g):
            place = (m + s) % g * per + layer
            out = lax.dynamic_update_slice_in_dim(out, homecoming[layer][s - 1], place, 2)
    logits, grads = lax.optimization_barrier((logits, grads))
    logits = take(logits.reshape(groups, g, own, spot), t // share, 1).reshape(1, total, spot)
    part = grads.shape[1]
    gs = grads[:9]
    gt = grads[9:15].reshape(2, 3, part, chans)
    gh = lax.dynamic_slice_in_dim(grads[15, 0], lax.axis_index("rep") * part, part, 0)

    return logits, out[None], gs, gt, gh


def solution(mesh):
    placed = (
        P("rep", "tile", None, None, None, None),
        P(),
        P(),
        P(),
        P("rep", None, "tile"),
        P("rep", None),
    )
    return jax.shard_map(
        body,
        mesh=mesh,
        in_specs=placed,
        out_specs=(
            P("rep", None, "tile"),
            P("rep", "tile", None, None, None, None),
            P(None, "rep", None),
            P(None, None, "rep", None),
            P("rep"),
        ),
        check_vma=False,
    )
```

```python
import functools

import jax
import jax.numpy as jnp
from jax import lax
from jax.experimental import pallas as pl
from jax.experimental.pallas import tpu as pltpu
from jax.sharding import PartitionSpec as P
import numpy as np

EPS = 1e-06
HALO = 6
F32 = jnp.float32
BF16 = jnp.bfloat16
VMEM_LIMIT = 52 * 1024 * 1024


def sigmoid(u):
    return 0.5 * jnp.tanh(0.5 * u) + 0.5


def silu_parts(half):
    t = jnp.tanh(half)
    a = 1.0 + t
    y = half * a
    return y, a + y * (1.0 - t)


def dot_nn(a, b):
    return jnp.dot(a, b, preferred_element_type=F32)


def dot_nt(a, b):
    return lax.dot_general(a, b, (((1,), (1,)), ((), ())), preferred_element_type=F32)


def channel_sum(v):
    return jnp.sum(v, axis=0, keepdims=True)


def spread(row, dst, r, order):
    chans, width = row.shape
    lane = lax.broadcasted_iota(jnp.int32, (chans, width), 1)
    prev = jnp.where(lane > 0, pltpu.roll(row, 1, 1), 0.0)
    nxt = jnp.where(lane < width - 1, pltpu.roll(row, width - 1, 1), 0.0)
    parts = (prev, row, nxt) if order > 0 else (nxt, row, prev)
    for j in range(3):
        dst[j * chans : (j + 1) * chans, r * width : (r + 1) * width] = parts[j].astype(BF16)


def conv_rows(w_ref, src, sign, rows, chans, width):
    step = 2 * width
    outs = [dot_nn(w_ref[...], src[:, p * step : (p + 1) * step]) for p in range(rows // 2)]

    def piece(i, r):
        half = slice((r % 2) * width, (r % 2 + 1) * width)
        return outs[r // 2][i * chans : (i + 1) * chans, half]

    result = []
    for r in range(rows):
        acc = piece(1, r)
        for i in (-1, 1):
            if 0 <= r + sign * i < rows:
                acc = acc + piece(i + 1, r + sign * i)
        result.append(acc)
    return result


def forward_kernel(middle, base, meta_ref, x_ref, w_ref, feat_ref, slope_ref, xc_ref, *rest):
    xt, xs, wf = rest[-3:]
    frames, chans, _, rows, width = x_ref.shape

    @pl.when((pl.program_id(0) == 0) & (pl.program_id(1) == 0))
    def _():
        for i in range(3):
            for j in range(3):
                wf[i * chans : (i + 1) * chans, j * chans : (j + 1) * chans] = (
                    w_ref[3 * i + j].astype(F32) * 0.5
                ).astype(BF16)

    for n in range(frames):
        xt[n] = x_ref[n, :, 0].astype(F32).reshape(chans * rows, width)
    for n in range(frames):
        for r in range(rows):
            row = xt[n, pl.ds(r, chans, stride=rows), :]
            spread(row, xs.at[n], r, 1)
            xc_ref[0, n, :, r * width : (r + 1) * width] = row.astype(BF16)
    for n in range(frames):
        for r, half in enumerate(conv_rows(wf, xs.at[n], 1, rows, chans, width)):
            cols = slice(r * width, (r + 1) * width)
            y, slope = silu_parts(half)
            feat_ref[0, n, :, cols] = y.astype(BF16)
            slope_ref[0, n, :, cols] = slope.astype(BF16)
    if middle:

        @pl.when(pl.program_id(1) == meta_ref[base + 1])
        def _():
            rest[0][0] = feat_ref[0]


def run_forward(meta, base, middle, count, x, w_spatial):
    n, chans, _, rows, width = x.shape
    vox = rows * width
    sds = jax.ShapeDtypeStruct
    frames = middle if middle and n % middle == 0 else 2 - n % 2
    shapes = [sds((count, n, chans, vox), BF16)] * 3
    specs = [pl.BlockSpec((1, frames, chans, vox), lambda k, f, meta: (k, f, 0, 0))] * 3
    if middle:
        shapes.append(sds((count, middle, chans, vox), BF16))
        specs.append(pl.BlockSpec((1, middle, chans, vox), lambda k, f, meta: (k, 0, 0, 0)))
    return pl.pallas_call(
        functools.partial(forward_kernel, middle, base),
        name="conv_forward",
        out_shape=shapes,
        grid_spec=pltpu.PrefetchScalarGridSpec(
            num_scalar_prefetch=1,
            grid=(count, n // frames),
            in_specs=[
                pl.BlockSpec(
                    (frames, chans, 1, rows, width),
                    lambda k, f, meta: (f, 0, meta[base] + k, 0, 0),
                ),
                pl.BlockSpec((9, chans, chans), lambda k, f, meta: (0, 0, 0)),
            ],
            out_specs=specs,
            scratch_shapes=[
                pltpu.VMEM((frames, chans * rows, width), F32),
                pltpu.VMEM((frames, 3 * chans, vox), BF16),
                pltpu.VMEM((3 * chans, 3 * chans), BF16),
            ],
        ),
        cost_estimate=pl.CostEstimate(flops=1000, bytes_accessed=1000, transcendentals=0),
    )(meta, x, w_spatial)


def temporal_kernel(
    places,
    last,
    aliased,
    base,
    dims,
    meta_ref,
    weight_ref,
    wt_ref,
    wtb_ref,
    whc_ref,
    tgt_ref,
    init_ref,
    wb_ref,
    *rest,
):
    own, chans, vox, total, members, width = dims
    rows = vox // width
    here = own // members
    counts = len(places)
    pieces = [ref.at[k] for ref, k in zip(rest[:counts], places)]
    slope_in = [ref.at[k] for ref, k in zip(rest[counts : counts + members], places)]
    xs_in = [ref.at[k] for ref, k in zip(rest[counts + members : counts + 2 * members], places)]
    rest = rest[counts + 2 * members + aliased :]
    logit_ref, grad_ref = rest[:2]
    out_ref, send_ref, back = rest[2:4] + rest[-1:]
    taps = grad_ref
    if last:
        grad_ref = rest[-2]
    (
        feats,
        slope,
        xs,
        n0,
        inv0,
        h1,
        n1,
        inv1,
        sp0,
        dh2,
        dm1,
        dm0,
        final_ref,
        dlog,
        ds,
        xt,
        tgt,
        sems,
    ) = rest[4:22]
    step = min(256, vox)
    lo, hi = HALO, HALO + own
    first = meta_ref[base]
    chunks = [slice(p * step, (p + 1) * step) for p in range(vox // step)]
    whole = slice(0, vox)

    early = [
        pltpu.make_async_copy(src, feats.at[pl.ds(meta_ref[base + 1 + k], src.shape[0])], sems.at[k])
        for k, src in enumerate(pieces)
    ]
    late = []
    for k in range(members):
        spot = pl.ds(meta_ref[base + 1 + k] - HALO, here)
        late.append(pltpu.make_async_copy(slope_in[k], slope.at[spot], sems.at[len(early) + k]))
        late.append(
            pltpu.make_async_copy(xs_in[k], xs.at[spot], sems.at[len(early) + members + k])
        )
    for copy in early + late:
        copy.start()
    for c in range(tgt_ref.shape[0]):
        tgt[:, c * tgt_ref.shape[2] : (c + 1) * tgt_ref.shape[2]] = tgt_ref[c].astype(F32)
    for copy in early:
        copy.wait()

    def frame_ok(f):
        g = first + f - HALO
        return jnp.where((g >= 0) & (g < total), 1.0, 0.0).astype(F32)

    def loop(a, b, *fns):
        def every(f, carry):
            for fn in fns:
                fn(f)
            return carry

        lax.fori_loop(a, b, every, 0)

    def stack(ref, f0, f1, f2, cols):
        return jnp.concatenate([ref[f0, :, cols], ref[f1, :, cols], ref[f2, :, cols]], axis=0)

    def rms(hid):
        return lax.rsqrt(channel_sum(hid * hid) * (1.0 / chans) + EPS)

    def norm0(f):
        for cols in chunks:
            hid = feats[f, :, cols].astype(F32)
            inv = rms(hid)
            n0[f, :, cols] = (hid * inv).astype(BF16)
            inv0[f, :, cols] = inv

    def layer0(f):
        ok = frame_ok(f)
        for cols in chunks:
            y, slope2 = silu_parts(dot_nn(wt_ref[0], stack(n0, f - 1, f, f + 1, cols)))
            hid = feats[f, :, cols].astype(F32) + y
            inv = rms(hid) * ok
            h1[f, :, cols] = hid
            n1[f, :, cols] = (hid * inv).astype(BF16)
            inv1[f, :, cols] = inv
            sp0[f, :, cols] = slope2

    def layer1(f):
        weight = weight_ref[f - 3]
        frame = jnp.clip(first + f - HALO, 0, total - 1)
        for cols in chunks:
            y, slope2 = silu_parts(dot_nn(wt_ref[1], stack(n1, f - 2, f, f + 2, cols)))
            hid = h1[f, :, cols] + y
            inv = rms(hid)
            unit = hid * inv
            logit = channel_sum(unit * whc_ref[...])
            logit_ref[f - 3, :, cols] = logit
            dlogit = weight * (sigmoid(logit) - tgt[pl.ds(frame, 1), cols])
            final_ref[f, :, cols] = unit.astype(BF16)
            dlog[f, :, cols] = dlogit
            dhid = (inv * dlogit) * (whc_ref[...] - unit * (logit * (1.0 / chans)))
            dh2[f, :, cols] = dhid
            dm1[f, :, cols] = (dhid * slope2).astype(BF16)

    def back1(f):
        for cols in chunks:
            dnorm = dot_nn(wtb_ref[1], stack(dm1, f + 2, f, f - 2, cols))
            unit = n1[f, :, cols].astype(F32)
            mean = channel_sum(dnorm * unit) * (1.0 / chans)
            dhid = dh2[f, :, cols] + inv1[f, :, cols] * (dnorm - unit * mean)
            dh2[f, :, cols] = dhid
            dm0[f, :, cols] = (dhid * sp0[f, :, cols]).astype(BF16)

    def back0(f):
        b = f - HALO
        for cols in chunks:
            dnorm = dot_nn(wtb_ref[0], stack(dm0, f + 1, f, f - 1, cols))
            unit = n0[f, :, cols].astype(F32)
            mean = channel_sum(dnorm * unit) * (1.0 / chans)
            dhid = dh2[f, :, cols] + inv0[f, :, cols] * (dnorm - unit * mean)
            dpre = dhid * slope[b, :, cols].astype(F32)
            for r in range(step // width):
                spread(dpre[:, r * width : (r + 1) * width], ds, cols.start // width + r, -1)
        center = xs[b]
        blank = jnp.zeros((chans, width), BF16)
        taller = jnp.concatenate([center[:, width:], blank], axis=1)
        lower = jnp.concatenate([blank, center[:, :-width]], axis=1)
        grad = dot_nt(ds[...], jnp.concatenate([lower, center, taller], axis=0))
        for j in range(3):
            grad_ref[j] += grad[j * chans : (j + 1) * chans]
        grad_ref[3] += dot_nt(dm0[f], stack(n0, f - 1, f, f + 1, whole))
        grad_ref[4] += dot_nt(dm1[f], stack(n1, f - 2, f, f + 2, whole))
        head = jnp.broadcast_to(dlog[f].astype(BF16), (chans, vox))
        grad_ref[5, :, :chans] += dot_nt(head, final_ref[f])
        for r, row in enumerate(conv_rows(wb_ref, ds, -1, rows, chans, width)):
            xt[pl.ds(r, chans, stride=rows), :] = row
        back[b] = xt[...].astype(BF16).reshape(chans, rows, width)

    grad_ref[...] = init_ref[...]
    stages = [
        (back0, 5, lo, hi),
        (back1, 3, lo - 1, hi + 1),
        (layer1, 0, 3, hi + 3),
        (layer0, -3, 1, hi + HALO - 1),
        (norm0, -5, 0, hi + HALO),
    ]
    cuts = sorted({a + d for _, d, a, _ in stages} | {b + d for _, d, _, b in stages})
    for a, b in zip(cuts, cuts[1:]):
        active = [(fn, d) for fn, d, p, n in stages if p + d <= a and b <= n + d]
        if a == lo + 5:
            for copy in late:
                copy.wait()
        loop(0, b - a, *[lambda i, fn=fn, f=a - d: fn(i + f) for fn, d in active])
    layer = meta_ref[base + 1 + counts]
    leaving = []
    for k in range(members):
        src = back.at[pl.ds(meta_ref[base + 1 + k] - HALO, here)]
        dst = send_ref.at[k - 1] if k else out_ref.at[:, :, layer]
        leaving.append(pltpu.make_async_copy(src, dst, sems.at[k]))
    for copy in leaving:
        copy.start()
    if last:
        for k in range(3):
            cols = slice(k * chans, (k + 1) * chans)
            for j in range(3):
                taps[3 * k + j] = grad_ref[j, :, cols] * 0.5
            for l in range(2):
                taps[9 + 3 * l + k] = grad_ref[3 + l, :, cols] * 0.5
        taps[15] = grad_ref[5, :, :chans]
    for copy in leaving:
        copy.wait()


def run_temporal(meta, base, vmem_args, weights, pieces, places, slopes, xss, last, into, dims, layers):
    own, chans, vox, total, members, width = dims
    rows, here = vox // width, own // members
    every = own + 2 * HALO
    sds = jax.ShapeDtypeStruct
    smem = pl.BlockSpec(memory_space=pltpu.SMEM)
    vmem = pl.BlockSpec(memory_space=pltpu.VMEM)
    hbm = pl.BlockSpec(memory_space=pl.ANY)
    loose = len(pieces) + 2 * members
    aliased = into is not None
    frame = lambda n, c, dt: pltpu.VMEM((n, c, vox), dt)
    sums = (6, chans, 3 * chans)
    shapes = [
        sds((own + 6, 1, vox), F32),
        sds((16, chans, chans) if last else sums, F32),
        sds((here, chans, layers, rows, width), BF16),
        sds((members - 1, here, chans, rows, width), BF16),
    ]
    specs = [vmem, vmem, hbm, hbm]
    return pl.pallas_call(
        functools.partial(temporal_kernel, tuple(places), last, aliased, base, dims),
        name="temporal",
        out_shape=shapes,
        in_specs=[smem, smem] + [vmem] * len(vmem_args) + [hbm] * (loose + aliased),
        out_specs=specs,
        input_output_aliases={2 + len(vmem_args) + loose: 2} if aliased else {},
        scratch_shapes=[
            frame(every, chans, BF16),
            frame(own, chans, BF16),
            frame(own, chans, BF16),
            frame(every, chans, BF16),
            frame(every, 1, F32),
            frame(every, chans, F32),
            frame(every, chans, BF16),
            frame(every, 1, F32),
            frame(every, chans, F32),
            frame(every, chans, F32),
            frame(every, chans, BF16),
            frame(every, chans, BF16),
            frame(every, chans, BF16),
            frame(every, 1, F32),
            pltpu.VMEM((3 * chans, vox), BF16),
            pltpu.VMEM((chans * rows, width), F32),
            pltpu.VMEM((total, vox), F32),
            pltpu.SemaphoreType.DMA((loose,)),
        ]
        + [pltpu.VMEM(sums, F32)] * last
        + [pltpu.VMEM((own, chans, rows, width), BF16)],
        compiler_params=pltpu.CompilerParams(vmem_limit_bytes=VMEM_LIMIT),
        cost_estimate=pl.CostEstimate(
            flops=3000 * own * chans * vox, bytes_accessed=100 * own * chans * vox, transcendentals=0
        ),
    )(meta, weights, *vmem_args, *pieces, *slopes, *xss, *([into] if aliased else []))


def group_size(tiles, frames_here, layers):
    for g in range(1, layers + 1):
        if layers % g == 0 and tiles % g == 0 and g * frames_here >= HALO:
            return g
    return layers


def pick(parts, start):
    doubled = jnp.stack(parts + parts)
    return lax.dynamic_slice_in_dim(doubled, start, len(parts), 0)


def take(value, index, axis):
    return lax.dynamic_index_in_dim(value, index, axis, False)


def sum_over_tiles(value, tiles, g, others):
    if tiles & (tiles - 1):
        return lax.psum(value.astype(BF16), "tile").astype(F32), others
    steps = [2**k for k in range(tiles.bit_length() - 1)]
    outer, inner = [k for k in steps if k >= g], [k for k in steps if k < g]
    rounds = [part[i : i + 2] for part in (outer, inner) for i in range(0, len(part), 2)]
    for number, bits in enumerate(rounds):
        if number == len(rounds) - 1:
            value, others = lax.optimization_barrier((value, others))
        masks = bits + [sum(bits)] * (len(bits) - 1)
        sent = value.astype(BF16)
        for k in masks:
            pairs = [(a, a ^ k) for a in range(tiles)]
            value = value + lax.ppermute(sent, "tile", pairs).astype(F32)
    return value, others


def sum_over_reps(value, axis):
    reps = lax.axis_size("rep")
    r = lax.axis_index("rep")
    n = value.shape[axis] // reps

    def share(k):
        return lax.dynamic_slice_in_dim(value, (k % reps) * n, n, axis)

    acc = share(r)
    for s in range(1, reps):
        pairs = [(a, (a + s) % reps) for a in range(reps)]
        acc = acc + lax.ppermute(share(r + s).astype(BF16), "rep", pairs).astype(F32)
    return acc


def body(inputs, w_spatial, w_temporal, w_head, targets, valid):
    _, here, chans, layers, rows, width = inputs.shape
    tiles = lax.axis_size("tile")
    total = here * tiles
    g = group_size(tiles, here, layers)
    per = layers // g
    own = g * here
    vox = rows * width
    t = lax.axis_index("tile")
    q, m = t // g, t % g
    spot = targets.shape[2]
    share = groups = tiles // g
    x = inputs[0]

    def swap(value, s):
        pairs = [(a, a // g * g + (a % g + s) % g) for a in range(tiles)]
        return lax.ppermute(value, "tile", pairs)

    def hop(value, shifts):
        pairs = [(a, a + shifts[a % g] * g) for a in range(tiles)]
        return lax.ppermute(value, "tile", [p for p in pairs if 0 <= p[1] < tiles])

    halved = (w_temporal.astype(F32) * 0.5).astype(BF16)
    wt = halved.transpose(0, 2, 1, 3).reshape(2, chans, 3 * chans)
    wtb = halved.transpose(0, 3, 1, 2).reshape(2, chans, 3 * chans)
    w9 = (w_spatial.astype(F32) * 0.5).astype(BF16).reshape(3, 3, chans, chans)
    wb = w9.transpose(0, 3, 1, 2).reshape(3 * chans, 3 * chans)
    whc = w_head.astype(F32)[:, None]

    mirrored = g == 2 and here <= HALO <= 2 * here
    extra = HALO - here if mirrored else 0
    up, down = own + HALO, HALO - here
    table, slots = [], {}
    for a in range(tiles):
        aq, am = a // g, a % g
        spots = [HALO + (am - s) % g * here for s in range(g)]
        if mirrored:
            for k in range(2):
                spots.append(up if am == k else down)
                if extra:
                    spots.append(0 if am == k else up + here)
        else:
            left, d = HALO, 1
            while left > 0:
                k = min(left, own)
                spots += [left - k, HALO + d * own]
                left -= k
                d += 1
        late = (here - extra) // max(extra, 1)
        row = []

        def put(name, *values):
            slots[name] = len(row)
            row.extend(values)

        put("mine", am * per, late if am == 0 else 0)
        put("theirs", 0, late if am == 1 else 0)
        for layer in range(per):
            put(("temporal", layer), aq * own, *spots, am * per + layer)
        table.append(row)
    meta = lax.dynamic_index_in_dim(jnp.asarray(np.array(table, np.int32)), t, 0, False)

    def arrive(value, layer):
        pieces = []
        for s in range(1, g):
            piece = lax.dynamic_slice_in_dim(value, (m + s) % g * per + layer, 1, 2)
            pieces.append(swap(piece, s))
        return pieces

    arriving = [arrive(x, 0)]
    mine = list(run_forward(meta, slots["mine"], extra, per, x, w_spatial))
    if per > 1:
        later, mine[1] = lax.optimization_barrier((x, mine[1]))
        arriving += [arrive(later, layer) for layer in range(1, per)]
    ahead = []
    if mirrored:
        ahead.append(hop(mine[0], (-1, 1)))
        if extra:
            ahead.append(hop(mine[3], (1, -1)))

    dims = (own, chans, vox, total, g, width)
    grads = jnp.zeros((6, chans, 3 * chans), F32)
    ready, asked = [], targets
    for layer in range(per):
        done = [mine]
        for piece in arriving[layer]:
            done.append(list(run_forward(meta, slots["theirs"], extra, 1, piece, w_spatial)))
        if layer == 0 and g > 1:
            asked, done[1][2] = lax.optimization_barrier((targets, done[1][2]))
        pieces = [d[0] for d in done]
        ranks = [layer] + [0] * (g - 1)
        if mirrored:
            pieces += ahead
            pieces.append(hop(done[1][0], (1, -1)))
            if extra:
                pieces.append(hop(done[1][3], (-1, 1)))
            for k in range(2):
                ranks += [0 if k else layer] * len(ahead)
        else:
            block = [p[k] for p, k in zip(pieces, ranks)]
            block = pick(block[::-1], g - 1 - m).reshape(own, chans, vox)
            left, d = HALO, 1
            while left > 0:
                k = min(left, own)
                pieces.append(hop(block[own - k :], (d,) * g)[None])
                pieces.append(hop(block[:k], (-d,) * g)[None])
                ranks += [0, 0]
                left -= k
                d += 1
        ready.append([layer, pieces, ranks, [d[1] for d in done], [d[2] for d in done]])

    everyone = jnp.broadcast_to(asked, (tiles, total, spot))
    everyone = lax.all_to_all(everyone, "tile", 0, 0, tiled=True)
    tgt = lax.dynamic_slice_in_dim(everyone, m * share, share, 0)
    if share % per:
        tgt = tgt.transpose(1, 0, 2).reshape(total, per, vox).transpose(1, 0, 2)
    frame_weight = jnp.pad(valid[0].astype(F32) / total, (3, 3))
    frame_weight = lax.dynamic_slice_in_dim(frame_weight, q * own, own + 6, 0)


    logits, out, homecoming = [], None, []
    for layer in range(per):
        _, pieces, ranks, slopes, xcs = ready[layer]
        part = share // per if share % per == 0 else 1
        logit, grads, out, sent = run_temporal(
            meta,
            slots["temporal", layer],
            (wt, wtb, whc, tgt[layer * part : (layer + 1) * part], grads, wb),
            frame_weight,
            pieces,
            ranks,
            slopes,
            xcs,
            layer == per - 1,
            out,
            dims,
            layers,
        )
        logits.append(logit[3 : 3 + own, 0])
        if layer < per - 1:
            following = ready[layer + 1]
            following[1], sent = lax.optimization_barrier((following[1], sent))
        homecoming.append([swap(sent[s - 1][:, :, None], -s) for s in range(1, g)])
    homecoming[:-1], grads = lax.optimization_barrier((homecoming[:-1], grads))

    logits = jnp.concatenate(logits, axis=1).astype(BF16).reshape(own, share, spot)
    logits = logits.transpose(1, 0, 2)
    logits = jnp.concatenate([logits] * g)
    logits = lax.all_to_all(logits, "tile", 0, 0, tiled=True)
    grads, homecoming = sum_over_tiles(sum_over_reps(grads, 1), tiles, g, homecoming)
    for layer in range(per):
        for s in range(1, g):
            place = (m + s) % g * per + layer
            out = lax.dynamic_update_slice_in_dim(out, homecoming[layer][s - 1], place, 2)
    logits, grads = lax.optimization_barrier((logits, grads))
    logits = take(logits.reshape(groups, g, own, spot), t // share, 1).reshape(1, total, spot)
    part = grads.shape[1]
    gs = grads[:9]
    gt = grads[9:15].reshape(2, 3, part, chans)
    gh = lax.dynamic_slice_in_dim(grads[15, 0], lax.axis_index("rep") * part, part, 0)

    return logits, out[None], gs, gt, gh


def solution(mesh):
    placed = (
        P("rep", "tile", None, None, None, None),
        P(),
        P(),
        P(),
        P("rep", None, "tile"),
        P("rep", None),
    )
    return jax.shard_map(
        body,
        mesh=mesh,
        in_specs=placed,
        out_specs=(
            P("rep", None, "tile"),
            P("rep", "tile", None, None, None, None),
            P(None, "rep", None),
            P(None, None, "rep", None),
            P("rep"),
        ),
        check_vma=False,
    )
```

```python
import functools

import jax
import jax.numpy as jnp
from jax import lax
from jax.experimental import pallas as pl
from jax.experimental.pallas import tpu as pltpu
from jax.sharding import PartitionSpec as P
import numpy as np

EPS = 1e-06
HALO = 6
F32 = jnp.float32
BF16 = jnp.bfloat16
VMEM_LIMIT = 52 * 1024 * 1024


def sigmoid(u):
    return 0.5 * jnp.tanh(0.5 * u) + 0.5


def silu_parts(half):
    t = jnp.tanh(half)
    a = 1.0 + t
    y = half * a
    return y, a + y * (1.0 - t)


def dot_nn(a, b):
    return jnp.dot(a, b, preferred_element_type=F32)


def dot_nt(a, b):
    return lax.dot_general(a, b, (((1,), (1,)), ((), ())), preferred_element_type=F32)


def channel_sum(v):
    return jnp.sum(v, axis=0, keepdims=True)


def spread(row, dst, r, order):
    chans, width = row.shape
    lane = lax.broadcasted_iota(jnp.int32, (chans, width), 1)
    prev = jnp.where(lane > 0, pltpu.roll(row, 1, 1), 0.0)
    nxt = jnp.where(lane < width - 1, pltpu.roll(row, width - 1, 1), 0.0)
    parts = (prev, row, nxt) if order > 0 else (nxt, row, prev)
    for j in range(3):
        dst[j * chans : (j + 1) * chans, r * width : (r + 1) * width] = parts[j].astype(BF16)


def conv_rows(w_ref, src, sign, rows, chans, width):
    step = 2 * width
    outs = [dot_nn(w_ref[...], src[:, p * step : (p + 1) * step]) for p in range(rows // 2)]

    def piece(i, r):
        half = slice((r % 2) * width, (r % 2 + 1) * width)
        return outs[r // 2][i * chans : (i + 1) * chans, half]

    result = []
    for r in range(rows):
        acc = piece(1, r)
        for i in (-1, 1):
            if 0 <= r + sign * i < rows:
                acc = acc + piece(i + 1, r + sign * i)
        result.append(acc)
    return result


def forward_kernel(middle, base, meta_ref, x_ref, w_ref, feat_ref, slope_ref, xc_ref, *rest):
    xt, xs, wf = rest[-3:]
    frames, chans, _, rows, width = x_ref.shape

    @pl.when((pl.program_id(0) == 0) & (pl.program_id(1) == 0))
    def _():
        for i in range(3):
            for j in range(3):
                wf[i * chans : (i + 1) * chans, j * chans : (j + 1) * chans] = (
                    w_ref[3 * i + j].astype(F32) * 0.5
                ).astype(BF16)

    for n in range(frames):
        xt[n] = x_ref[n, :, 0].astype(F32).reshape(chans * rows, width)
    for n in range(frames):
        for r in range(rows):
            row = xt[n, pl.ds(r, chans, stride=rows), :]
            spread(row, xs.at[n], r, 1)
            xc_ref[0, n, :, r * width : (r + 1) * width] = row.astype(BF16)
    for n in range(frames):
        for r, half in enumerate(conv_rows(wf, xs.at[n], 1, rows, chans, width)):
            cols = slice(r * width, (r + 1) * width)
            y, slope = silu_parts(half)
            feat_ref[0, n, :, cols] = y.astype(BF16)
            slope_ref[0, n, :, cols] = slope.astype(BF16)
    if middle:

        @pl.when(pl.program_id(1) == meta_ref[base + 1])
        def _():
            rest[0][0] = feat_ref[0]


def run_forward(meta, base, middle, count, x, w_spatial):
    n, chans, _, rows, width = x.shape
    vox = rows * width
    sds = jax.ShapeDtypeStruct
    frames = middle if middle and n % middle == 0 else 2 - n % 2
    shapes = [sds((count, n, chans, vox), BF16)] * 3
    specs = [pl.BlockSpec((1, frames, chans, vox), lambda k, f, meta: (k, f, 0, 0))] * 3
    if middle:
        shapes.append(sds((count, middle, chans, vox), BF16))
        specs.append(pl.BlockSpec((1, middle, chans, vox), lambda k, f, meta: (k, 0, 0, 0)))
    return pl.pallas_call(
        functools.partial(forward_kernel, middle, base),
        name="conv_forward",
        out_shape=shapes,
        grid_spec=pltpu.PrefetchScalarGridSpec(
            num_scalar_prefetch=1,
            grid=(count, n // frames),
            in_specs=[
                pl.BlockSpec(
                    (frames, chans, 1, rows, width),
                    lambda k, f, meta: (f, 0, meta[base] + k, 0, 0),
                ),
                pl.BlockSpec((9, chans, chans), lambda k, f, meta: (0, 0, 0)),
            ],
            out_specs=specs,
            scratch_shapes=[
                pltpu.VMEM((frames, chans * rows, width), F32),
                pltpu.VMEM((frames, 3 * chans, vox), BF16),
                pltpu.VMEM((3 * chans, 3 * chans), BF16),
            ],
        ),
        cost_estimate=pl.CostEstimate(flops=1000, bytes_accessed=1000, transcendentals=0),
    )(meta, x, w_spatial)


def window_kernel(own, g, tgt_ref, win_ref, pad):
    total, spot = tgt_ref.shape[1:]
    pad[0:8] = jnp.zeros((8, spot), F32)
    pad[8 : 8 + total] = tgt_ref[0].astype(F32)
    pad[8 + total :] = jnp.zeros((8, spot), F32)
    for a in range(win_ref.shape[0]):
        first = a // g * own + 4
        win_ref[a] = pad[first : first + own + 8].astype(BF16)


def run_windows(targets, tiles, own, g):
    _, total, spot = targets.shape
    vmem = pl.BlockSpec(memory_space=pltpu.VMEM)
    return pl.pallas_call(
        functools.partial(window_kernel, own, g),
        name="windows",
        out_shape=jax.ShapeDtypeStruct((tiles, own + 8, spot), BF16),
        in_specs=[vmem],
        out_specs=vmem,
        scratch_shapes=[pltpu.VMEM((total + 16, spot), F32)],
        cost_estimate=pl.CostEstimate(flops=1000, bytes_accessed=1000, transcendentals=0),
    )(targets)


def finish_kernel(arrived, g, value_ref, *rest):
    logit_ref, out_ref, gs_ref, gt_ref, gh_ref = rest[arrived:]
    part, chans = value_ref.shape[1:]
    groups = out_ref.shape[0]
    member = lax.axis_index("tile") // groups
    for q in range(groups):
        out_ref[q] = logit_ref[q * g + member]

    def total(k):
        acc = value_ref[k]
        for ref in rest[:arrived]:
            acc = acc + ref[k].astype(F32)
        return acc

    for k in range(9):
        gs_ref[k] = total(k)
    for k in range(6):
        gt_ref[k // 3, k % 3] = total(9 + k)
    shape = (chans, part)
    mine = lax.broadcasted_iota(jnp.int32, shape, 1) + lax.axis_index("rep") * part
    chosen = jnp.where(lax.broadcasted_iota(jnp.int32, shape, 0) == mine, 1.0, 0.0)
    picked = jnp.dot(total(15), chosen, precision=lax.Precision.HIGHEST, preferred_element_type=F32)
    gh_ref[...] = picked[0:1]


def run_finish(value, arrived, logits, groups, g):
    _, part, chans = value.shape
    _, own, spot = logits.shape
    sds = jax.ShapeDtypeStruct
    vmem = pl.BlockSpec(memory_space=pltpu.VMEM)
    return pl.pallas_call(
        functools.partial(finish_kernel, len(arrived), g),
        name="finish",
        out_shape=(
            sds((groups, own, spot), BF16),
            sds((9, part, chans), F32),
            sds((2, 3, part, chans), F32),
            sds((1, part), F32),
        ),
        in_specs=[vmem] * (2 + len(arrived)),
        out_specs=[vmem] * 4,
        cost_estimate=pl.CostEstimate(flops=1000, bytes_accessed=1000, transcendentals=0),
    )(value, *arrived, logits)


def temporal_kernel(
    places,
    last,
    aliased,
    base,
    dims,
    meta_ref,
    weight_ref,
    wt_ref,
    wtb_ref,
    whc_ref,
    tgt_ref,
    init_ref,
    wb_ref,
    *rest,
):
    own, chans, vox, total, members, width = dims
    rows = vox // width
    here = own // members
    counts = len(places)
    pieces = [ref.at[k] for ref, k in zip(rest[:counts], places)]
    slope_in = [ref.at[k] for ref, k in zip(rest[counts : counts + members], places)]
    xs_in = [ref.at[k] for ref, k in zip(rest[counts + members : counts + 2 * members], places)]
    rest = rest[counts + 2 * members + aliased :]
    logit_ref, grad_ref = rest[:2]
    out_ref, send_ref, back = rest[2:4] + rest[-1:]
    taps = grad_ref
    if last:
        grad_ref = rest[-2]
    (
        feats,
        slope,
        xs,
        n0,
        inv0,
        h1,
        n1,
        inv1,
        sp0,
        dh2,
        dm1,
        dm0,
        final_ref,
        dlog,
        ds,
        xt,
        tgt,
        sems,
    ) = rest[4:22]
    step = min(256, vox)
    lo, hi = HALO, HALO + own
    first = meta_ref[base]
    chunks = [slice(p * step, (p + 1) * step) for p in range(vox // step)]
    whole = slice(0, vox)

    early = [
        pltpu.make_async_copy(src, feats.at[pl.ds(meta_ref[base + 1 + k], src.shape[0])], sems.at[k])
        for k, src in enumerate(pieces)
    ]
    late = []
    for k in range(members):
        spot = pl.ds(meta_ref[base + 1 + k] - HALO, here)
        late.append(pltpu.make_async_copy(slope_in[k], slope.at[spot], sems.at[len(early) + k]))
        late.append(
            pltpu.make_async_copy(xs_in[k], xs.at[spot], sems.at[len(early) + members + k])
        )
    for copy in early + late:
        copy.start()
    for c in range(tgt_ref.shape[0]):
        tgt[:, c * tgt_ref.shape[2] : (c + 1) * tgt_ref.shape[2]] = tgt_ref[c].astype(F32)
    for copy in early:
        copy.wait()

    def frame_ok(f):
        g = first + f - HALO
        return jnp.where((g >= 0) & (g < total), 1.0, 0.0).astype(F32)

    def loop(a, b, *fns):
        def every(f, carry):
            for fn in fns:
                fn(f)
            return carry

        lax.fori_loop(a, b, every, 0)

    def stack(ref, f0, f1, f2, cols):
        return jnp.concatenate([ref[f0, :, cols], ref[f1, :, cols], ref[f2, :, cols]], axis=0)

    def rms(hid):
        return lax.rsqrt(channel_sum(hid * hid) * (1.0 / chans) + EPS)

    def norm0(f):
        for cols in chunks:
            hid = feats[f, :, cols].astype(F32)
            inv = rms(hid)
            n0[f, :, cols] = (hid * inv).astype(BF16)
            inv0[f, :, cols] = inv

    def layer0(f):
        ok = frame_ok(f)
        for cols in chunks:
            y, slope2 = silu_parts(dot_nn(wt_ref[0], stack(n0, f - 1, f, f + 1, cols)))
            hid = feats[f, :, cols].astype(F32) + y
            inv = rms(hid) * ok
            h1[f, :, cols] = hid
            n1[f, :, cols] = (hid * inv).astype(BF16)
            inv1[f, :, cols] = inv
            sp0[f, :, cols] = slope2

    def layer1(f):
        weight = weight_ref[f - 3]
        for cols in chunks:
            y, slope2 = silu_parts(dot_nn(wt_ref[1], stack(n1, f - 2, f, f + 2, cols)))
            hid = h1[f, :, cols] + y
            inv = rms(hid)
            unit = hid * inv
            logit = channel_sum(unit * whc_ref[...])
            logit_ref[f - 3, :, cols] = logit
            dlogit = weight * (sigmoid(logit) - tgt[pl.ds(f - 2, 1), cols])
            final_ref[f, :, cols] = unit.astype(BF16)
            dlog[f, :, cols] = dlogit
            dhid = (inv * dlogit) * (whc_ref[...] - unit * (logit * (1.0 / chans)))
            dh2[f, :, cols] = dhid
            dm1[f, :, cols] = (dhid * slope2).astype(BF16)

    def back1(f):
        for cols in chunks:
            dnorm = dot_nn(wtb_ref[1], stack(dm1, f + 2, f, f - 2, cols))
            unit = n1[f, :, cols].astype(F32)
            mean = channel_sum(dnorm * unit) * (1.0 / chans)
            dhid = dh2[f, :, cols] + inv1[f, :, cols] * (dnorm - unit * mean)
            dh2[f, :, cols] = dhid
            dm0[f, :, cols] = (dhid * sp0[f, :, cols]).astype(BF16)

    def back0(f):
        b = f - HALO
        for cols in chunks:
            dnorm = dot_nn(wtb_ref[0], stack(dm0, f + 1, f, f - 1, cols))
            unit = n0[f, :, cols].astype(F32)
            mean = channel_sum(dnorm * unit) * (1.0 / chans)
            dhid = dh2[f, :, cols] + inv0[f, :, cols] * (dnorm - unit * mean)
            dpre = dhid * slope[b, :, cols].astype(F32)
            for r in range(step // width):
                spread(dpre[:, r * width : (r + 1) * width], ds, cols.start // width + r, -1)
        center = xs[b]
        blank = jnp.zeros((chans, width), BF16)
        taller = jnp.concatenate([center[:, width:], blank], axis=1)
        lower = jnp.concatenate([blank, center[:, :-width]], axis=1)
        grad = dot_nt(ds[...], jnp.concatenate([lower, center, taller], axis=0))
        for j in range(3):
            grad_ref[j] += grad[j * chans : (j + 1) * chans]
        grad_ref[3] += dot_nt(dm0[f], stack(n0, f - 1, f, f + 1, whole))
        grad_ref[4] += dot_nt(dm1[f], stack(n1, f - 2, f, f + 2, whole))
        head = jnp.broadcast_to(dlog[f].astype(BF16), (chans, vox))
        grad_ref[5, :, :chans] += dot_nt(head, final_ref[f])
        for r, row in enumerate(conv_rows(wb_ref, ds, -1, rows, chans, width)):
            xt[pl.ds(r, chans, stride=rows), :] = row
        back[b] = xt[...].astype(BF16).reshape(chans, rows, width)

    grad_ref[...] = init_ref[...]
    stages = [
        (back0, 5, lo, hi),
        (back1, 3, lo - 1, hi + 1),
        (layer1, 0, 3, hi + 3),
        (layer0, -3, 1, hi + HALO - 1),
        (norm0, -5, 0, hi + HALO),
    ]
    cuts = sorted({a + d for _, d, a, _ in stages} | {b + d for _, d, _, b in stages})
    for a, b in zip(cuts, cuts[1:]):
        active = [(fn, d) for fn, d, p, n in stages if p + d <= a and b <= n + d]
        if a == lo + 5:
            for copy in late:
                copy.wait()
        loop(0, b - a, *[lambda i, fn=fn, f=a - d: fn(i + f) for fn, d in active])
    layer = meta_ref[base + 1 + counts]
    leaving = []
    for k in range(members):
        src = back.at[pl.ds(meta_ref[base + 1 + k] - HALO, here)]
        dst = send_ref.at[k - 1] if k else out_ref.at[:, :, layer]
        leaving.append(pltpu.make_async_copy(src, dst, sems.at[k]))
    for copy in leaving:
        copy.start()
    if last:
        for k in range(3):
            cols = slice(k * chans, (k + 1) * chans)
            for j in range(3):
                taps[3 * k + j] = grad_ref[j, :, cols] * 0.5
            for l in range(2):
                taps[9 + 3 * l + k] = grad_ref[3 + l, :, cols] * 0.5
        taps[15] = grad_ref[5, :, :chans]
    for copy in leaving:
        copy.wait()


def run_temporal(meta, base, vmem_args, weights, pieces, places, slopes, xss, last, into, dims, layers):
    own, chans, vox, total, members, width = dims
    rows, here = vox // width, own // members
    every = own + 2 * HALO
    sds = jax.ShapeDtypeStruct
    smem = pl.BlockSpec(memory_space=pltpu.SMEM)
    vmem = pl.BlockSpec(memory_space=pltpu.VMEM)
    hbm = pl.BlockSpec(memory_space=pl.ANY)
    loose = len(pieces) + 2 * members
    aliased = into is not None
    frame = lambda n, c, dt: pltpu.VMEM((n, c, vox), dt)
    sums = (6, chans, 3 * chans)
    shapes = [
        sds((own + 6, 1, vox), F32),
        sds((16, chans, chans) if last else sums, F32),
        sds((here, chans, layers, rows, width), BF16),
        sds((members - 1, here, chans, rows, width), BF16),
    ]
    specs = [vmem, vmem, hbm, hbm]
    return pl.pallas_call(
        functools.partial(temporal_kernel, tuple(places), last, aliased, base, dims),
        name="temporal",
        out_shape=shapes,
        in_specs=[smem, smem] + [vmem] * len(vmem_args) + [hbm] * (loose + aliased),
        out_specs=specs,
        input_output_aliases={2 + len(vmem_args) + loose: 2} if aliased else {},
        scratch_shapes=[
            frame(every, chans, BF16),
            frame(own, chans, BF16),
            frame(own, chans, BF16),
            frame(every, chans, BF16),
            frame(every, 1, F32),
            frame(every, chans, F32),
            frame(every, chans, BF16),
            frame(every, 1, F32),
            frame(every, chans, F32),
            frame(every, chans, F32),
            frame(every, chans, BF16),
            frame(every, chans, BF16),
            frame(every, chans, BF16),
            frame(every, 1, F32),
            pltpu.VMEM((3 * chans, vox), BF16),
            pltpu.VMEM((chans * rows, width), F32),
            pltpu.VMEM((own + 8, vox), F32),
            pltpu.SemaphoreType.DMA((loose,)),
        ]
        + [pltpu.VMEM(sums, F32)] * last
        + [pltpu.VMEM((own, chans, rows, width), BF16)],
        compiler_params=pltpu.CompilerParams(vmem_limit_bytes=VMEM_LIMIT),
        cost_estimate=pl.CostEstimate(
            flops=3000 * own * chans * vox, bytes_accessed=100 * own * chans * vox, transcendentals=0
        ),
    )(meta, weights, *vmem_args, *pieces, *slopes, *xss, *([into] if aliased else []))


def group_size(tiles, frames_here, layers):
    for g in range(1, layers + 1):
        if layers % g == 0 and tiles % g == 0 and g * frames_here >= HALO:
            return g
    return layers


def pick(parts, start):
    doubled = jnp.stack(parts + parts)
    return lax.dynamic_slice_in_dim(doubled, start, len(parts), 0)


def take(value, index, axis):
    return lax.dynamic_index_in_dim(value, index, axis, False)


def sum_over_tiles(value, tiles, g, others):
    if tiles & (tiles - 1):
        return lax.psum(value.astype(BF16), "tile").astype(F32), [], others
    steps = [2**k for k in range(tiles.bit_length() - 1)]
    outer, inner = [k for k in steps if k >= g], [k for k in steps if k < g]
    rounds = [part[i : i + 2] for part in (outer, inner) for i in range(0, len(part), 2)]
    for number, bits in enumerate(rounds):
        if number == len(rounds) - 1:
            value, others = lax.optimization_barrier((value, others))
        masks = bits + [sum(bits)] * (len(bits) - 1)
        sent, arrived = value.astype(BF16), []
        for k in masks:
            pairs = [(a, a ^ k) for a in range(tiles)]
            arrived.append(lax.ppermute(sent, "tile", pairs))
        if number < len(rounds) - 1:
            for piece in arrived:
                value = value + piece.astype(F32)
    return value, arrived, others


def sum_over_reps(value, axis):
    reps = lax.axis_size("rep")
    r = lax.axis_index("rep")
    n = value.shape[axis] // reps

    def share(k):
        return lax.dynamic_slice_in_dim(value, (k % reps) * n, n, axis)

    acc = share(r)
    for s in range(1, reps):
        pairs = [(a, (a + s) % reps) for a in range(reps)]
        acc = acc + lax.ppermute(share(r + s).astype(BF16), "rep", pairs).astype(F32)
    return acc


def body(inputs, w_spatial, w_temporal, w_head, targets, valid):
    _, here, chans, layers, rows, width = inputs.shape
    tiles = lax.axis_size("tile")
    total = here * tiles
    g = group_size(tiles, here, layers)
    per = layers // g
    own = g * here
    vox = rows * width
    t = lax.axis_index("tile")
    q, m = t // g, t % g
    spot = targets.shape[2]
    share = groups = tiles // g
    x = inputs[0]

    def swap(value, s):
        pairs = [(a, a // g * g + (a % g + s) % g) for a in range(tiles)]
        return lax.ppermute(value, "tile", pairs)

    def hop(value, shifts):
        pairs = [(a, a + shifts[a % g] * g) for a in range(tiles)]
        return lax.ppermute(value, "tile", [p for p in pairs if 0 <= p[1] < tiles])

    halved = (w_temporal.astype(F32) * 0.5).astype(BF16)
    wt = halved.transpose(0, 2, 1, 3).reshape(2, chans, 3 * chans)
    wtb = halved.transpose(0, 3, 1, 2).reshape(2, chans, 3 * chans)
    w9 = (w_spatial.astype(F32) * 0.5).astype(BF16).reshape(3, 3, chans, chans)
    wb = w9.transpose(0, 3, 1, 2).reshape(3 * chans, 3 * chans)
    whc = w_head.astype(F32)[:, None]

    mirrored = g == 2 and here <= HALO <= 2 * here
    extra = HALO - here if mirrored else 0
    up, down = own + HALO, HALO - here
    table, slots = [], {}
    for a in range(tiles):
        aq, am = a // g, a % g
        spots = [HALO + (am - s) % g * here for s in range(g)]
        if mirrored:
            for k in range(2):
                spots.append(up if am == k else down)
                if extra:
                    spots.append(0 if am == k else up + here)
        else:
            left, d = HALO, 1
            while left > 0:
                k = min(left, own)
                spots += [left - k, HALO + d * own]
                left -= k
                d += 1
        late = (here - extra) // max(extra, 1)
        row = []

        def put(name, *values):
            slots[name] = len(row)
            row.extend(values)

        put("mine", am * per, late if am == 0 else 0)
        for layer in range(per):
            put(("theirs", layer), layer, late if am == 1 else 0)
            put(("temporal", layer), aq * own, *spots, am * per + layer)
        table.append(row)
    meta = lax.dynamic_index_in_dim(jnp.asarray(np.array(table, np.int32)), t, 0, False)

    arriving = [
        swap(lax.dynamic_slice_in_dim(x, (m + s) % g * per, per, 2), s) for s in range(1, g)
    ]
    mine = list(run_forward(meta, slots["mine"], extra, per, x, w_spatial))
    ahead = []
    if mirrored:
        ahead.append(hop(mine[0], (-1, 1)))
        if extra:
            ahead.append(hop(mine[3], (1, -1)))

    dims = (own, chans, vox, total, g, width)
    grads = jnp.zeros((6, chans, 3 * chans), F32)
    asked, mine[2] = lax.optimization_barrier((targets, mine[2]))
    ready = []
    for layer in range(per):
        done = [mine]
        if layer:
            ahead, arriving = lax.optimization_barrier((ahead, arriving))
        for piece in arriving:
            done.append(list(run_forward(meta, slots["theirs", layer], extra, 1, piece, w_spatial)))
        pieces = [d[0] for d in done]
        ranks = [layer] + [0] * (g - 1)
        if mirrored:
            pieces += ahead
            pieces.append(hop(done[1][0], (1, -1)))
            if extra:
                pieces.append(hop(done[1][3], (-1, 1)))
            for k in range(2):
                ranks += [0 if k else layer] * len(ahead)
        else:
            block = [p[k] for p, k in zip(pieces, ranks)]
            block = pick(block[::-1], g - 1 - m).reshape(own, chans, vox)
            left, d = HALO, 1
            while left > 0:
                k = min(left, own)
                pieces.append(hop(block[own - k :], (d,) * g)[None])
                pieces.append(hop(block[:k], (-d,) * g)[None])
                ranks += [0, 0]
                left -= k
                d += 1
        ready.append([layer, pieces, ranks, [d[1] for d in done], [d[2] for d in done]])

    windows = run_windows(asked, tiles, own, g)
    windows = lax.all_to_all(windows, "tile", 0, 0, tiled=True)
    tgt = lax.dynamic_slice_in_dim(windows, m * share, share, 0)
    if share % per:
        tgt = tgt.transpose(1, 0, 2).reshape(own + 8, per, vox).transpose(1, 0, 2)
    frame_weight = jnp.pad(valid[0].astype(F32) / total, (3, 3))
    frame_weight = lax.dynamic_slice_in_dim(frame_weight, q * own, own + 6, 0)


    logits, out, homecoming = [], None, []
    for layer in range(per):
        _, pieces, ranks, slopes, xcs = ready[layer]
        part = share // per if share % per == 0 else 1
        logit, grads, out, sent = run_temporal(
            meta,
            slots["temporal", layer],
            (wt, wtb, whc, tgt[layer * part : (layer + 1) * part], grads, wb),
            frame_weight,
            pieces,
            ranks,
            slopes,
            xcs,
            layer == per - 1,
            out,
            dims,
            layers,
        )
        logits.append(logit[3 : 3 + own, 0])
        if layer < per - 1:
            following = ready[layer + 1]
            following[1], sent = lax.optimization_barrier((following[1], sent))
        homecoming.append([swap(sent[s - 1][:, :, None], -s) for s in range(1, g)])
    homecoming[:-1], grads = lax.optimization_barrier((homecoming[:-1], grads))

    logits = jnp.concatenate(logits, axis=1).astype(BF16).reshape(own, share, spot)
    logits = logits.transpose(1, 0, 2)
    logits = jnp.concatenate([logits] * g)
    logits = lax.all_to_all(logits, "tile", 0, 0, tiled=True)
    grads, arrived, homecoming = sum_over_tiles(sum_over_reps(grads, 1), tiles, g, homecoming)
    for layer in range(per):
        for s in range(1, g):
            place = (m + s) % g * per + layer
            out = lax.dynamic_update_slice_in_dim(out, homecoming[layer][s - 1], place, 2)
    logits, gs, gt, gh = run_finish(grads, arrived, logits, groups, g)
    logits, gh = logits.reshape(1, total, spot), gh[0]
    return logits, out[None], gs, gt, gh


def solution(mesh):
    placed = (
        P("rep", "tile", None, None, None, None),
        P(),
        P(),
        P(),
        P("rep", None, "tile"),
        P("rep", None),
    )
    return jax.shard_map(
        body,
        mesh=mesh,
        in_specs=placed,
        out_specs=(
            P("rep", None, "tile"),
            P("rep", "tile", None, None, None, None),
            P(None, "rep", None),
            P(None, None, "rep", None),
            P("rep"),
        ),
        check_vma=False,
    )
```

```python
import functools

import jax
import jax.numpy as jnp
from jax import lax
from jax.experimental import pallas as pl
from jax.experimental.pallas import tpu as pltpu
from jax.sharding import PartitionSpec as P
import numpy as np

EPS = 1e-06
HALO = 6
F32 = jnp.float32
BF16 = jnp.bfloat16
VMEM_LIMIT = 52 * 1024 * 1024


def sigmoid(u):
    return 0.5 * jnp.tanh(0.5 * u) + 0.5


def silu_parts(half):
    t = jnp.tanh(half)
    a = 1.0 + t
    y = half * a
    return y, a + y * (1.0 - t)


def dot_nn(a, b):
    return jnp.dot(a, b, preferred_element_type=F32)


def dot_nt(a, b):
    return lax.dot_general(a, b, (((1,), (1,)), ((), ())), preferred_element_type=F32)


def channel_sum(v):
    return jnp.sum(v, axis=0, keepdims=True)


def spread(row, dst, r, order):
    chans, width = row.shape
    lane = lax.broadcasted_iota(jnp.int32, (chans, width), 1)
    prev = jnp.where(lane > 0, pltpu.roll(row, 1, 1), 0.0)
    nxt = jnp.where(lane < width - 1, pltpu.roll(row, width - 1, 1), 0.0)
    parts = (prev, row, nxt) if order > 0 else (nxt, row, prev)
    for j in range(3):
        dst[j * chans : (j + 1) * chans, r * width : (r + 1) * width] = parts[j].astype(BF16)


def conv_rows(w_ref, src, sign, rows, chans, width):
    step = 2 * width
    outs = [dot_nn(w_ref[...], src[:, p * step : (p + 1) * step]) for p in range(rows // 2)]

    def piece(i, r):
        half = slice((r % 2) * width, (r % 2 + 1) * width)
        return outs[r // 2][i * chans : (i + 1) * chans, half]

    result = []
    for r in range(rows):
        acc = piece(1, r)
        for i in (-1, 1):
            if 0 <= r + sign * i < rows:
                acc = acc + piece(i + 1, r + sign * i)
        result.append(acc)
    return result


def forward_kernel(middle, base, meta_ref, x_ref, w_ref, feat_ref, slope_ref, xc_ref, *rest):
    xt, xs, wf = rest[-3:]
    frames, chans, _, rows, width = x_ref.shape

    @pl.when((pl.program_id(0) == 0) & (pl.program_id(1) == 0))
    def _():
        for i in range(3):
            for j in range(3):
                wf[i * chans : (i + 1) * chans, j * chans : (j + 1) * chans] = (
                    w_ref[3 * i + j].astype(F32) * 0.5
                ).astype(BF16)

    for n in range(frames):
        xt[n] = x_ref[n, :, 0].astype(F32).reshape(chans * rows, width)
    for n in range(frames):
        for r in range(rows):
            row = xt[n, pl.ds(r, chans, stride=rows), :]
            spread(row, xs.at[n], r, 1)
            xc_ref[0, n, :, r * width : (r + 1) * width] = row.astype(BF16)
    for n in range(frames):
        for r, half in enumerate(conv_rows(wf, xs.at[n], 1, rows, chans, width)):
            cols = slice(r * width, (r + 1) * width)
            y, slope = silu_parts(half)
            feat_ref[0, n, :, cols] = y.astype(BF16)
            slope_ref[0, n, :, cols] = slope.astype(BF16)
    if middle:

        @pl.when(pl.program_id(1) == meta_ref[base + 1])
        def _():
            rest[0][0] = feat_ref[0]


def run_forward(meta, base, middle, count, x, w_spatial):
    n, chans, _, rows, width = x.shape
    vox = rows * width
    sds = jax.ShapeDtypeStruct
    frames = middle if middle and n % middle == 0 else 2 - n % 2
    shapes = [sds((count, n, chans, vox), BF16)] * 3
    specs = [pl.BlockSpec((1, frames, chans, vox), lambda k, f, meta: (k, f, 0, 0))] * 3
    if middle:
        shapes.append(sds((count, middle, chans, vox), BF16))
        specs.append(pl.BlockSpec((1, middle, chans, vox), lambda k, f, meta: (k, 0, 0, 0)))
    return pl.pallas_call(
        functools.partial(forward_kernel, middle, base),
        name="conv_forward",
        out_shape=shapes,
        grid_spec=pltpu.PrefetchScalarGridSpec(
            num_scalar_prefetch=1,
            grid=(count, n // frames),
            in_specs=[
                pl.BlockSpec(
                    (frames, chans, 1, rows, width),
                    lambda k, f, meta: (f, 0, meta[base] + k, 0, 0),
                ),
                pl.BlockSpec((9, chans, chans), lambda k, f, meta: (0, 0, 0)),
            ],
            out_specs=specs,
            scratch_shapes=[
                pltpu.VMEM((frames, chans * rows, width), F32),
                pltpu.VMEM((frames, 3 * chans, vox), BF16),
                pltpu.VMEM((3 * chans, 3 * chans), BF16),
            ],
        ),
        cost_estimate=pl.CostEstimate(flops=1000, bytes_accessed=1000, transcendentals=0),
    )(meta, x, w_spatial)


def window_kernel(own, g, tgt_ref, win_ref, pad):
    total, spot = tgt_ref.shape[1:]
    pad[0:8] = jnp.zeros((8, spot), F32)
    pad[8 : 8 + total] = tgt_ref[0].astype(F32)
    pad[8 + total :] = jnp.zeros((8, spot), F32)
    for a in range(win_ref.shape[0]):
        first = a // g * own + 4
        win_ref[a] = pad[first : first + own + 8].astype(BF16)


def run_windows(targets, tiles, own, g):
    _, total, spot = targets.shape
    vmem = pl.BlockSpec(memory_space=pltpu.VMEM)
    return pl.pallas_call(
        functools.partial(window_kernel, own, g),
        name="windows",
        out_shape=jax.ShapeDtypeStruct((tiles, own + 8, spot), BF16),
        in_specs=[vmem],
        out_specs=vmem,
        scratch_shapes=[pltpu.VMEM((total + 16, spot), F32)],
        cost_estimate=pl.CostEstimate(flops=1000, bytes_accessed=1000, transcendentals=0),
    )(targets)


def finish_kernel(arrived, g, value_ref, *rest):
    logit_ref, out_ref, gs_ref, gt_ref, gh_ref = rest[arrived:]
    part, chans = value_ref.shape[1:]
    groups = out_ref.shape[0]
    member = lax.axis_index("tile") // groups
    for q in range(groups):
        out_ref[q] = logit_ref[q * g + member]

    def total(k):
        acc = value_ref[k]
        for ref in rest[:arrived]:
            acc = acc + ref[k].astype(F32)
        return acc

    for k in range(9):
        gs_ref[k] = total(k)
    for k in range(6):
        gt_ref[k // 3, k % 3] = total(9 + k)
    shape = (chans, part)
    mine = lax.broadcasted_iota(jnp.int32, shape, 1) + lax.axis_index("rep") * part
    chosen = jnp.where(lax.broadcasted_iota(jnp.int32, shape, 0) == mine, 1.0, 0.0)
    picked = jnp.dot(total(15), chosen, precision=lax.Precision.HIGHEST, preferred_element_type=F32)
    gh_ref[...] = picked[0:1]


def run_finish(value, arrived, logits, groups, g):
    _, part, chans = value.shape
    _, own, spot = logits.shape
    sds = jax.ShapeDtypeStruct
    vmem = pl.BlockSpec(memory_space=pltpu.VMEM)
    return pl.pallas_call(
        functools.partial(finish_kernel, len(arrived), g),
        name="finish",
        out_shape=(
            sds((groups, own, spot), BF16),
            sds((9, part, chans), F32),
            sds((2, 3, part, chans), F32),
            sds((1, part), F32),
        ),
        in_specs=[vmem] * (2 + len(arrived)),
        out_specs=[vmem] * 4,
        cost_estimate=pl.CostEstimate(flops=1000, bytes_accessed=1000, transcendentals=0),
    )(value, *arrived, logits)


def temporal_kernel(
    places,
    last,
    aliased,
    base,
    dims,
    meta_ref,
    weight_ref,
    wt_ref,
    wtb_ref,
    whc_ref,
    tgt_ref,
    init_ref,
    wb_ref,
    *rest,
):
    own, chans, vox, total, members, width = dims
    rows = vox // width
    here = own // members
    counts = len(places)
    pieces = [ref.at[k] for ref, k in zip(rest[:counts], places)]
    slope_in = [ref.at[k] for ref, k in zip(rest[counts : counts + members], places)]
    xs_in = [ref.at[k] for ref, k in zip(rest[counts + members : counts + 2 * members], places)]
    rest = rest[counts + 2 * members + aliased :]
    logit_ref, grad_ref = rest[:2]
    out_ref, send_ref, back = rest[2:4] + rest[-1:]
    taps = grad_ref
    if last:
        grad_ref = rest[-2]
    (
        feats,
        slope,
        xs,
        n0,
        inv0,
        h1,
        n1,
        inv1,
        sp0,
        dh2,
        dm1,
        dm0,
        final_ref,
        dlog,
        ds,
        xt,
        tgt,
        sems,
    ) = rest[4:22]
    step = min(256, vox)
    lo, hi = HALO, HALO + own
    first = meta_ref[base]
    chunks = [slice(p * step, (p + 1) * step) for p in range(vox // step)]
    whole = slice(0, vox)

    early = [
        pltpu.make_async_copy(src, feats.at[pl.ds(meta_ref[base + 1 + k], src.shape[0])], sems.at[k])
        for k, src in enumerate(pieces)
    ]
    late = []
    for k in range(members):
        spot = pl.ds(meta_ref[base + 1 + k] - HALO, here)
        late.append(pltpu.make_async_copy(slope_in[k], slope.at[spot], sems.at[len(early) + k]))
        late.append(
            pltpu.make_async_copy(xs_in[k], xs.at[spot], sems.at[len(early) + members + k])
        )
    for copy in early + late:
        copy.start()
    for c in range(tgt_ref.shape[0]):
        tgt[:, c * tgt_ref.shape[2] : (c + 1) * tgt_ref.shape[2]] = tgt_ref[c].astype(F32)
    for copy in early:
        copy.wait()

    def frame_ok(f):
        g = first + f - HALO
        return jnp.where((g >= 0) & (g < total), 1.0, 0.0).astype(F32)

    def loop(a, b, *fns):
        def every(f, carry):
            for fn in fns:
                fn(f)
            return carry

        lax.fori_loop(a, b, every, 0)

    def stack(ref, f0, f1, f2, cols):
        return jnp.concatenate([ref[f0, :, cols], ref[f1, :, cols], ref[f2, :, cols]], axis=0)

    def rms(hid):
        return lax.rsqrt(channel_sum(hid * hid) * (1.0 / chans) + EPS)

    def norm0(f):
        for cols in chunks:
            hid = feats[f, :, cols].astype(F32)
            inv = rms(hid)
            n0[f, :, cols] = (hid * inv).astype(BF16)
            inv0[f, :, cols] = inv

    def layer0(f):
        ok = frame_ok(f)
        for cols in chunks:
            y, slope2 = silu_parts(dot_nn(wt_ref[0], stack(n0, f - 1, f, f + 1, cols)))
            hid = feats[f, :, cols].astype(F32) + y
            inv = rms(hid) * ok
            h1[f, :, cols] = hid
            n1[f, :, cols] = (hid * inv).astype(BF16)
            inv1[f, :, cols] = inv
            sp0[f, :, cols] = slope2

    def layer1(f):
        weight = weight_ref[f - 3]
        for cols in chunks:
            y, slope2 = silu_parts(dot_nn(wt_ref[1], stack(n1, f - 2, f, f + 2, cols)))
            hid = h1[f, :, cols] + y
            inv = rms(hid)
            unit = hid * inv
            logit = channel_sum(unit * whc_ref[...])
            logit_ref[f - 3, :, cols] = logit
            dlogit = weight * (sigmoid(logit) - tgt[pl.ds(f - 2, 1), cols])
            final_ref[f, :, cols] = unit.astype(BF16)
            dlog[f, :, cols] = dlogit
            dhid = (inv * dlogit) * (whc_ref[...] - unit * (logit * (1.0 / chans)))
            dh2[f, :, cols] = dhid
            dm1[f, :, cols] = (dhid * slope2).astype(BF16)

    def back1(f):
        for cols in chunks:
            dnorm = dot_nn(wtb_ref[1], stack(dm1, f + 2, f, f - 2, cols))
            unit = n1[f, :, cols].astype(F32)
            mean = channel_sum(dnorm * unit) * (1.0 / chans)
            dhid = dh2[f, :, cols] + inv1[f, :, cols] * (dnorm - unit * mean)
            dh2[f, :, cols] = dhid
            dm0[f, :, cols] = (dhid * sp0[f, :, cols]).astype(BF16)

    def back0(f):
        b = f - HALO
        for cols in chunks:
            dnorm = dot_nn(wtb_ref[0], stack(dm0, f + 1, f, f - 1, cols))
            unit = n0[f, :, cols].astype(F32)
            mean = channel_sum(dnorm * unit) * (1.0 / chans)
            dhid = dh2[f, :, cols] + inv0[f, :, cols] * (dnorm - unit * mean)
            dpre = dhid * slope[b, :, cols].astype(F32)
            for r in range(step // width):
                spread(dpre[:, r * width : (r + 1) * width], ds, cols.start // width + r, -1)
        center = xs[b]
        blank = jnp.zeros((chans, width), BF16)
        taller = jnp.concatenate([center[:, width:], blank], axis=1)
        lower = jnp.concatenate([blank, center[:, :-width]], axis=1)
        grad = dot_nt(ds[...], jnp.concatenate([lower, center, taller], axis=0))
        for j in range(3):
            grad_ref[j] += grad[j * chans : (j + 1) * chans]
        grad_ref[3] += dot_nt(dm0[f], stack(n0, f - 1, f, f + 1, whole))
        grad_ref[4] += dot_nt(dm1[f], stack(n1, f - 2, f, f + 2, whole))
        head = jnp.broadcast_to(dlog[f].astype(BF16), (chans, vox))
        grad_ref[5, :, :chans] += dot_nt(head, final_ref[f])
        for r, row in enumerate(conv_rows(wb_ref, ds, -1, rows, chans, width)):
            xt[pl.ds(r, chans, stride=rows), :] = row
        back[b] = xt[...].astype(BF16).reshape(chans, rows, width)

    grad_ref[...] = init_ref[...]
    stages = [
        (back0, 5, lo, hi),
        (back1, 3, lo - 1, hi + 1),
        (layer1, 0, 3, hi + 3),
        (layer0, -3, 1, hi + HALO - 1),
        (norm0, -5, 0, hi + HALO),
    ]
    cuts = sorted({a + d for _, d, a, _ in stages} | {b + d for _, d, _, b in stages})
    for a, b in zip(cuts, cuts[1:]):
        active = [(fn, d) for fn, d, p, n in stages if p + d <= a and b <= n + d]
        if a == lo + 5:
            for copy in late:
                copy.wait()
        loop(0, b - a, *[lambda i, fn=fn, f=a - d: fn(i + f) for fn, d in active])
    layer = meta_ref[base + 1 + counts]
    leaving = []
    for k in range(members):
        src = back.at[pl.ds(meta_ref[base + 1 + k] - HALO, here)]
        dst = send_ref.at[k - 1] if k else out_ref.at[:, :, layer]
        leaving.append(pltpu.make_async_copy(src, dst, sems.at[k]))
    for copy in leaving:
        copy.start()
    if last:
        for k in range(3):
            cols = slice(k * chans, (k + 1) * chans)
            for j in range(3):
                taps[3 * k + j] = grad_ref[j, :, cols] * 0.5
            for l in range(2):
                taps[9 + 3 * l + k] = grad_ref[3 + l, :, cols] * 0.5
        taps[15] = grad_ref[5, :, :chans]
    for copy in leaving:
        copy.wait()


def run_temporal(meta, base, vmem_args, weights, pieces, places, slopes, xss, last, into, dims, layers):
    own, chans, vox, total, members, width = dims
    rows, here = vox // width, own // members
    every = own + 2 * HALO
    sds = jax.ShapeDtypeStruct
    smem = pl.BlockSpec(memory_space=pltpu.SMEM)
    vmem = pl.BlockSpec(memory_space=pltpu.VMEM)
    hbm = pl.BlockSpec(memory_space=pl.ANY)
    loose = len(pieces) + 2 * members
    aliased = into is not None
    frame = lambda n, c, dt: pltpu.VMEM((n, c, vox), dt)
    sums = (6, chans, 3 * chans)
    shapes = [
        sds((own + 6, 1, vox), F32),
        sds((16, chans, chans) if last else sums, F32),
        sds((here, chans, layers, rows, width), BF16),
        sds((members - 1, here, chans, rows, width), BF16),
    ]
    specs = [vmem, vmem, hbm, hbm]
    return pl.pallas_call(
        functools.partial(temporal_kernel, tuple(places), last, aliased, base, dims),
        name="temporal",
        out_shape=shapes,
        in_specs=[smem, smem] + [vmem] * len(vmem_args) + [hbm] * (loose + aliased),
        out_specs=specs,
        input_output_aliases={2 + len(vmem_args) + loose: 2} if aliased else {},
        scratch_shapes=[
            frame(every, chans, BF16),
            frame(own, chans, BF16),
            frame(own, chans, BF16),
            frame(every, chans, BF16),
            frame(every, 1, F32),
            frame(every, chans, F32),
            frame(every, chans, BF16),
            frame(every, 1, F32),
            frame(every, chans, F32),
            frame(every, chans, F32),
            frame(every, chans, BF16),
            frame(every, chans, BF16),
            frame(every, chans, BF16),
            frame(every, 1, F32),
            pltpu.VMEM((3 * chans, vox), BF16),
            pltpu.VMEM((chans * rows, width), F32),
            pltpu.VMEM((own + 8, vox), F32),
            pltpu.SemaphoreType.DMA((loose,)),
        ]
        + [pltpu.VMEM(sums, F32)] * last
        + [pltpu.VMEM((own, chans, rows, width), BF16)],
        compiler_params=pltpu.CompilerParams(vmem_limit_bytes=VMEM_LIMIT),
        cost_estimate=pl.CostEstimate(
            flops=3000 * own * chans * vox, bytes_accessed=100 * own * chans * vox, transcendentals=0
        ),
    )(meta, weights, *vmem_args, *pieces, *slopes, *xss, *([into] if aliased else []))


def group_size(tiles, frames_here, layers):
    for g in range(1, layers + 1):
        if layers % g == 0 and tiles % g == 0 and g * frames_here >= HALO:
            return g
    return layers


def pick(parts, start):
    doubled = jnp.stack(parts + parts)
    return lax.dynamic_slice_in_dim(doubled, start, len(parts), 0)


def take(value, index, axis):
    return lax.dynamic_index_in_dim(value, index, axis, False)


def sum_over_tiles(value, tiles, g, others):
    if tiles & (tiles - 1):
        return lax.psum(value.astype(BF16), "tile").astype(F32), [], others
    steps = [2**k for k in range(tiles.bit_length() - 1)]
    outer, inner = [k for k in steps if k >= g], [k for k in steps if k < g]
    rounds = [part[i : i + 2] for part in (outer, inner) for i in range(0, len(part), 2)]
    for number, bits in enumerate(rounds):
        if number == len(rounds) - 1:
            value, others = lax.optimization_barrier((value, others))
        masks = bits + [sum(bits)] * (len(bits) - 1)
        sent, arrived = value.astype(BF16), []
        for k in masks:
            pairs = [(a, a ^ k) for a in range(tiles)]
            arrived.append(lax.ppermute(sent, "tile", pairs))
        if number < len(rounds) - 1:
            for piece in arrived:
                value = value + piece.astype(F32)
    return value, arrived, others


def sum_over_reps(value, axis):
    reps = lax.axis_size("rep")
    r = lax.axis_index("rep")
    n = value.shape[axis] // reps

    def share(k):
        return lax.dynamic_slice_in_dim(value, (k % reps) * n, n, axis)

    acc = share(r)
    for s in range(1, reps):
        pairs = [(a, (a + s) % reps) for a in range(reps)]
        acc = acc + lax.ppermute(share(r + s).astype(BF16), "rep", pairs).astype(F32)
    return acc


def body(inputs, w_spatial, w_temporal, w_head, targets, valid):
    _, here, chans, layers, rows, width = inputs.shape
    tiles = lax.axis_size("tile")
    total = here * tiles
    g = group_size(tiles, here, layers)
    per = layers // g
    own = g * here
    vox = rows * width
    t = lax.axis_index("tile")
    q, m = t // g, t % g
    spot = targets.shape[2]
    share = groups = tiles // g
    x = inputs[0]

    def swap(value, s):
        pairs = [(a, a // g * g + (a % g + s) % g) for a in range(tiles)]
        return lax.ppermute(value, "tile", pairs)

    def hop(value, shifts):
        pairs = [(a, a + shifts[a % g] * g) for a in range(tiles)]
        return lax.ppermute(value, "tile", [p for p in pairs if 0 <= p[1] < tiles])

    halved = (w_temporal.astype(F32) * 0.5).astype(BF16)
    wt = halved.transpose(0, 2, 1, 3).reshape(2, chans, 3 * chans)
    wtb = halved.transpose(0, 3, 1, 2).reshape(2, chans, 3 * chans)
    w9 = (w_spatial.astype(F32) * 0.5).astype(BF16).reshape(3, 3, chans, chans)
    wb = w9.transpose(0, 3, 1, 2).reshape(3 * chans, 3 * chans)
    whc = w_head.astype(F32)[:, None]

    mirrored = g == 2 and here <= HALO <= 2 * here
    extra = HALO - here if mirrored else 0
    up, down = own + HALO, HALO - here
    table, slots = [], {}
    for a in range(tiles):
        aq, am = a // g, a % g
        spots = [HALO + (am - s) % g * here for s in range(g)]
        if mirrored:
            for k in range(2):
                spots.append(up if am == k else down)
                if extra:
                    spots.append(0 if am == k else up + here)
        else:
            left, d = HALO, 1
            while left > 0:
                k = min(left, own)
                spots += [left - k, HALO + d * own]
                left -= k
                d += 1
        late = (here - extra) // max(extra, 1)
        row = []

        def put(name, *values):
            slots[name] = len(row)
            row.extend(values)

        put("mine", am * per, late if am == 0 else 0)
        for layer in range(per):
            put(("theirs", layer), 0, late if am == 1 else 0)
            put(("temporal", layer), aq * own, *spots, am * per + layer)
        table.append(row)
    meta = lax.dynamic_index_in_dim(jnp.asarray(np.array(table, np.int32)), t, 0, False)

    leaving = [
        [lax.dynamic_slice_in_dim(x, (m + s) % g * per + layer, 1, 2) for s in range(1, g)]
        for layer in range(per)
    ]
    arriving = [[swap(piece, s + 1) for s, piece in enumerate(leaving[0])]]
    mine = list(run_forward(meta, slots["mine"], extra, per, x, w_spatial))
    leaving[1:], mine[1] = lax.optimization_barrier((leaving[1:], mine[1]))
    for pieces in leaving[1:]:
        arriving.append([swap(piece, s + 1) for s, piece in enumerate(pieces)])
    ahead = []
    if mirrored:
        ahead.append(hop(mine[0], (-1, 1)))
        if extra:
            mine[3], arriving[0] = lax.optimization_barrier((mine[3], arriving[0]))
            ahead.append(hop(mine[3], (1, -1)))

    dims = (own, chans, vox, total, g, width)
    grads = jnp.zeros((6, chans, 3 * chans), F32)
    asked, mine[2] = lax.optimization_barrier((targets, mine[2]))
    ready = []
    for layer in range(per):
        done = [mine]
        if layer:
            ahead, arriving[layer] = lax.optimization_barrier((ahead, arriving[layer]))
        for piece in arriving[layer]:
            done.append(list(run_forward(meta, slots["theirs", layer], extra, 1, piece, w_spatial)))
        pieces = [d[0] for d in done]
        ranks = [layer] + [0] * (g - 1)
        if mirrored:
            pieces += ahead
            pieces.append(hop(done[1][0], (1, -1)))
            if extra:
                pieces.append(hop(done[1][3], (-1, 1)))
            for k in range(2):
                ranks += [0 if k else layer] * len(ahead)
        else:
            block = [p[k] for p, k in zip(pieces, ranks)]
            block = pick(block[::-1], g - 1 - m).reshape(own, chans, vox)
            left, d = HALO, 1
            while left > 0:
                k = min(left, own)
                pieces.append(hop(block[own - k :], (d,) * g)[None])
                pieces.append(hop(block[:k], (-d,) * g)[None])
                ranks += [0, 0]
                left -= k
                d += 1
        ready.append([layer, pieces, ranks, [d[1] for d in done], [d[2] for d in done]])

    windows = run_windows(asked, tiles, own, g)
    windows = lax.all_to_all(windows, "tile", 0, 0, tiled=True)
    tgt = lax.dynamic_slice_in_dim(windows, m * share, share, 0)
    if share % per:
        tgt = tgt.transpose(1, 0, 2).reshape(own + 8, per, vox).transpose(1, 0, 2)
    frame_weight = jnp.pad(valid[0].astype(F32) / total, (3, 3))
    frame_weight = lax.dynamic_slice_in_dim(frame_weight, q * own, own + 6, 0)


    logits, out, homecoming = [], None, []
    for layer in range(per):
        _, pieces, ranks, slopes, xcs = ready[layer]
        part = share // per if share % per == 0 else 1
        logit, grads, out, sent = run_temporal(
            meta,
            slots["temporal", layer],
            (wt, wtb, whc, tgt[layer * part : (layer + 1) * part], grads, wb),
            frame_weight,
            pieces,
            ranks,
            slopes,
            xcs,
            layer == per - 1,
            out,
            dims,
            layers,
        )
        logits.append(logit[3 : 3 + own, 0])
        if layer < per - 1:
            following = ready[layer + 1]
            following[1], sent = lax.optimization_barrier((following[1], sent))
        homecoming.append([swap(sent[s - 1][:, :, None], -s) for s in range(1, g)])
    homecoming[:-1], grads = lax.optimization_barrier((homecoming[:-1], grads))

    logits = jnp.concatenate(logits, axis=1).astype(BF16).reshape(own, share, spot)
    logits = logits.transpose(1, 0, 2)
    logits = jnp.concatenate([logits] * g)
    logits = lax.all_to_all(logits, "tile", 0, 0, tiled=True)
    grads, arrived, homecoming = sum_over_tiles(sum_over_reps(grads, 1), tiles, g, homecoming)
    for layer in range(per):
        for s in range(1, g):
            place = (m + s) % g * per + layer
            out = lax.dynamic_update_slice_in_dim(out, homecoming[layer][s - 1], place, 2)
    logits, gs, gt, gh = run_finish(grads, arrived, logits, groups, g)
    logits, gh = logits.reshape(1, total, spot), gh[0]
    return logits, out[None], gs, gt, gh


def solution(mesh):
    placed = (
        P("rep", "tile", None, None, None, None),
        P(),
        P(),
        P(),
        P("rep", None, "tile"),
        P("rep", None),
    )
    return jax.shard_map(
        body,
        mesh=mesh,
        in_specs=placed,
        out_specs=(
            P("rep", None, "tile"),
            P("rep", "tile", None, None, None, None),
            P(None, "rep", None),
            P(None, None, "rep", None),
            P("rep"),
        ),
        check_vma=False,
    )
```

```python
import functools

import jax
import jax.numpy as jnp
from jax import lax
from jax.experimental import pallas as pl
from jax.experimental.pallas import tpu as pltpu
from jax.sharding import PartitionSpec as P
import numpy as np

EPS = 1e-06
HALO = 6
F32 = jnp.float32
BF16 = jnp.bfloat16
VMEM_LIMIT = 52 * 1024 * 1024


def sigmoid(u):
    return 0.5 * jnp.tanh(0.5 * u) + 0.5


def silu_parts(half):
    t = jnp.tanh(half)
    a = 1.0 + t
    y = half * a
    return y, a + y * (1.0 - t)


def dot_nn(a, b):
    return jnp.dot(a, b, preferred_element_type=F32)


def dot_nt(a, b):
    return lax.dot_general(a, b, (((1,), (1,)), ((), ())), preferred_element_type=F32)


def channel_sum(v):
    return jnp.sum(v, axis=0, keepdims=True)


def spread(row, dst, r, order):
    chans, width = row.shape
    lane = lax.broadcasted_iota(jnp.int32, (chans, width), 1)
    prev = jnp.where(lane > 0, pltpu.roll(row, 1, 1), 0.0)
    nxt = jnp.where(lane < width - 1, pltpu.roll(row, width - 1, 1), 0.0)
    parts = (prev, row, nxt) if order > 0 else (nxt, row, prev)
    for j in range(3):
        dst[j * chans : (j + 1) * chans, r * width : (r + 1) * width] = parts[j].astype(BF16)


def conv_rows(w_ref, src, sign, rows, chans, width):
    step = 2 * width
    outs = [dot_nn(w_ref[...], src[:, p * step : (p + 1) * step]) for p in range(rows // 2)]

    def piece(i, r):
        half = slice((r % 2) * width, (r % 2 + 1) * width)
        return outs[r // 2][i * chans : (i + 1) * chans, half]

    result = []
    for r in range(rows):
        acc = piece(1, r)
        for i in (-1, 1):
            if 0 <= r + sign * i < rows:
                acc = acc + piece(i + 1, r + sign * i)
        result.append(acc)
    return result


def forward_kernel(middle, block, x_ref, w_ref, feat_ref, slope_ref, xc_ref, *rest):
    xt, xs, wf = rest[-3:]
    frames, chans, _, rows, width = x_ref.shape

    @pl.when((pl.program_id(0) == 0) & (pl.program_id(1) == 0))
    def _():
        for i in range(3):
            for j in range(3):
                wf[i * chans : (i + 1) * chans, j * chans : (j + 1) * chans] = (
                    w_ref[3 * i + j].astype(F32) * 0.5
                ).astype(BF16)

    for n in range(frames):
        xt[n] = x_ref[n, :, 0].astype(F32).reshape(chans * rows, width)
    for n in range(frames):
        for r in range(rows):
            row = xt[n, pl.ds(r, chans, stride=rows), :]
            spread(row, xs.at[n], r, 1)
            xc_ref[0, n, :, r * width : (r + 1) * width] = row.astype(BF16)
    for n in range(frames):
        for r, half in enumerate(conv_rows(wf, xs.at[n], 1, rows, chans, width)):
            cols = slice(r * width, (r + 1) * width)
            y, slope = silu_parts(half)
            feat_ref[0, n, :, cols] = y.astype(BF16)
            slope_ref[0, n, :, cols] = slope.astype(BF16)
    if middle:

        @pl.when(pl.program_id(1) == block())
        def _():
            rest[0][0] = feat_ref[0]


def run_forward(first, block, middle, count, x, w_spatial):
    n, chans, _, rows, width = x.shape
    vox = rows * width
    sds = jax.ShapeDtypeStruct
    frames = middle if middle and n % middle == 0 else 2 - n % 2
    shapes = [sds((count, n, chans, vox), BF16)] * 3
    specs = [pl.BlockSpec((1, frames, chans, vox), lambda k, f: (k, f, 0, 0))] * 3
    if middle:
        shapes.append(sds((count, middle, chans, vox), BF16))
        specs.append(pl.BlockSpec((1, middle, chans, vox), lambda k, f: (k, 0, 0, 0)))
    return pl.pallas_call(
        functools.partial(forward_kernel, middle, block),
        name="conv_forward",
        out_shape=shapes,
        grid_spec=pl.GridSpec(
            grid=(count, n // frames),
            in_specs=[
                pl.BlockSpec(
                    (frames, chans, 1, rows, width),
                    lambda k, f: (f, 0, first() + k, 0, 0),
                ),
                pl.BlockSpec((9, chans, chans), lambda k, f: (0, 0, 0)),
            ],
            out_specs=specs,
            scratch_shapes=[
                pltpu.VMEM((frames, chans * rows, width), F32),
                pltpu.VMEM((frames, 3 * chans, vox), BF16),
                pltpu.VMEM((3 * chans, 3 * chans), BF16),
            ],
        ),
        cost_estimate=pl.CostEstimate(flops=1000, bytes_accessed=1000, transcendentals=0),
    )(x, w_spatial)


def window_kernel(own, g, tgt_ref, win_ref, pad):
    total, spot = tgt_ref.shape[1:]
    pad[0:8] = jnp.zeros((8, spot), F32)
    pad[8 : 8 + total] = tgt_ref[0].astype(F32)
    pad[8 + total :] = jnp.zeros((8, spot), F32)
    for a in range(win_ref.shape[0]):
        first = a // g * own + 4
        win_ref[a] = pad[first : first + own + 8].astype(BF16)


def run_windows(targets, tiles, own, g):
    _, total, spot = targets.shape
    vmem = pl.BlockSpec(memory_space=pltpu.VMEM)
    return pl.pallas_call(
        functools.partial(window_kernel, own, g),
        name="windows",
        out_shape=jax.ShapeDtypeStruct((tiles, own + 8, spot), BF16),
        in_specs=[vmem],
        out_specs=vmem,
        scratch_shapes=[pltpu.VMEM((total + 16, spot), F32)],
        cost_estimate=pl.CostEstimate(flops=1000, bytes_accessed=1000, transcendentals=0),
    )(targets)


def finish_kernel(arrived, g, value_ref, *rest):
    logit_ref, out_ref, gs_ref, gt_ref, gh_ref = rest[arrived:]
    part, chans = value_ref.shape[1:]
    groups = out_ref.shape[0]
    member = lax.axis_index("tile") // groups
    for q in range(groups):
        out_ref[q] = logit_ref[q * g + member]

    def total(k):
        acc = value_ref[k]
        for ref in rest[:arrived]:
            acc = acc + ref[k].astype(F32)
        return acc

    for k in range(9):
        gs_ref[k] = total(k)
    for k in range(6):
        gt_ref[k // 3, k % 3] = total(9 + k)
    shape = (chans, part)
    mine = lax.broadcasted_iota(jnp.int32, shape, 1) + lax.axis_index("rep") * part
    chosen = jnp.where(lax.broadcasted_iota(jnp.int32, shape, 0) == mine, 1.0, 0.0)
    picked = jnp.dot(total(15), chosen, precision=lax.Precision.HIGHEST, preferred_element_type=F32)
    gh_ref[...] = picked[0:1]


def run_finish(value, arrived, logits, groups, g):
    _, part, chans = value.shape
    _, own, spot = logits.shape
    sds = jax.ShapeDtypeStruct
    vmem = pl.BlockSpec(memory_space=pltpu.VMEM)
    return pl.pallas_call(
        functools.partial(finish_kernel, len(arrived), g),
        name="finish",
        out_shape=(
            sds((groups, own, spot), BF16),
            sds((9, part, chans), F32),
            sds((2, 3, part, chans), F32),
            sds((1, part), F32),
        ),
        in_specs=[vmem] * (2 + len(arrived)),
        out_specs=[vmem] * 4,
        cost_estimate=pl.CostEstimate(flops=1000, bytes_accessed=1000, transcendentals=0),
    )(value, *arrived, logits)


def temporal_kernel(
    places,
    last,
    aliased,
    base,
    dims,
    meta_ref,
    weight_ref,
    wt_ref,
    wtb_ref,
    whc_ref,
    tgt_ref,
    init_ref,
    wb_ref,
    *rest,
):
    own, chans, vox, total, members, width = dims
    rows = vox // width
    here = own // members
    counts = len(places)
    pieces = [ref.at[k] for ref, k in zip(rest[:counts], places)]
    slope_in = [ref.at[k] for ref, k in zip(rest[counts : counts + members], places)]
    xs_in = [ref.at[k] for ref, k in zip(rest[counts + members : counts + 2 * members], places)]
    rest = rest[counts + 2 * members + aliased :]
    logit_ref, grad_ref = rest[:2]
    out_ref, send_ref, back = rest[2:4] + rest[-1:]
    taps = grad_ref
    if last:
        grad_ref = rest[-2]
    (
        feats,
        slope,
        xs,
        n0,
        inv0,
        h1,
        n1,
        inv1,
        sp0,
        dh2,
        dm1,
        dm0,
        final_ref,
        dlog,
        ds,
        xt,
        tgt,
        sems,
    ) = rest[4:22]
    step = min(256, vox)
    lo, hi = HALO, HALO + own
    first = meta_ref[base]
    chunks = [slice(p * step, (p + 1) * step) for p in range(vox // step)]
    whole = slice(0, vox)

    early = [
        pltpu.make_async_copy(src, feats.at[pl.ds(meta_ref[base + 1 + k], src.shape[0])], sems.at[k])
        for k, src in enumerate(pieces)
    ]
    late = []
    for k in range(members):
        spot = pl.ds(meta_ref[base + 1 + k] - HALO, here)
        late.append(pltpu.make_async_copy(slope_in[k], slope.at[spot], sems.at[len(early) + k]))
        late.append(
            pltpu.make_async_copy(xs_in[k], xs.at[spot], sems.at[len(early) + members + k])
        )
    for copy in early + late:
        copy.start()
    for c in range(tgt_ref.shape[0]):
        tgt[:, c * tgt_ref.shape[2] : (c + 1) * tgt_ref.shape[2]] = tgt_ref[c].astype(F32)
    for copy in early:
        copy.wait()

    def frame_ok(f):
        g = first + f - HALO
        return jnp.where((g >= 0) & (g < total), 1.0, 0.0).astype(F32)

    def loop(a, b, *fns):
        def every(f, carry):
            for fn in fns:
                fn(f)
            return carry

        lax.fori_loop(a, b, every, 0)

    def stack(ref, f0, f1, f2, cols):
        return jnp.concatenate([ref[f0, :, cols], ref[f1, :, cols], ref[f2, :, cols]], axis=0)

    def rms(hid):
        return lax.rsqrt(channel_sum(hid * hid) * (1.0 / chans) + EPS)

    def norm0(f):
        for cols in chunks:
            hid = feats[f, :, cols].astype(F32)
            inv = rms(hid)
            n0[f, :, cols] = (hid * inv).astype(BF16)
            inv0[f, :, cols] = inv

    def layer0(f):
        ok = frame_ok(f)
        for cols in chunks:
            y, slope2 = silu_parts(dot_nn(wt_ref[0], stack(n0, f - 1, f, f + 1, cols)))
            hid = feats[f, :, cols].astype(F32) + y
            inv = rms(hid) * ok
            h1[f, :, cols] = hid
            n1[f, :, cols] = (hid * inv).astype(BF16)
            inv1[f, :, cols] = inv
            sp0[f, :, cols] = slope2

    def layer1(f):
        weight = weight_ref[f - 3]
        for cols in chunks:
            y, slope2 = silu_parts(dot_nn(wt_ref[1], stack(n1, f - 2, f, f + 2, cols)))
            hid = h1[f, :, cols] + y
            inv = rms(hid)
            unit = hid * inv
            logit = channel_sum(unit * whc_ref[...])
            logit_ref[f - 3, :, cols] = logit
            dlogit = weight * (sigmoid(logit) - tgt[pl.ds(f - 2, 1), cols])
            final_ref[f, :, cols] = unit.astype(BF16)
            dlog[f, :, cols] = dlogit
            dhid = (inv * dlogit) * (whc_ref[...] - unit * (logit * (1.0 / chans)))
            dh2[f, :, cols] = dhid
            dm1[f, :, cols] = (dhid * slope2).astype(BF16)

    def back1(f):
        for cols in chunks:
            dnorm = dot_nn(wtb_ref[1], stack(dm1, f + 2, f, f - 2, cols))
            unit = n1[f, :, cols].astype(F32)
            mean = channel_sum(dnorm * unit) * (1.0 / chans)
            dhid = dh2[f, :, cols] + inv1[f, :, cols] * (dnorm - unit * mean)
            dh2[f, :, cols] = dhid
            dm0[f, :, cols] = (dhid * sp0[f, :, cols]).astype(BF16)

    def back0(f):
        b = f - HALO
        for cols in chunks:
            dnorm = dot_nn(wtb_ref[0], stack(dm0, f + 1, f, f - 1, cols))
            unit = n0[f, :, cols].astype(F32)
            mean = channel_sum(dnorm * unit) * (1.0 / chans)
            dhid = dh2[f, :, cols] + inv0[f, :, cols] * (dnorm - unit * mean)
            dpre = dhid * slope[b, :, cols].astype(F32)
            for r in range(step // width):
                spread(dpre[:, r * width : (r + 1) * width], ds, cols.start // width + r, -1)
        center = xs[b]
        blank = jnp.zeros((chans, width), BF16)
        taller = jnp.concatenate([center[:, width:], blank], axis=1)
        lower = jnp.concatenate([blank, center[:, :-width]], axis=1)
        grad = dot_nt(ds[...], jnp.concatenate([lower, center, taller], axis=0))
        for j in range(3):
            grad_ref[j] += grad[j * chans : (j + 1) * chans]
        grad_ref[3] += dot_nt(dm0[f], stack(n0, f - 1, f, f + 1, whole))
        grad_ref[4] += dot_nt(dm1[f], stack(n1, f - 2, f, f + 2, whole))
        head = jnp.broadcast_to(dlog[f].astype(BF16), (chans, vox))
        grad_ref[5, :, :chans] += dot_nt(head, final_ref[f])
        for r, row in enumerate(conv_rows(wb_ref, ds, -1, rows, chans, width)):
            xt[pl.ds(r, chans, stride=rows), :] = row
        back[b] = xt[...].astype(BF16).reshape(chans, rows, width)

    grad_ref[...] = init_ref[...]
    stages = [
        (back0, 5, lo, hi),
        (back1, 3, lo - 1, hi + 1),
        (layer1, 0, 3, hi + 3),
        (layer0, -3, 1, hi + HALO - 1),
        (norm0, -5, 0, hi + HALO),
    ]
    cuts = sorted({a + d for _, d, a, _ in stages} | {b + d for _, d, _, b in stages})
    for a, b in zip(cuts, cuts[1:]):
        active = [(fn, d) for fn, d, p, n in stages if p + d <= a and b <= n + d]
        if a == lo + 5:
            for copy in late:
                copy.wait()
        loop(0, b - a, *[lambda i, fn=fn, f=a - d: fn(i + f) for fn, d in active])
    layer = meta_ref[base + 1 + counts]
    leaving = []
    for k in range(members):
        src = back.at[pl.ds(meta_ref[base + 1 + k] - HALO, here)]
        dst = send_ref.at[k - 1] if k else out_ref.at[:, :, layer]
        leaving.append(pltpu.make_async_copy(src, dst, sems.at[k]))
    for copy in leaving:
        copy.start()
    if last:
        for k in range(3):
            cols = slice(k * chans, (k + 1) * chans)
            for j in range(3):
                taps[3 * k + j] = grad_ref[j, :, cols] * 0.5
            for l in range(2):
                taps[9 + 3 * l + k] = grad_ref[3 + l, :, cols] * 0.5
        taps[15] = grad_ref[5, :, :chans]
    for copy in leaving:
        copy.wait()


def run_temporal(meta, base, vmem_args, weights, pieces, places, slopes, xss, last, into, dims, layers):
    own, chans, vox, total, members, width = dims
    rows, here = vox // width, own // members
    every = own + 2 * HALO
    sds = jax.ShapeDtypeStruct
    smem = pl.BlockSpec(memory_space=pltpu.SMEM)
    vmem = pl.BlockSpec(memory_space=pltpu.VMEM)
    hbm = pl.BlockSpec(memory_space=pl.ANY)
    loose = len(pieces) + 2 * members
    aliased = into is not None
    frame = lambda n, c, dt: pltpu.VMEM((n, c, vox), dt)
    sums = (6, chans, 3 * chans)
    shapes = [
        sds((own + 6, 1, vox), F32),
        sds((16, chans, chans) if last else sums, F32),
        sds((here, chans, layers, rows, width), BF16),
        sds((members - 1, here, chans, rows, width), BF16),
    ]
    specs = [vmem, vmem, hbm, hbm]
    return pl.pallas_call(
        functools.partial(temporal_kernel, tuple(places), last, aliased, base, dims),
        name="temporal",
        out_shape=shapes,
        in_specs=[smem, smem] + [vmem] * len(vmem_args) + [hbm] * (loose + aliased),
        out_specs=specs,
        input_output_aliases={2 + len(vmem_args) + loose: 2} if aliased else {},
        scratch_shapes=[
            frame(every, chans, BF16),
            frame(own, chans, BF16),
            frame(own, chans, BF16),
            frame(every, chans, BF16),
            frame(every, 1, F32),
            frame(every, chans, F32),
            frame(every, chans, BF16),
            frame(every, 1, F32),
            frame(every, chans, F32),
            frame(every, chans, F32),
            frame(every, chans, BF16),
            frame(every, chans, BF16),
            frame(every, chans, BF16),
            frame(every, 1, F32),
            pltpu.VMEM((3 * chans, vox), BF16),
            pltpu.VMEM((chans * rows, width), F32),
            pltpu.VMEM((own + 8, vox), F32),
            pltpu.SemaphoreType.DMA((loose,)),
        ]
        + [pltpu.VMEM(sums, F32)] * last
        + [pltpu.VMEM((own, chans, rows, width), BF16)],
        compiler_params=pltpu.CompilerParams(vmem_limit_bytes=VMEM_LIMIT),
        cost_estimate=pl.CostEstimate(
            flops=3000 * own * chans * vox, bytes_accessed=100 * own * chans * vox, transcendentals=0
        ),
    )(meta, weights, *vmem_args, *pieces, *slopes, *xss, *([into] if aliased else []))


def group_size(tiles, frames_here, layers):
    for g in range(1, layers + 1):
        if layers % g == 0 and tiles % g == 0 and g * frames_here >= HALO:
            return g
    return layers


def pick(parts, start):
    doubled = jnp.stack(parts + parts)
    return lax.dynamic_slice_in_dim(doubled, start, len(parts), 0)


def take(value, index, axis):
    return lax.dynamic_index_in_dim(value, index, axis, False)


def sum_over_tiles(value, tiles, g, others):
    if tiles & (tiles - 1):
        return lax.psum(value.astype(BF16), "tile").astype(F32), [], others
    steps = [2**k for k in range(tiles.bit_length() - 1)]
    outer, inner = [k for k in steps if k >= g], [k for k in steps if k < g]
    rounds = [part[i : i + 2] for part in (outer, inner) for i in range(0, len(part), 2)]
    for number, bits in enumerate(rounds):
        if number == len(rounds) - 1:
            value, others = lax.optimization_barrier((value, others))
        masks = bits + [sum(bits)] * (len(bits) - 1)
        sent, arrived = value.astype(BF16), []
        for k in masks:
            pairs = [(a, a ^ k) for a in range(tiles)]
            arrived.append(lax.ppermute(sent, "tile", pairs))
        if number < len(rounds) - 1:
            for piece in arrived:
                value = value + piece.astype(F32)
    return value, arrived, others


def sum_over_reps(value, axis):
    reps = lax.axis_size("rep")
    r = lax.axis_index("rep")
    n = value.shape[axis] // reps

    def share(k):
        return lax.dynamic_slice_in_dim(value, (k % reps) * n, n, axis)

    acc = share(r)
    for s in range(1, reps):
        pairs = [(a, (a + s) % reps) for a in range(reps)]
        acc = acc + lax.ppermute(share(r + s).astype(BF16), "rep", pairs).astype(F32)
    return acc


def body(inputs, w_spatial, w_temporal, w_head, targets, valid):
    _, here, chans, layers, rows, width = inputs.shape
    tiles = lax.axis_size("tile")
    total = here * tiles
    g = group_size(tiles, here, layers)
    per = layers // g
    own = g * here
    vox = rows * width
    t = lax.axis_index("tile")
    q, m = t // g, t % g
    spot = targets.shape[2]
    share = groups = tiles // g
    x = inputs[0]

    def swap(value, s):
        pairs = [(a, a // g * g + (a % g + s) % g) for a in range(tiles)]
        return lax.ppermute(value, "tile", pairs)

    def hop(value, shifts):
        pairs = [(a, a + shifts[a % g] * g) for a in range(tiles)]
        return lax.ppermute(value, "tile", [p for p in pairs if 0 <= p[1] < tiles])

    halved = (w_temporal.astype(F32) * 0.5).astype(BF16)
    wt = halved.transpose(0, 2, 1, 3).reshape(2, chans, 3 * chans)
    wtb = halved.transpose(0, 3, 1, 2).reshape(2, chans, 3 * chans)
    w9 = (w_spatial.astype(F32) * 0.5).astype(BF16).reshape(3, 3, chans, chans)
    wb = w9.transpose(0, 3, 1, 2).reshape(3 * chans, 3 * chans)
    whc = w_head.astype(F32)[:, None]

    mirrored = g == 2 and here <= HALO <= 2 * here
    extra = HALO - here if mirrored else 0
    up, down = own + HALO, HALO - here
    table, slots = [], {}
    for a in range(tiles):
        aq, am = a // g, a % g
        spots = [HALO + (am - s) % g * here for s in range(g)]
        if mirrored:
            for k in range(2):
                spots.append(up if am == k else down)
                if extra:
                    spots.append(0 if am == k else up + here)
        else:
            left, d = HALO, 1
            while left > 0:
                k = min(left, own)
                spots += [left - k, HALO + d * own]
                left -= k
                d += 1
        row = []

        def put(name, *values):
            slots[name] = len(row)
            row.extend(values)

        for layer in range(per):
            put(("temporal", layer), aq * own, *spots, am * per + layer)
        table.append(row)
    meta = lax.dynamic_index_in_dim(jnp.asarray(np.array(table, np.int32)), t, 0, False)

    leaving = [
        [lax.dynamic_slice_in_dim(x, (m + s) % g * per + layer, 1, 2) for s in range(1, g)]
        for layer in range(per)
    ]
    arriving = [[swap(piece, s + 1) for s, piece in enumerate(leaving[0])]]
    def member():
        return lax.rem(lax.axis_index("tile"), g)

    def last_if(k):
        return lambda: jnp.where(member() == k, (here - extra) // max(extra, 1), 0)

    mine = list(run_forward(lambda: member() * per, last_if(0), extra, per, x, w_spatial))
    leaving[1:], mine[1] = lax.optimization_barrier((leaving[1:], mine[1]))
    for pieces in leaving[1:]:
        arriving.append([swap(piece, s + 1) for s, piece in enumerate(pieces)])
    ahead = []
    if mirrored:
        ahead.append(hop(mine[0], (-1, 1)))
        if extra:
            mine[3], arriving[0] = lax.optimization_barrier((mine[3], arriving[0]))
            ahead.append(hop(mine[3], (1, -1)))

    dims = (own, chans, vox, total, g, width)
    grads = jnp.zeros((6, chans, 3 * chans), F32)
    asked, mine[2] = lax.optimization_barrier((targets, mine[2]))
    ready = []
    for layer in range(per):
        done = [mine]
        for piece in arriving[layer]:
            done.append(list(run_forward(lambda: 0, last_if(1), extra, 1, piece, w_spatial)))
        pieces = [d[0] for d in done]
        ranks = [layer] + [0] * (g - 1)
        if mirrored:
            if layer:
                ahead, done[1][0] = lax.optimization_barrier((ahead, done[1][0]))
            pieces += [*ahead, hop(done[1][0], (1, -1))]
            if extra:
                if layer:
                    before = ready[-1][1]
                    before[-1], done[1][3] = lax.optimization_barrier((before[-1], done[1][3]))
                pieces.append(hop(done[1][3], (-1, 1)))
            for k in range(2):
                ranks += [0 if k else layer] * len(ahead)
        else:
            block = [p[k] for p, k in zip(pieces, ranks)]
            block = pick(block[::-1], g - 1 - m).reshape(own, chans, vox)
            left, d = HALO, 1
            while left > 0:
                k = min(left, own)
                pieces.append(hop(block[own - k :], (d,) * g)[None])
                pieces.append(hop(block[:k], (-d,) * g)[None])
                ranks += [0, 0]
                left -= k
                d += 1
        ready.append([layer, pieces, ranks, [d[1] for d in done], [d[2] for d in done]])

    windows = run_windows(asked, tiles, own, g)
    windows = lax.all_to_all(windows, "tile", 0, 0, tiled=True)
    tgt = lax.dynamic_slice_in_dim(windows, m * share, share, 0)
    if share % per:
        tgt = tgt.transpose(1, 0, 2).reshape(own + 8, per, vox).transpose(1, 0, 2)
    frame_weight = jnp.pad(valid[0].astype(F32) / total, (3, 3))
    frame_weight = lax.dynamic_slice_in_dim(frame_weight, q * own, own + 6, 0)


    logits, out, homecoming = [], None, []
    for layer in range(per):
        _, pieces, ranks, slopes, xcs = ready[layer]
        part = share // per if share % per == 0 else 1
        logit, grads, out, sent = run_temporal(
            meta,
            slots["temporal", layer],
            (wt, wtb, whc, tgt[layer * part : (layer + 1) * part], grads, wb),
            frame_weight,
            pieces,
            ranks,
            slopes,
            xcs,
            layer == per - 1,
            out,
            dims,
            layers,
        )
        logits.append(logit[3 : 3 + own, 0])
        if layer < per - 1:
            following = ready[layer + 1]
            following[1], sent = lax.optimization_barrier((following[1], sent))
        homecoming.append([swap(sent[s - 1][:, :, None], -s) for s in range(1, g)])
    homecoming[:-1], grads = lax.optimization_barrier((homecoming[:-1], grads))

    logits = jnp.concatenate(logits, axis=1).astype(BF16).reshape(own, share, spot)
    logits = logits.transpose(1, 0, 2)
    logits = jnp.concatenate([logits] * g)
    logits = lax.all_to_all(logits, "tile", 0, 0, tiled=True)
    grads, arrived, homecoming = sum_over_tiles(sum_over_reps(grads, 1), tiles, g, homecoming)
    for layer in range(per):
        for s in range(1, g):
            place = (m + s) % g * per + layer
            out = lax.dynamic_update_slice_in_dim(out, homecoming[layer][s - 1], place, 2)
    logits, gs, gt, gh = run_finish(grads, arrived, logits, groups, g)
    logits, gh = logits.reshape(1, total, spot), gh[0]
    return logits, out[None], gs, gt, gh


def solution(mesh):
    placed = (
        P("rep", "tile", None, None, None, None),
        P(),
        P(),
        P(),
        P("rep", None, "tile"),
        P("rep", None),
    )
    return jax.shard_map(
        body,
        mesh=mesh,
        in_specs=placed,
        out_specs=(
            P("rep", None, "tile"),
            P("rep", "tile", None, None, None, None),
            P(None, "rep", None),
            P(None, None, "rep", None),
            P("rep"),
        ),
        check_vma=False,
    )
```

```python
import functools

import jax
import jax.numpy as jnp
from jax import lax
from jax.experimental import pallas as pl
from jax.experimental.pallas import tpu as pltpu
from jax.sharding import PartitionSpec as P
import numpy as np

EPS = 1e-06
HALO = 6
F32 = jnp.float32
BF16 = jnp.bfloat16
VMEM_LIMIT = 52 * 1024 * 1024


def sigmoid(u):
    return 0.5 * jnp.tanh(0.5 * u) + 0.5


def silu_parts(half):
    t = jnp.tanh(half)
    a = 1.0 + t
    y = half * a
    return y, a + y * (1.0 - t)


def dot_nn(a, b):
    return jnp.dot(a, b, preferred_element_type=F32)


def dot_nt(a, b):
    return lax.dot_general(a, b, (((1,), (1,)), ((), ())), preferred_element_type=F32)


def channel_sum(v):
    return jnp.sum(v, axis=0, keepdims=True)


def spread(row, dst, r, order):
    chans, width = row.shape
    lane = lax.broadcasted_iota(jnp.int32, (chans, width), 1)
    prev = jnp.where(lane > 0, pltpu.roll(row, 1, 1), 0.0)
    nxt = jnp.where(lane < width - 1, pltpu.roll(row, width - 1, 1), 0.0)
    parts = (prev, row, nxt) if order > 0 else (nxt, row, prev)
    for j in range(3):
        dst[j * chans : (j + 1) * chans, r * width : (r + 1) * width] = parts[j].astype(BF16)


def conv_rows(w_ref, src, sign, rows, chans, width):
    step = 2 * width
    outs = [dot_nn(w_ref[...], src[:, p * step : (p + 1) * step]) for p in range(rows // 2)]

    def piece(i, r):
        half = slice((r % 2) * width, (r % 2 + 1) * width)
        return outs[r // 2][i * chans : (i + 1) * chans, half]

    result = []
    for r in range(rows):
        acc = piece(1, r)
        for i in (-1, 1):
            if 0 <= r + sign * i < rows:
                acc = acc + piece(i + 1, r + sign * i)
        result.append(acc)
    return result


def forward_kernel(middle, block, x_ref, w_ref, feat_ref, slope_ref, xc_ref, *rest):
    xt, xs, wf = rest[-3:]
    frames, chans, _, rows, width = x_ref.shape

    @pl.when((pl.program_id(0) == 0) & (pl.program_id(1) == 0))
    def _():
        for i in range(3):
            for j in range(3):
                wf[i * chans : (i + 1) * chans, j * chans : (j + 1) * chans] = (
                    w_ref[3 * i + j].astype(F32) * 0.5
                ).astype(BF16)

    for n in range(frames):
        xt[n] = x_ref[n, :, 0].astype(F32).reshape(chans * rows, width)
    for n in range(frames):
        for r in range(rows):
            row = xt[n, pl.ds(r, chans, stride=rows), :]
            spread(row, xs.at[n], r, 1)
            xc_ref[0, n, :, r * width : (r + 1) * width] = row.astype(BF16)
    for n in range(frames):
        for r, half in enumerate(conv_rows(wf, xs.at[n], 1, rows, chans, width)):
            cols = slice(r * width, (r + 1) * width)
            y, slope = silu_parts(half)
            feat_ref[0, n, :, cols] = y.astype(BF16)
            slope_ref[0, n, :, cols] = slope.astype(BF16)
    if middle:

        @pl.when(pl.program_id(1) == block())
        def _():
            rest[0][0] = feat_ref[0]


def run_forward(first, block, middle, count, x, w_spatial):
    n, chans, _, rows, width = x.shape
    vox = rows * width
    sds = jax.ShapeDtypeStruct
    frames = middle if middle and n % middle == 0 else 2 - n % 2
    shapes = [sds((count, n, chans, vox), BF16)] * 3
    specs = [pl.BlockSpec((1, frames, chans, vox), lambda k, f: (k, f, 0, 0))] * 3
    if middle:
        shapes.append(sds((count, middle, chans, vox), BF16))
        specs.append(pl.BlockSpec((1, middle, chans, vox), lambda k, f: (k, 0, 0, 0)))
    return pl.pallas_call(
        functools.partial(forward_kernel, middle, block),
        name="conv_forward",
        out_shape=shapes,
        grid_spec=pl.GridSpec(
            grid=(count, n // frames),
            in_specs=[
                pl.BlockSpec(
                    (frames, chans, 1, rows, width),
                    lambda k, f: (f, 0, first() + k, 0, 0),
                ),
                pl.BlockSpec((9, chans, chans), lambda k, f: (0, 0, 0)),
            ],
            out_specs=specs,
            scratch_shapes=[
                pltpu.VMEM((frames, chans * rows, width), F32),
                pltpu.VMEM((frames, 3 * chans, vox), BF16),
                pltpu.VMEM((3 * chans, 3 * chans), BF16),
            ],
        ),
        cost_estimate=pl.CostEstimate(flops=1000, bytes_accessed=1000, transcendentals=0),
    )(x, w_spatial)


def window_kernel(own, g, tgt_ref, win_ref, pad):
    total, spot = tgt_ref.shape[1:]
    pad[0:8] = jnp.zeros((8, spot), F32)
    pad[8 : 8 + total] = tgt_ref[0].astype(F32)
    pad[8 + total :] = jnp.zeros((8, spot), F32)
    for a in range(win_ref.shape[0]):
        first = a // g * own + 4
        win_ref[a] = pad[first : first + own + 8].astype(BF16)


def run_windows(targets, tiles, own, g):
    _, total, spot = targets.shape
    vmem = pl.BlockSpec(memory_space=pltpu.VMEM)
    return pl.pallas_call(
        functools.partial(window_kernel, own, g),
        name="windows",
        out_shape=jax.ShapeDtypeStruct((tiles, own + 8, spot), BF16),
        in_specs=[vmem],
        out_specs=vmem,
        scratch_shapes=[pltpu.VMEM((total + 16, spot), F32)],
        compiler_params=pltpu.CompilerParams(vmem_limit_bytes=4 * 1024 * 1024),
        cost_estimate=pl.CostEstimate(flops=1000, bytes_accessed=1000, transcendentals=0),
    )(targets)


def finish_kernel(arrived, g, value_ref, *rest):
    logit_ref, out_ref, gs_ref, gt_ref, gh_ref = rest[arrived:]
    part, chans = value_ref.shape[1:]
    groups = out_ref.shape[0]
    member = lax.axis_index("tile") // groups
    for q in range(groups):
        out_ref[q] = logit_ref[q * g + member]

    def total(k):
        acc = value_ref[k]
        for ref in rest[:arrived]:
            acc = acc + ref[k].astype(F32)
        return acc

    for k in range(9):
        gs_ref[k] = total(k)
    for k in range(6):
        gt_ref[k // 3, k % 3] = total(9 + k)
    shape = (chans, part)
    mine = lax.broadcasted_iota(jnp.int32, shape, 1) + lax.axis_index("rep") * part
    chosen = jnp.where(lax.broadcasted_iota(jnp.int32, shape, 0) == mine, 1.0, 0.0)
    picked = jnp.dot(total(15), chosen, precision=lax.Precision.HIGHEST, preferred_element_type=F32)
    gh_ref[...] = picked[0:1]


def run_finish(value, arrived, logits, groups, g):
    _, part, chans = value.shape
    _, own, spot = logits.shape
    sds = jax.ShapeDtypeStruct
    vmem = pl.BlockSpec(memory_space=pltpu.VMEM)
    return pl.pallas_call(
        functools.partial(finish_kernel, len(arrived), g),
        name="finish",
        out_shape=(
            sds((groups, own, spot), BF16),
            sds((9, part, chans), F32),
            sds((2, 3, part, chans), F32),
            sds((1, part), F32),
        ),
        in_specs=[vmem] * (2 + len(arrived)),
        out_specs=[vmem] * 4,
        compiler_params=pltpu.CompilerParams(vmem_limit_bytes=4 * 1024 * 1024),
        cost_estimate=pl.CostEstimate(flops=1000, bytes_accessed=1000, transcendentals=0),
    )(value, *arrived, logits)


def temporal_kernel(
    places,
    last,
    aliased,
    base,
    dims,
    meta_ref,
    weight_ref,
    wt_ref,
    wtb_ref,
    whc_ref,
    tgt_ref,
    init_ref,
    wb_ref,
    *rest,
):
    own, chans, vox, total, members, width = dims
    rows = vox // width
    here = own // members
    counts = len(places)
    pieces = [ref.at[k] for ref, k in zip(rest[:counts], places)]
    slope_in = [ref.at[k] for ref, k in zip(rest[counts : counts + members], places)]
    xs_in = [ref.at[k] for ref, k in zip(rest[counts + members : counts + 2 * members], places)]
    rest = rest[counts + 2 * members + aliased :]
    logit_ref, grad_ref = rest[:2]
    out_ref, send_ref, back = rest[2:4] + rest[-1:]
    taps = grad_ref
    if last:
        grad_ref = rest[-2]
    (
        feats,
        slope,
        xs,
        n0,
        inv0,
        h1,
        n1,
        inv1,
        sp0,
        dh2,
        dm1,
        dm0,
        final_ref,
        dlog,
        ds,
        xt,
        tgt,
        sems,
    ) = rest[4:22]
    step = min(256, vox)
    lo, hi = HALO, HALO + own
    first = meta_ref[base]
    chunks = [slice(p * step, (p + 1) * step) for p in range(vox // step)]
    whole = slice(0, vox)

    early = [
        pltpu.make_async_copy(src, feats.at[pl.ds(meta_ref[base + 1 + k], src.shape[0])], sems.at[k])
        for k, src in enumerate(pieces)
    ]
    late = []
    for k in range(members):
        spot = pl.ds(meta_ref[base + 1 + k] - HALO, here)
        late.append(pltpu.make_async_copy(slope_in[k], slope.at[spot], sems.at[len(early) + k]))
        late.append(
            pltpu.make_async_copy(xs_in[k], xs.at[spot], sems.at[len(early) + members + k])
        )
    for copy in early:
        copy.start()
    for c in range(tgt_ref.shape[0]):
        tgt[:, c * tgt_ref.shape[2] : (c + 1) * tgt_ref.shape[2]] = tgt_ref[c].astype(F32)
    for copy in early:
        copy.wait()
    for copy in late:
        copy.start()

    def frame_ok(f):
        g = first + f - HALO
        return jnp.where((g >= 0) & (g < total), 1.0, 0.0).astype(F32)

    def loop(a, b, *fns):
        def every(f, carry):
            for fn in fns:
                fn(f)
            return carry

        lax.fori_loop(a, b, every, 0)

    def stack(ref, f0, f1, f2, cols):
        return jnp.concatenate([ref[f0, :, cols], ref[f1, :, cols], ref[f2, :, cols]], axis=0)

    def rms(hid):
        return lax.rsqrt(channel_sum(hid * hid) * (1.0 / chans) + EPS)

    def norm0(f):
        for cols in chunks:
            hid = feats[f, :, cols].astype(F32)
            inv = rms(hid)
            n0[f, :, cols] = (hid * inv).astype(BF16)
            inv0[f, :, cols] = inv

    def layer0(f):
        ok = frame_ok(f)
        for cols in chunks:
            y, slope2 = silu_parts(dot_nn(wt_ref[0], stack(n0, f - 1, f, f + 1, cols)))
            hid = feats[f, :, cols].astype(F32) + y
            inv = rms(hid) * ok
            h1[f, :, cols] = hid
            n1[f, :, cols] = (hid * inv).astype(BF16)
            inv1[f, :, cols] = inv
            sp0[f, :, cols] = slope2

    def layer1(f):
        weight = weight_ref[f - 3]
        for cols in chunks:
            y, slope2 = silu_parts(dot_nn(wt_ref[1], stack(n1, f - 2, f, f + 2, cols)))
            hid = h1[f, :, cols] + y
            inv = rms(hid)
            unit = hid * inv
            logit = channel_sum(unit * whc_ref[...])
            logit_ref[f - 3, :, cols] = logit
            dlogit = weight * (sigmoid(logit) - tgt[pl.ds(f - 2, 1), cols])
            final_ref[f, :, cols] = unit.astype(BF16)
            dlog[f, :, cols] = dlogit
            dhid = (inv * dlogit) * (whc_ref[...] - unit * (logit * (1.0 / chans)))
            dh2[f, :, cols] = dhid
            dm1[f, :, cols] = (dhid * slope2).astype(BF16)

    def back1(f):
        for cols in chunks:
            dnorm = dot_nn(wtb_ref[1], stack(dm1, f + 2, f, f - 2, cols))
            unit = n1[f, :, cols].astype(F32)
            mean = channel_sum(dnorm * unit) * (1.0 / chans)
            dhid = dh2[f, :, cols] + inv1[f, :, cols] * (dnorm - unit * mean)
            dh2[f, :, cols] = dhid
            dm0[f, :, cols] = (dhid * sp0[f, :, cols]).astype(BF16)

    def back0(f):
        b = f - HALO
        for cols in chunks:
            dnorm = dot_nn(wtb_ref[0], stack(dm0, f + 1, f, f - 1, cols))
            unit = n0[f, :, cols].astype(F32)
            mean = channel_sum(dnorm * unit) * (1.0 / chans)
            dhid = dh2[f, :, cols] + inv0[f, :, cols] * (dnorm - unit * mean)
            dpre = dhid * slope[b, :, cols].astype(F32)
            for r in range(step // width):
                spread(dpre[:, r * width : (r + 1) * width], ds, cols.start // width + r, -1)
        center = xs[b]
        blank = jnp.zeros((chans, width), BF16)
        taller = jnp.concatenate([center[:, width:], blank], axis=1)
        lower = jnp.concatenate([blank, center[:, :-width]], axis=1)
        grad = dot_nt(ds[...], jnp.concatenate([lower, center, taller], axis=0))
        for j in range(3):
            grad_ref[j] += grad[j * chans : (j + 1) * chans]
        grad_ref[3] += dot_nt(dm0[f], stack(n0, f - 1, f, f + 1, whole))
        grad_ref[4] += dot_nt(dm1[f], stack(n1, f - 2, f, f + 2, whole))
        head = jnp.broadcast_to(dlog[f].astype(BF16), (chans, vox))
        grad_ref[5, :, :chans] += dot_nt(head, final_ref[f])
        for r, row in enumerate(conv_rows(wb_ref, ds, -1, rows, chans, width)):
            xt[pl.ds(r, chans, stride=rows), :] = row
        back[b] = xt[...].astype(BF16).reshape(chans, rows, width)

    grad_ref[...] = init_ref[...]
    stages = [
        (back0, 5, lo, hi),
        (back1, 3, lo - 1, hi + 1),
        (layer1, 0, 3, hi + 3),
        (layer0, -3, 1, hi + HALO - 1),
        (norm0, -5, 0, hi + HALO),
    ]
    cuts = sorted({a + d for _, d, a, _ in stages} | {b + d for _, d, _, b in stages})
    for a, b in zip(cuts, cuts[1:]):
        active = [(fn, d) for fn, d, p, n in stages if p + d <= a and b <= n + d]
        if a == lo + 5:
            for copy in late:
                copy.wait()
        loop(0, b - a, *[lambda i, fn=fn, f=a - d: fn(i + f) for fn, d in active])
    layer = meta_ref[base + 1 + counts]
    leaving = []
    for k in range(members):
        src = back.at[pl.ds(meta_ref[base + 1 + k] - HALO, here)]
        dst = send_ref.at[k - 1] if k else out_ref.at[:, :, layer]
        leaving.append(pltpu.make_async_copy(src, dst, sems.at[k]))
    for copy in leaving:
        copy.start()
    if last:
        for k in range(3):
            cols = slice(k * chans, (k + 1) * chans)
            for j in range(3):
                taps[3 * k + j] = grad_ref[j, :, cols] * 0.5
            for l in range(2):
                taps[9 + 3 * l + k] = grad_ref[3 + l, :, cols] * 0.5
        taps[15] = grad_ref[5, :, :chans]
    for copy in leaving:
        copy.wait()


def run_temporal(meta, base, vmem_args, weights, pieces, places, slopes, xss, last, into, dims, layers):
    own, chans, vox, total, members, width = dims
    rows, here = vox // width, own // members
    every = own + 2 * HALO
    sds = jax.ShapeDtypeStruct
    smem = pl.BlockSpec(memory_space=pltpu.SMEM)
    vmem = pl.BlockSpec(memory_space=pltpu.VMEM)
    hbm = pl.BlockSpec(memory_space=pl.ANY)
    loose = len(pieces) + 2 * members
    aliased = into is not None
    frame = lambda n, c, dt: pltpu.VMEM((n, c, vox), dt)
    sums = (6, chans, 3 * chans)
    shapes = [
        sds((own + 6, 1, vox), F32),
        sds((16, chans, chans) if last else sums, F32),
        sds((here, chans, layers, rows, width), BF16),
        sds((members - 1, here, chans, rows, width), BF16),
    ]
    specs = [vmem, vmem, hbm, hbm]
    return pl.pallas_call(
        functools.partial(temporal_kernel, tuple(places), last, aliased, base, dims),
        name="temporal",
        out_shape=shapes,
        in_specs=[smem, smem] + [vmem] * len(vmem_args) + [hbm] * (loose + aliased),
        out_specs=specs,
        input_output_aliases={2 + len(vmem_args) + loose: 2} if aliased else {},
        scratch_shapes=[
            frame(every, chans, BF16),
            frame(own, chans, BF16),
            frame(own, chans, BF16),
            frame(every, chans, BF16),
            frame(every, 1, F32),
            frame(every, chans, F32),
            frame(every, chans, BF16),
            frame(every, 1, F32),
            frame(every, chans, F32),
            frame(every, chans, F32),
            frame(every, chans, BF16),
            frame(every, chans, BF16),
            frame(every, chans, BF16),
            frame(every, 1, F32),
            pltpu.VMEM((3 * chans, vox), BF16),
            pltpu.VMEM((chans * rows, width), F32),
            pltpu.VMEM((own + 8, vox), F32),
            pltpu.SemaphoreType.DMA((loose,)),
        ]
        + [pltpu.VMEM(sums, F32)] * last
        + [pltpu.VMEM((own, chans, rows, width), BF16)],
        compiler_params=pltpu.CompilerParams(vmem_limit_bytes=VMEM_LIMIT),
        cost_estimate=pl.CostEstimate(
            flops=3000 * own * chans * vox, bytes_accessed=100 * own * chans * vox, transcendentals=0
        ),
    )(meta, weights, *vmem_args, *pieces, *slopes, *xss, *([into] if aliased else []))


def group_size(tiles, frames_here, layers):
    for g in range(1, layers + 1):
        if layers % g == 0 and tiles % g == 0 and g * frames_here >= HALO:
            return g
    return layers


def pick(parts, start):
    doubled = jnp.stack(parts + parts)
    return lax.dynamic_slice_in_dim(doubled, start, len(parts), 0)


def take(value, index, axis):
    return lax.dynamic_index_in_dim(value, index, axis, False)


def sum_over_tiles(value, tiles, g, others):
    if tiles & (tiles - 1):
        return lax.psum(value.astype(BF16), "tile").astype(F32), [], others
    steps = [2**k for k in range(tiles.bit_length() - 1)]
    outer, inner = [k for k in steps if k >= g], [k for k in steps if k < g]
    rounds = [part[i : i + 2] for part in (outer, inner) for i in range(0, len(part), 2)]
    for number, bits in enumerate(rounds):
        if number == len(rounds) - 1:
            value, others = lax.optimization_barrier((value, others))
        masks = bits + [sum(bits)] * (len(bits) - 1)
        sent, arrived = value.astype(BF16), []
        for k in masks:
            pairs = [(a, a ^ k) for a in range(tiles)]
            arrived.append(lax.ppermute(sent, "tile", pairs))
        if number < len(rounds) - 1:
            for piece in arrived:
                value = value + piece.astype(F32)
    return value, arrived, others


def sum_over_reps(value, axis):
    reps = lax.axis_size("rep")
    r = lax.axis_index("rep")
    n = value.shape[axis] // reps

    def share(k):
        return lax.dynamic_slice_in_dim(value, (k % reps) * n, n, axis)

    acc = share(r)
    for s in range(1, reps):
        pairs = [(a, (a + s) % reps) for a in range(reps)]
        acc = acc + lax.ppermute(share(r + s).astype(BF16), "rep", pairs).astype(F32)
    return acc


def body(inputs, w_spatial, w_temporal, w_head, targets, valid):
    _, here, chans, layers, rows, width = inputs.shape
    tiles = lax.axis_size("tile")
    total = here * tiles
    g = group_size(tiles, here, layers)
    per = layers // g
    own = g * here
    vox = rows * width
    t = lax.axis_index("tile")
    q, m = t // g, t % g
    spot = targets.shape[2]
    share = groups = tiles // g
    x = inputs[0]

    def swap(value, s):
        pairs = [(a, a // g * g + (a % g + s) % g) for a in range(tiles)]
        return lax.ppermute(value, "tile", pairs)

    def hop(value, shifts):
        pairs = [(a, a + shifts[a % g] * g) for a in range(tiles)]
        return lax.ppermute(value, "tile", [p for p in pairs if 0 <= p[1] < tiles])

    halved = (w_temporal.astype(F32) * 0.5).astype(BF16)
    wt = halved.transpose(0, 2, 1, 3).reshape(2, chans, 3 * chans)
    wtb = halved.transpose(0, 3, 1, 2).reshape(2, chans, 3 * chans)
    w9 = (w_spatial.astype(F32) * 0.5).astype(BF16).reshape(3, 3, chans, chans)
    wb = w9.transpose(0, 3, 1, 2).reshape(3 * chans, 3 * chans)
    whc = w_head.astype(F32)[:, None]

    mirrored = g == 2 and here <= HALO <= 2 * here
    extra = HALO - here if mirrored else 0
    up, down = own + HALO, HALO - here
    table, slots = [], {}
    for a in range(tiles):
        aq, am = a // g, a % g
        spots = [HALO + (am - s) % g * here for s in range(g)]
        if mirrored:
            for k in range(2):
                spots.append(up if am == k else down)
                if extra:
                    spots.append(0 if am == k else up + here)
        else:
            left, d = HALO, 1
            while left > 0:
                k = min(left, own)
                spots += [left - k, HALO + d * own]
                left -= k
                d += 1
        row = []

        def put(name, *values):
            slots[name] = len(row)
            row.extend(values)

        for layer in range(per):
            put(("temporal", layer), aq * own, *spots, am * per + layer)
        table.append(row)
    meta = lax.dynamic_index_in_dim(jnp.asarray(np.array(table, np.int32)), t, 0, False)

    leaving = [
        [lax.dynamic_slice_in_dim(x, (m + s) % g * per + layer, 1, 2) for s in range(1, g)]
        for layer in range(per)
    ]
    arriving = [[swap(piece, s + 1) for s, piece in enumerate(leaving[0])]]
    def member():
        return lax.rem(lax.axis_index("tile"), g)

    def last_if(k):
        return lambda: jnp.where(member() == k, (here - extra) // max(extra, 1), 0)

    mine = list(run_forward(lambda: member() * per, last_if(0), extra, per, x, w_spatial))
    leaving[1:], mine[1] = lax.optimization_barrier((leaving[1:], mine[1]))
    for pieces in leaving[1:]:
        arriving.append([swap(piece, s + 1) for s, piece in enumerate(pieces)])
    ahead = []
    if mirrored:
        ahead.append(hop(mine[0], (-1, 1)))
        if extra:
            mine[3], arriving[0] = lax.optimization_barrier((mine[3], arriving[0]))
            ahead.append(hop(mine[3], (1, -1)))

    dims = (own, chans, vox, total, g, width)
    grads = jnp.zeros((6, chans, 3 * chans), F32)
    asked, mine[2] = lax.optimization_barrier((targets, mine[2]))
    ready = []
    for layer in range(per):
        done = [mine]
        for piece in arriving[layer]:
            done.append(list(run_forward(lambda: 0, last_if(1), extra, 1, piece, w_spatial)))
        pieces = [d[0] for d in done]
        ranks = [layer] + [0] * (g - 1)
        if mirrored:
            if layer:
                ahead, done[1][0] = lax.optimization_barrier((ahead, done[1][0]))
            pieces += [*ahead, hop(done[1][0], (1, -1))]
            if extra:
                if layer:
                    before = ready[-1][1]
                    before[-1], done[1][3] = lax.optimization_barrier((before[-1], done[1][3]))
                pieces.append(hop(done[1][3], (-1, 1)))
            for k in range(2):
                ranks += [0 if k else layer] * len(ahead)
        else:
            block = [p[k] for p, k in zip(pieces, ranks)]
            block = pick(block[::-1], g - 1 - m).reshape(own, chans, vox)
            left, d = HALO, 1
            while left > 0:
                k = min(left, own)
                pieces.append(hop(block[own - k :], (d,) * g)[None])
                pieces.append(hop(block[:k], (-d,) * g)[None])
                ranks += [0, 0]
                left -= k
                d += 1
        ready.append([layer, pieces, ranks, [d[1] for d in done], [d[2] for d in done]])

    windows = run_windows(asked, tiles, own, g)
    windows = lax.all_to_all(windows, "tile", 0, 0, tiled=True)
    tgt = lax.dynamic_slice_in_dim(windows, m * share, share, 0)
    if share % per:
        tgt = tgt.transpose(1, 0, 2).reshape(own + 8, per, vox).transpose(1, 0, 2)
    frame_weight = jnp.pad(valid[0].astype(F32) / total, (3, 3))
    frame_weight = lax.dynamic_slice_in_dim(frame_weight, q * own, own + 6, 0)


    logits, out, homecoming = [], None, []
    for layer in range(per):
        _, pieces, ranks, slopes, xcs = ready[layer]
        part = share // per if share % per == 0 else 1
        logit, grads, out, sent = run_temporal(
            meta,
            slots["temporal", layer],
            (wt, wtb, whc, tgt[layer * part : (layer + 1) * part], grads, wb),
            frame_weight,
            pieces,
            ranks,
            slopes,
            xcs,
            layer == per - 1,
            out,
            dims,
            layers,
        )
        logits.append(logit[3 : 3 + own, 0])
        if layer < per - 1:
            following = ready[layer + 1]
            following[1], sent = lax.optimization_barrier((following[1], sent))
        homecoming.append([swap(sent[s - 1][:, :, None], -s) for s in range(1, g)])
    homecoming[:-1], grads = lax.optimization_barrier((homecoming[:-1], grads))

    logits = jnp.concatenate(logits, axis=1).astype(BF16).reshape(own, share, spot)
    logits = logits.transpose(1, 0, 2)
    logits = jnp.concatenate([logits] * g)
    logits = lax.all_to_all(logits, "tile", 0, 0, tiled=True)
    grads, arrived, homecoming = sum_over_tiles(sum_over_reps(grads, 1), tiles, g, homecoming)
    for layer in range(per):
        for s in range(1, g):
            place = (m + s) % g * per + layer
            out = lax.dynamic_update_slice_in_dim(out, homecoming[layer][s - 1], place, 2)
    logits, gs, gt, gh = run_finish(grads, arrived, logits, groups, g)
    logits, gh = logits.reshape(1, total, spot), gh[0]
    return logits, out[None], gs, gt, gh


def solution(mesh):
    placed = (
        P("rep", "tile", None, None, None, None),
        P(),
        P(),
        P(),
        P("rep", None, "tile"),
        P("rep", None),
    )
    return jax.shard_map(
        body,
        mesh=mesh,
        in_specs=placed,
        out_specs=(
            P("rep", None, "tile"),
            P("rep", "tile", None, None, None, None),
            P(None, "rep", None),
            P(None, None, "rep", None),
            P("rep"),
        ),
        check_vma=False,
    )
```

```python
import functools

import jax
import jax.numpy as jnp
from jax import lax
from jax.experimental import pallas as pl
from jax.experimental.pallas import tpu as pltpu
from jax.sharding import PartitionSpec as P
import numpy as np

EPS = 1e-06
HALO = 6
F32 = jnp.float32
BF16 = jnp.bfloat16
VMEM_LIMIT = 52 * 1024 * 1024


def sigmoid(u):
    return 0.5 * jnp.tanh(0.5 * u) + 0.5


def silu_parts(half):
    t = jnp.tanh(half)
    a = 1.0 + t
    y = half * a
    return y, a + y * (1.0 - t)


def dot_nn(a, b):
    return jnp.dot(a, b, preferred_element_type=F32)


def dot_nt(a, b):
    return lax.dot_general(a, b, (((1,), (1,)), ((), ())), preferred_element_type=F32)


def channel_sum(v):
    return jnp.sum(v, axis=0, keepdims=True)


def spread(row, dst, r, order):
    chans, width = row.shape
    lane = lax.broadcasted_iota(jnp.int32, (chans, width), 1)
    prev = jnp.where(lane > 0, pltpu.roll(row, 1, 1), 0.0)
    nxt = jnp.where(lane < width - 1, pltpu.roll(row, width - 1, 1), 0.0)
    parts = (prev, row, nxt) if order > 0 else (nxt, row, prev)
    for j in range(3):
        dst[j * chans : (j + 1) * chans, r * width : (r + 1) * width] = parts[j].astype(BF16)


def conv_rows(w_ref, src, sign, rows, chans, width):
    step = 2 * width
    outs = [dot_nn(w_ref[...], src[:, p * step : (p + 1) * step]) for p in range(rows // 2)]

    def piece(i, r):
        half = slice((r % 2) * width, (r % 2 + 1) * width)
        return outs[r // 2][i * chans : (i + 1) * chans, half]

    result = []
    for r in range(rows):
        acc = piece(1, r)
        for i in (-1, 1):
            if 0 <= r + sign * i < rows:
                acc = acc + piece(i + 1, r + sign * i)
        result.append(acc)
    return result


def forward_kernel(middle, block, x_ref, w_ref, feat_ref, slope_ref, xc_ref, *rest):
    xt, xs, wf = rest[-3:]
    frames, chans, _, rows, width = x_ref.shape

    @pl.when((pl.program_id(0) == 0) & (pl.program_id(1) == 0))
    def _():
        for i in range(3):
            for j in range(3):
                wf[i * chans : (i + 1) * chans, j * chans : (j + 1) * chans] = (
                    w_ref[3 * i + j].astype(F32) * 0.5
                ).astype(BF16)

    for n in range(frames):
        xt[n] = x_ref[n, :, 0].astype(F32).reshape(chans * rows, width)
    for n in range(frames):
        for r in range(rows):
            row = xt[n, pl.ds(r, chans, stride=rows), :]
            spread(row, xs.at[n], r, 1)
            xc_ref[0, n, :, r * width : (r + 1) * width] = row.astype(BF16)
    for n in range(frames):
        for r, half in enumerate(conv_rows(wf, xs.at[n], 1, rows, chans, width)):
            cols = slice(r * width, (r + 1) * width)
            y, slope = silu_parts(half)
            feat_ref[0, n, :, cols] = y.astype(BF16)
            slope_ref[0, n, :, cols] = slope.astype(BF16)
    if middle:

        @pl.when(pl.program_id(1) == block())
        def _():
            rest[0][0] = feat_ref[0]


def run_forward(first, block, middle, count, x, w_spatial):
    n, chans, _, rows, width = x.shape
    vox = rows * width
    sds = jax.ShapeDtypeStruct
    frames = middle if middle and n % middle == 0 else 2 - n % 2
    shapes = [sds((count, n, chans, vox), BF16)] * 3
    specs = [pl.BlockSpec((1, frames, chans, vox), lambda k, f: (k, f, 0, 0))] * 3
    if middle:
        shapes.append(sds((count, middle, chans, vox), BF16))
        specs.append(pl.BlockSpec((1, middle, chans, vox), lambda k, f: (k, 0, 0, 0)))
    return pl.pallas_call(
        functools.partial(forward_kernel, middle, block),
        name="conv_forward",
        out_shape=shapes,
        grid_spec=pl.GridSpec(
            grid=(count, n // frames),
            in_specs=[
                pl.BlockSpec(
                    (frames, chans, 1, rows, width),
                    lambda k, f: (f, 0, first() + k, 0, 0),
                ),
                pl.BlockSpec((9, chans, chans), lambda k, f: (0, 0, 0)),
            ],
            out_specs=specs,
            scratch_shapes=[
                pltpu.VMEM((frames, chans * rows, width), F32),
                pltpu.VMEM((frames, 3 * chans, vox), BF16),
                pltpu.VMEM((3 * chans, 3 * chans), BF16),
            ],
        ),
        cost_estimate=pl.CostEstimate(flops=1000, bytes_accessed=1000, transcendentals=0),
    )(x, w_spatial)


def window_kernel(own, g, tgt_ref, win_ref, pad):
    total, spot = tgt_ref.shape[1:]
    pad[0:8] = jnp.zeros((8, spot), F32)
    pad[8 : 8 + total] = tgt_ref[0].astype(F32)
    pad[8 + total :] = jnp.zeros((8, spot), F32)
    for a in range(win_ref.shape[0]):
        first = a // g * own + 4
        win_ref[a] = pad[first : first + own + 8].astype(BF16)


def run_windows(targets, tiles, own, g):
    _, total, spot = targets.shape
    vmem = pl.BlockSpec(memory_space=pltpu.VMEM)
    return pl.pallas_call(
        functools.partial(window_kernel, own, g),
        name="windows",
        out_shape=jax.ShapeDtypeStruct((tiles, own + 8, spot), BF16),
        in_specs=[vmem],
        out_specs=vmem,
        scratch_shapes=[pltpu.VMEM((total + 16, spot), F32)],
        compiler_params=pltpu.CompilerParams(vmem_limit_bytes=4 * 1024 * 1024),
        cost_estimate=pl.CostEstimate(flops=1000, bytes_accessed=1000, transcendentals=0),
    )(targets)


def finish_kernel(arrived, g, value_ref, *rest):
    logit_ref, out_ref, gs_ref, gt_ref, gh_ref = rest[arrived:]
    part, chans = value_ref.shape[1:]
    groups = out_ref.shape[0]
    member = lax.axis_index("tile") // groups
    for q in range(groups):
        out_ref[q] = logit_ref[q * g + member]

    def total(k):
        acc = value_ref[k]
        for ref in rest[:arrived]:
            acc = acc + ref[k].astype(F32)
        return acc

    for k in range(9):
        gs_ref[k] = total(k)
    for k in range(6):
        gt_ref[k // 3, k % 3] = total(9 + k)
    shape = (chans, part)
    mine = lax.broadcasted_iota(jnp.int32, shape, 1) + lax.axis_index("rep") * part
    chosen = jnp.where(lax.broadcasted_iota(jnp.int32, shape, 0) == mine, 1.0, 0.0)
    picked = jnp.dot(total(15), chosen, precision=lax.Precision.HIGHEST, preferred_element_type=F32)
    gh_ref[...] = picked[0:1]


def run_finish(value, arrived, logits, groups, g):
    _, part, chans = value.shape
    _, own, spot = logits.shape
    sds = jax.ShapeDtypeStruct
    vmem = pl.BlockSpec(memory_space=pltpu.VMEM)
    return pl.pallas_call(
        functools.partial(finish_kernel, len(arrived), g),
        name="finish",
        out_shape=(
            sds((groups, own, spot), BF16),
            sds((9, part, chans), F32),
            sds((2, 3, part, chans), F32),
            sds((1, part), F32),
        ),
        in_specs=[vmem] * (2 + len(arrived)),
        out_specs=[vmem] * 4,
        compiler_params=pltpu.CompilerParams(vmem_limit_bytes=4 * 1024 * 1024),
        cost_estimate=pl.CostEstimate(flops=1000, bytes_accessed=1000, transcendentals=0),
    )(value, *arrived, logits)


def temporal_kernel(
    places,
    last,
    aliased,
    base,
    dims,
    meta_ref,
    weight_ref,
    wt_ref,
    wtb_ref,
    whc_ref,
    tgt_ref,
    init_ref,
    wb_ref,
    *rest,
):
    own, chans, vox, total, members, width = dims
    rows = vox // width
    here = own // members
    counts = len(places)
    pieces = [ref.at[k] for ref, k in zip(rest[:counts], places)]
    slope_in = [ref.at[k] for ref, k in zip(rest[counts : counts + members], places)]
    xs_in = [ref.at[k] for ref, k in zip(rest[counts + members : counts + 2 * members], places)]
    rest = rest[counts + 2 * members + aliased :]
    logit_ref, grad_ref = rest[:2]
    out_ref, send_ref, back = rest[2:4] + rest[-1:]
    taps = grad_ref
    if last:
        grad_ref = rest[-2]
    (
        feats,
        slope,
        xs,
        n0,
        inv0,
        h1,
        n1,
        inv1,
        sp0,
        dh2,
        dm1,
        dm0,
        final_ref,
        dlog,
        ds,
        xt,
        tgt,
        sems,
    ) = rest[4:22]
    step = min(512, vox)
    lo, hi = HALO, HALO + own
    first = meta_ref[base]
    chunks = [slice(p * step, (p + 1) * step) for p in range(vox // step)]
    whole = slice(0, vox)

    early = [
        pltpu.make_async_copy(src, feats.at[pl.ds(meta_ref[base + 1 + k], src.shape[0])], sems.at[k])
        for k, src in enumerate(pieces)
    ]
    late = []
    for k in range(members):
        spot = pl.ds(meta_ref[base + 1 + k] - HALO, here)
        late.append(pltpu.make_async_copy(slope_in[k], slope.at[spot], sems.at[len(early) + k]))
        late.append(
            pltpu.make_async_copy(xs_in[k], xs.at[spot], sems.at[len(early) + members + k])
        )
    for copy in early:
        copy.start()
    for c in range(tgt_ref.shape[0]):
        tgt[:, c * tgt_ref.shape[2] : (c + 1) * tgt_ref.shape[2]] = tgt_ref[c].astype(F32)
    for copy in early:
        copy.wait()
    for copy in late:
        copy.start()

    def frame_ok(f):
        g = first + f - HALO
        return jnp.where((g >= 0) & (g < total), 1.0, 0.0).astype(F32)

    def loop(a, b, *fns):
        def every(f, carry):
            for fn in fns:
                fn(f)
            return carry

        lax.fori_loop(a, b, every, 0)

    def stack(ref, f0, f1, f2, cols):
        return jnp.concatenate([ref[f0, :, cols], ref[f1, :, cols], ref[f2, :, cols]], axis=0)

    def rms(hid):
        return lax.rsqrt(channel_sum(hid * hid) * (1.0 / chans) + EPS)

    def norm0(f):
        for cols in chunks:
            hid = feats[f, :, cols].astype(F32)
            inv = rms(hid)
            n0[f, :, cols] = (hid * inv).astype(BF16)
            inv0[f, :, cols] = inv

    def layer0(f):
        ok = frame_ok(f)
        for cols in chunks:
            y, slope2 = silu_parts(dot_nn(wt_ref[0], stack(n0, f - 1, f, f + 1, cols)))
            hid = feats[f, :, cols].astype(F32) + y
            inv = rms(hid) * ok
            h1[f, :, cols] = hid
            n1[f, :, cols] = (hid * inv).astype(BF16)
            inv1[f, :, cols] = inv
            sp0[f, :, cols] = slope2

    def layer1(f):
        weight = weight_ref[f - 3]
        for cols in chunks:
            y, slope2 = silu_parts(dot_nn(wt_ref[1], stack(n1, f - 2, f, f + 2, cols)))
            hid = h1[f, :, cols] + y
            inv = rms(hid)
            unit = hid * inv
            logit = channel_sum(unit * whc_ref[...])
            logit_ref[f - 3, :, cols] = logit
            dlogit = weight * (sigmoid(logit) - tgt[pl.ds(f - 2, 1), cols])
            final_ref[f, :, cols] = unit.astype(BF16)
            dlog[f, :, cols] = dlogit
            dhid = (inv * dlogit) * (whc_ref[...] - unit * (logit * (1.0 / chans)))
            dh2[f, :, cols] = dhid
            dm1[f, :, cols] = (dhid * slope2).astype(BF16)

    def back1(f):
        for cols in chunks:
            dnorm = dot_nn(wtb_ref[1], stack(dm1, f + 2, f, f - 2, cols))
            unit = n1[f, :, cols].astype(F32)
            mean = channel_sum(dnorm * unit) * (1.0 / chans)
            dhid = dh2[f, :, cols] + inv1[f, :, cols] * (dnorm - unit * mean)
            dh2[f, :, cols] = dhid
            dm0[f, :, cols] = (dhid * sp0[f, :, cols]).astype(BF16)

    def back0(f):
        b = f - HALO
        for cols in chunks:
            dnorm = dot_nn(wtb_ref[0], stack(dm0, f + 1, f, f - 1, cols))
            unit = n0[f, :, cols].astype(F32)
            mean = channel_sum(dnorm * unit) * (1.0 / chans)
            dhid = dh2[f, :, cols] + inv0[f, :, cols] * (dnorm - unit * mean)
            dpre = dhid * slope[b, :, cols].astype(F32)
            for r in range(step // width):
                spread(dpre[:, r * width : (r + 1) * width], ds, cols.start // width + r, -1)
        center = xs[b]
        blank = jnp.zeros((chans, width), BF16)
        taller = jnp.concatenate([center[:, width:], blank], axis=1)
        lower = jnp.concatenate([blank, center[:, :-width]], axis=1)
        grad = dot_nt(ds[...], jnp.concatenate([lower, center, taller], axis=0))
        for j in range(3):
            grad_ref[j] += grad[j * chans : (j + 1) * chans]
        grad_ref[3] += dot_nt(dm0[f], stack(n0, f - 1, f, f + 1, whole))
        grad_ref[4] += dot_nt(dm1[f], stack(n1, f - 2, f, f + 2, whole))
        head = jnp.broadcast_to(dlog[f].astype(BF16), (chans, vox))
        grad_ref[5, :, :chans] += dot_nt(head, final_ref[f])
        for r, row in enumerate(conv_rows(wb_ref, ds, -1, rows, chans, width)):
            xt[pl.ds(r, chans, stride=rows), :] = row
        back[b] = xt[...].astype(BF16).reshape(chans, rows, width)

    grad_ref[...] = init_ref[...]
    stages = [
        (back0, 5, lo, hi),
        (back1, 3, lo - 1, hi + 1),
        (layer1, 0, 3, hi + 3),
        (layer0, -3, 1, hi + HALO - 1),
        (norm0, -5, 0, hi + HALO),
    ]
    cuts = sorted({a + d for _, d, a, _ in stages} | {b + d for _, d, _, b in stages})
    for a, b in zip(cuts, cuts[1:]):
        active = [(fn, d) for fn, d, p, n in stages if p + d <= a and b <= n + d]
        if a == lo + 5:
            for copy in late:
                copy.wait()
        loop(0, b - a, *[lambda i, fn=fn, f=a - d: fn(i + f) for fn, d in active])
    layer = meta_ref[base + 1 + counts]
    leaving = []
    for k in range(members):
        src = back.at[pl.ds(meta_ref[base + 1 + k] - HALO, here)]
        dst = send_ref.at[k - 1] if k else out_ref.at[:, :, layer]
        leaving.append(pltpu.make_async_copy(src, dst, sems.at[k]))
    for copy in leaving:
        copy.start()
    if last:
        for k in range(3):
            cols = slice(k * chans, (k + 1) * chans)
            for j in range(3):
                taps[3 * k + j] = grad_ref[j, :, cols] * 0.5
            for l in range(2):
                taps[9 + 3 * l + k] = grad_ref[3 + l, :, cols] * 0.5
        taps[15] = grad_ref[5, :, :chans]
    for copy in leaving:
        copy.wait()


def run_temporal(meta, base, vmem_args, weights, pieces, places, slopes, xss, last, into, dims, layers):
    own, chans, vox, total, members, width = dims
    rows, here = vox // width, own // members
    every = own + 2 * HALO
    sds = jax.ShapeDtypeStruct
    smem = pl.BlockSpec(memory_space=pltpu.SMEM)
    vmem = pl.BlockSpec(memory_space=pltpu.VMEM)
    hbm = pl.BlockSpec(memory_space=pl.ANY)
    loose = len(pieces) + 2 * members
    aliased = into is not None
    frame = lambda n, c, dt: pltpu.VMEM((n, c, vox), dt)
    sums = (6, chans, 3 * chans)
    shapes = [
        sds((own + 6, 1, vox), F32),
        sds((16, chans, chans) if last else sums, F32),
        sds((here, chans, layers, rows, width), BF16),
        sds((members - 1, here, chans, rows, width), BF16),
    ]
    specs = [vmem, vmem, hbm, hbm]
    return pl.pallas_call(
        functools.partial(temporal_kernel, tuple(places), last, aliased, base, dims),
        name="temporal",
        out_shape=shapes,
        in_specs=[smem, smem] + [vmem] * len(vmem_args) + [hbm] * (loose + aliased),
        out_specs=specs,
        input_output_aliases={2 + len(vmem_args) + loose: 2} if aliased else {},
        scratch_shapes=[
            frame(every, chans, BF16),
            frame(own, chans, BF16),
            frame(own, chans, BF16),
            frame(every, chans, BF16),
            frame(every, 1, F32),
            frame(every, chans, F32),
            frame(every, chans, BF16),
            frame(every, 1, F32),
            frame(every, chans, F32),
            frame(every, chans, F32),
            frame(every, chans, BF16),
            frame(every, chans, BF16),
            frame(every, chans, BF16),
            frame(every, 1, F32),
            pltpu.VMEM((3 * chans, vox), BF16),
            pltpu.VMEM((chans * rows, width), F32),
            pltpu.VMEM((own + 8, vox), F32),
            pltpu.SemaphoreType.DMA((loose,)),
        ]
        + [pltpu.VMEM(sums, F32)] * last
        + [pltpu.VMEM((own, chans, rows, width), BF16)],
        compiler_params=pltpu.CompilerParams(vmem_limit_bytes=VMEM_LIMIT),
        cost_estimate=pl.CostEstimate(
            flops=3000 * own * chans * vox, bytes_accessed=100 * own * chans * vox, transcendentals=0
        ),
    )(meta, weights, *vmem_args, *pieces, *slopes, *xss, *([into] if aliased else []))


def group_size(tiles, frames_here, layers):
    for g in range(1, layers + 1):
        if layers % g == 0 and tiles % g == 0 and g * frames_here >= HALO:
            return g
    return layers


def pick(parts, start):
    doubled = jnp.stack(parts + parts)
    return lax.dynamic_slice_in_dim(doubled, start, len(parts), 0)


def take(value, index, axis):
    return lax.dynamic_index_in_dim(value, index, axis, False)


def sum_over_tiles(value, tiles, g, others):
    if tiles & (tiles - 1):
        return lax.psum(value.astype(BF16), "tile").astype(F32), [], others
    steps = [2**k for k in range(tiles.bit_length() - 1)]
    outer, inner = [k for k in steps if k >= g], [k for k in steps if k < g]
    rounds = [part[i : i + 2] for part in (outer, inner) for i in range(0, len(part), 2)]
    for number, bits in enumerate(rounds):
        if number == len(rounds) - 1:
            value, others = lax.optimization_barrier((value, others))
        masks = bits + [sum(bits)] * (len(bits) - 1)
        sent, arrived = value.astype(BF16), []
        for k in masks:
            pairs = [(a, a ^ k) for a in range(tiles)]
            arrived.append(lax.ppermute(sent, "tile", pairs))
        if number < len(rounds) - 1:
            for piece in arrived:
                value = value + piece.astype(F32)
    return value, arrived, others


def sum_over_reps(value, axis):
    reps = lax.axis_size("rep")
    r = lax.axis_index("rep")
    n = value.shape[axis] // reps

    def share(k):
        return lax.dynamic_slice_in_dim(value, (k % reps) * n, n, axis)

    acc = share(r)
    for s in range(1, reps):
        pairs = [(a, (a + s) % reps) for a in range(reps)]
        acc = acc + lax.ppermute(share(r + s).astype(BF16), "rep", pairs).astype(F32)
    return acc


def body(inputs, w_spatial, w_temporal, w_head, targets, valid):
    _, here, chans, layers, rows, width = inputs.shape
    tiles = lax.axis_size("tile")
    total = here * tiles
    g = group_size(tiles, here, layers)
    per = layers // g
    own = g * here
    vox = rows * width
    t = lax.axis_index("tile")
    q, m = t // g, t % g
    spot = targets.shape[2]
    share = groups = tiles // g
    x = inputs[0]

    def swap(value, s):
        pairs = [(a, a // g * g + (a % g + s) % g) for a in range(tiles)]
        return lax.ppermute(value, "tile", pairs)

    def hop(value, shifts):
        pairs = [(a, a + shifts[a % g] * g) for a in range(tiles)]
        return lax.ppermute(value, "tile", [p for p in pairs if 0 <= p[1] < tiles])

    halved = (w_temporal.astype(F32) * 0.5).astype(BF16)
    wt = halved.transpose(0, 2, 1, 3).reshape(2, chans, 3 * chans)
    wtb = halved.transpose(0, 3, 1, 2).reshape(2, chans, 3 * chans)
    w9 = (w_spatial.astype(F32) * 0.5).astype(BF16).reshape(3, 3, chans, chans)
    wb = w9.transpose(0, 3, 1, 2).reshape(3 * chans, 3 * chans)
    whc = w_head.astype(F32)[:, None]

    mirrored = g == 2 and here <= HALO <= 2 * here
    extra = HALO - here if mirrored else 0
    up, down = own + HALO, HALO - here
    table, slots = [], {}
    for a in range(tiles):
        aq, am = a // g, a % g
        spots = [HALO + (am - s) % g * here for s in range(g)]
        if mirrored:
            for k in range(2):
                spots.append(up if am == k else down)
                if extra:
                    spots.append(0 if am == k else up + here)
        else:
            left, d = HALO, 1
            while left > 0:
                k = min(left, own)
                spots += [left - k, HALO + d * own]
                left -= k
                d += 1
        row = []

        def put(name, *values):
            slots[name] = len(row)
            row.extend(values)

        for layer in range(per):
            put(("temporal", layer), aq * own, *spots, am * per + layer)
        table.append(row)
    meta = lax.dynamic_index_in_dim(jnp.asarray(np.array(table, np.int32)), t, 0, False)

    leaving = [
        [lax.dynamic_slice_in_dim(x, (m + s) % g * per + layer, 1, 2) for s in range(1, g)]
        for layer in range(per)
    ]
    arriving = [[swap(piece, s + 1) for s, piece in enumerate(leaving[0])]]
    def member():
        return lax.rem(lax.axis_index("tile"), g)

    def last_if(k):
        return lambda: jnp.where(member() == k, (here - extra) // max(extra, 1), 0)

    mine = list(run_forward(lambda: member() * per, last_if(0), extra, per, x, w_spatial))
    leaving[1:], mine[1] = lax.optimization_barrier((leaving[1:], mine[1]))
    for pieces in leaving[1:]:
        arriving.append([swap(piece, s + 1) for s, piece in enumerate(pieces)])
    ahead = []
    if mirrored:
        ahead.append(hop(mine[0], (-1, 1)))
        if extra:
            mine[3], arriving[0] = lax.optimization_barrier((mine[3], arriving[0]))
            ahead.append(hop(mine[3], (1, -1)))

    dims = (own, chans, vox, total, g, width)
    grads = jnp.zeros((6, chans, 3 * chans), F32)
    asked, mine[2] = lax.optimization_barrier((targets, mine[2]))
    ready = []
    for layer in range(per):
        done = [mine]
        for piece in arriving[layer]:
            done.append(list(run_forward(lambda: 0, last_if(1), extra, 1, piece, w_spatial)))
        pieces = [d[0] for d in done]
        ranks = [layer] + [0] * (g - 1)
        if mirrored:
            if layer:
                ahead, done[1][0] = lax.optimization_barrier((ahead, done[1][0]))
            pieces += [*ahead, hop(done[1][0], (1, -1))]
            if extra:
                if layer:
                    before = ready[-1][1]
                    before[-1], done[1][3] = lax.optimization_barrier((before[-1], done[1][3]))
                pieces.append(hop(done[1][3], (-1, 1)))
            for k in range(2):
                ranks += [0 if k else layer] * len(ahead)
        else:
            block = [p[k] for p, k in zip(pieces, ranks)]
            block = pick(block[::-1], g - 1 - m).reshape(own, chans, vox)
            left, d = HALO, 1
            while left > 0:
                k = min(left, own)
                pieces.append(hop(block[own - k :], (d,) * g)[None])
                pieces.append(hop(block[:k], (-d,) * g)[None])
                ranks += [0, 0]
                left -= k
                d += 1
        ready.append([layer, pieces, ranks, [d[1] for d in done], [d[2] for d in done]])

    windows = run_windows(asked, tiles, own, g)
    windows = lax.all_to_all(windows, "tile", 0, 0, tiled=True)
    tgt = lax.dynamic_slice_in_dim(windows, m * share, share, 0)
    if share % per:
        tgt = tgt.transpose(1, 0, 2).reshape(own + 8, per, vox).transpose(1, 0, 2)
    frame_weight = jnp.pad(valid[0].astype(F32) / total, (3, 3))
    frame_weight = lax.dynamic_slice_in_dim(frame_weight, q * own, own + 6, 0)


    logits, out, homecoming = [], None, []
    for layer in range(per):
        _, pieces, ranks, slopes, xcs = ready[layer]
        part = share // per if share % per == 0 else 1
        logit, grads, out, sent = run_temporal(
            meta,
            slots["temporal", layer],
            (wt, wtb, whc, tgt[layer * part : (layer + 1) * part], grads, wb),
            frame_weight,
            pieces,
            ranks,
            slopes,
            xcs,
            layer == per - 1,
            out,
            dims,
            layers,
        )
        logits.append(logit[3 : 3 + own, 0])
        if layer < per - 1:
            following = ready[layer + 1]
            following[1], sent = lax.optimization_barrier((following[1], sent))
        homecoming.append([swap(sent[s - 1][:, :, None], -s) for s in range(1, g)])
    homecoming[:-1], grads = lax.optimization_barrier((homecoming[:-1], grads))

    logits = jnp.concatenate(logits, axis=1).astype(BF16).reshape(own, share, spot)
    logits = logits.transpose(1, 0, 2)
    logits = jnp.concatenate([logits] * g)
    logits = lax.all_to_all(logits, "tile", 0, 0, tiled=True)
    grads, arrived, homecoming = sum_over_tiles(sum_over_reps(grads, 1), tiles, g, homecoming)
    for layer in range(per):
        for s in range(1, g):
            place = (m + s) % g * per + layer
            out = lax.dynamic_update_slice_in_dim(out, homecoming[layer][s - 1], place, 2)
    logits, gs, gt, gh = run_finish(grads, arrived, logits, groups, g)
    logits, gh = logits.reshape(1, total, spot), gh[0]
    return logits, out[None], gs, gt, gh


def solution(mesh):
    placed = (
        P("rep", "tile", None, None, None, None),
        P(),
        P(),
        P(),
        P("rep", None, "tile"),
        P("rep", None),
    )
    return jax.shard_map(
        body,
        mesh=mesh,
        in_specs=placed,
        out_specs=(
            P("rep", None, "tile"),
            P("rep", "tile", None, None, None, None),
            P(None, "rep", None),
            P(None, None, "rep", None),
            P("rep"),
        ),
        check_vma=False,
    )
```
